32 devices in a mesh: groups: 2 (over x), ctx: 16 (over z, y, core).
Axes of the slice: x: 2, y: 2, z: 4, core: 2. Of those that a mesh axis runs over, the one named last changes fastest.
Arguments:
- query_video: bfloat16 [12288, 1536], P(('groups', 'ctx')), parts along dimension 0, may hold values from -10 to 10
- key_video: bfloat16 [12288, 1536], P(('groups', 'ctx')), parts along dimension 0, may hold values from -5 to 5
- value_video: bfloat16 [12288, 1536], P(('groups', 'ctx')), parts along dimension 0, may hold values from -6 to 6
- query_text: bfloat16 [512, 1536], P(('groups', 'ctx')), parts along dimension 0, may hold values from -10 to 10
- key_text: bfloat16 [512, 1536], P(('groups', 'ctx')), parts along dimension 0, may hold values from -5 to 5
- value_text: bfloat16 [512, 1536], P(('groups', 'ctx')), parts along dimension 0, may hold values from -6 to 6
- key_tiles: int32 [32, 3], P(('groups', 'ctx')), parts along dimension 0, may hold values from 0 to 15, as said below
- tile_owner: int32 [32], P('groups'), parts along dimension 0, may hold values from 0 to 15, as said below
- text_count: int32 [2], P('groups'), parts along dimension 0, may hold values from 64 to 256
Outputs:
- video_out: bfloat16 [12288, 1536], P(('groups', 'ctx')), parts along dimension 0
- text_out: bfloat16 [512, 1536], P(('groups', 'ctx')), parts along dimension 0
The draws below stay inside these ranges and needn't reach their ends.
There are 2 independent parts, one for each index of `groups`. The reference program is written for one: setup_inputs(seed, part) draws one part's arguments, and reference() takes and returns one part's arrays. A program takes and returns all parts, laid end to end along the dimension named above; each array names one. Nothing has to cross between parts.
Inputs may be any that keep to these rules, and one draw needn't show every extreme that they name: `key_tiles`: each list names 3 different tiles, the query tile itself among them; every listed tile has a stored position whose device (position) is at most 2 away from the query tile's device, and every list names one exactly 2 away. `tile_owner`: A permutation of the tile numbers.
All inputs are finite; a program needn't handle non-finite values.
Results may differ from the reference program's by a relative error of at most 0.0032.
Values may be sent and summed in bfloat16 or wider, within the bound.
A program may use at most 384 MiB of HBM per device.

```python
import math
import jax
import jax.numpy as jnp
from jax import lax

TILE = 384
HEADS = 12
HD = 128
NB = 3
REACH = 2
TXT = 256
TPD = 1
TILES = 16
VID = 6144


def rough_rows(key, row_count, spread, limit):
    drawn = jax.random.normal(key, (row_count, HEADS * HD), jnp.float32)
    return jnp.clip(drawn * spread, -limit, limit)


def draw_query_video(key, part):
    rows_drawn = rough_rows(jax.random.fold_in(key, 1), VID, 2.5, 10.0)
    return rows_drawn.astype(jnp.bfloat16)


def draw_key_video(key, part):
    rows_drawn = rough_rows(jax.random.fold_in(key, 2), VID, 1.0, 5.0)
    return rows_drawn.astype(jnp.bfloat16)


def draw_query_text(key, part):
    rows_drawn = rough_rows(jax.random.fold_in(key, 4), TXT, 2.5, 10.0)
    return rows_drawn.astype(jnp.bfloat16)


def draw_key_text(key, part):
    rows_drawn = rough_rows(jax.random.fold_in(key, 5), TXT, 1.0, 5.0)
    return rows_drawn.astype(jnp.bfloat16)


def tile_layout(key):
    layout_key = jax.random.fold_in(key, 11)
    slot_ids = jnp.arange(TILES, dtype=jnp.int32)
    device_ids = slot_ids // TPD
    window_size = (2 * REACH + 1) * TPD
    window_steps = jnp.arange(window_size, dtype=jnp.int32)
    candidates = (device_ids[:, None] - REACH) * TPD + window_steps[None, :]
    inside = (candidates >= 0) & (candidates < TILES)
    random_part = jax.random.randint(layout_key, (TILES, window_size), 0, 4096, dtype=jnp.int32)
    ranking = random_part * window_size + window_steps[None, :]
    remote_partner = inside & (jnp.abs(candidates // TPD - device_ids[:, None]) == REACH)
    far_rank = jnp.where(remote_partner, ranking, -1)
    far_best = jnp.max(far_rank, axis=1, keepdims=True)
    ranking = jnp.where(remote_partner & (far_rank == far_best), ranking + 2 ** 24, ranking)
    ranking = jnp.where(candidates == slot_ids[:, None], ranking + 2 ** 25, ranking)
    ranking = jnp.where(inside, ranking, -2 ** 26)
    chosen = lax.top_k(ranking, NB)[1]
    picked_slots = jnp.take_along_axis(candidates, chosen, axis=1)
    spatial_order = jax.random.permutation(jax.random.fold_in(key, 12), TILES).astype(jnp.int32)
    owner_table = jnp.zeros((TILES,), jnp.int32).at[spatial_order].set(slot_ids)
    listed = spatial_order[picked_slots]
    return (listed.astype(jnp.int32), owner_table)


def draw_key_tiles(key, part):
    return tile_layout(key)[0]


def draw_tile_owner(key, part):
    return tile_layout(key)[1]


def levels(stream_key, extent, shards, low, largest):
    factor_of, own = 1.0, jax.random.fold_in(stream_key, 6)
    for dim, parts in shards:
        draws = jnp.exp(jax.random.uniform(jax.random.fold_in(own, dim), (parts,), jnp.float32, low / len(shards), largest / len(shards)))
        factor_of = factor_of * jnp.repeat(draws, extent[dim] // parts).reshape([-1 if axis == dim else 1 for axis in range(len(extent))])
    return factor_of


def normal_values(rng, shape, deviation, most, pieces=(), kind=jnp.bfloat16):
    values = deviation * jax.random.normal(rng, shape, jnp.float32)
    if pieces:
        values = values * levels(rng, shape, pieces, -0.22, 0.18)
    return jnp.clip(values, -most, most).astype(kind)


def setup_inputs(seed: int = 0, part: int = 0) -> dict:
    arg_keys = jax.random.split(jax.random.key(seed), 10)
    own_keys = jax.random.split(jax.random.fold_in(arg_keys[9], part), 10)
    query_video = draw_query_video(jax.random.fold_in(jax.random.fold_in(arg_keys[9], part), 71), part)
    key_video = draw_key_video(jax.random.fold_in(jax.random.fold_in(arg_keys[9], part), 71), part)
    value_video = normal_values(own_keys[2], (VID, HEADS * HD), 1.0, 6.0, ((0, 16),))
    query_text = draw_query_text(jax.random.fold_in(jax.random.fold_in(arg_keys[9], part), 71), part)
    key_text = draw_key_text(jax.random.fold_in(jax.random.fold_in(arg_keys[9], part), 71), part)
    value_text = normal_values(own_keys[5], (TXT, HEADS * HD), 1.0, 6.0, ((0, 16),))
    key_tiles = draw_key_tiles(jax.random.fold_in(jax.random.fold_in(arg_keys[9], part), 71), part)
    tile_owner = draw_tile_owner(jax.random.fold_in(jax.random.fold_in(arg_keys[9], part), 71), part)
    text_count = jax.random.randint(own_keys[8], (1,), TXT // 4, TXT + 1).astype(jnp.int32)
    return dict(query_video=query_video, key_video=key_video, value_video=value_video, query_text=query_text, key_text=key_text, value_text=value_text, key_tiles=key_tiles, tile_owner=tile_owner, text_count=text_count)


def rounded_copy(values):
    return lax.optimization_barrier(values.astype(jnp.bfloat16)).astype(jnp.float32)

def reference(query_video, key_video, value_video, query_text, key_text, value_text, key_tiles, tile_owner, text_count):
    feature_width = HEADS * HD
    inverse_root_dimension = 1.0 / math.sqrt(HD)
    text_ok = jnp.arange(TXT) < text_count[0]
    key_slots = tile_owner[key_tiles].astype(jnp.int32)
    key_grid = key_video.reshape(TILES, TILE, HEADS, HD)
    value_grid = value_video.reshape(TILES, TILE, HEADS, HD)
    text_keys = key_text.reshape(TXT, HEADS, HD).astype(jnp.float32)
    text_values = value_text.reshape(TXT, HEADS, HD).astype(jnp.float32)

    def one_tile(tile_data):
        query_tile, slot_list = tile_data
        adjacent_tile_lookups = key_grid[slot_list].reshape(NB * TILE, HEADS, HD).astype(jnp.float32)
        value_rows = value_grid[slot_list].reshape(NB * TILE, HEADS, HD).astype(jnp.float32)
        asking_token_array = query_tile.reshape(TILE, HEADS, HD).astype(jnp.float32)
        frame_affinity_array = jnp.einsum('qhd,khd->hqk', asking_token_array, adjacent_tile_lookups) * inverse_root_dimension
        wording_affinity_array = jnp.einsum('qhd,khd->hqk', asking_token_array, text_keys) * inverse_root_dimension
        wording_affinity_array = jnp.where(text_ok[None, None, :], wording_affinity_array, -jnp.inf)
        scores = jnp.concatenate([frame_affinity_array, wording_affinity_array], axis=-1)
        row_max = lax.optimization_barrier(jnp.max(scores, axis=-1, keepdims=True))
        weights = jnp.exp(scores - row_max)
        row_total = lax.optimization_barrier(jnp.sum(weights, axis=-1))
        rounded_scores = rounded_copy(weights)
        combined_value_rows = jnp.concatenate([value_rows, text_values], axis=0)
        output_tile = jnp.einsum('hqk,khd->qhd', rounded_scores, combined_value_rows)
        output_tile = output_tile / jnp.transpose(row_total)[:, :, None]
        return output_tile.reshape(TILE, feature_width).astype(jnp.bfloat16)
    video_out = lax.map(one_tile, (query_video.reshape(TILES, TILE, feature_width), key_slots))
    video_out = video_out.reshape(VID, feature_width)
    blocks = TILES // TPD
    video_block = TPD * TILE
    text_block = TXT // blocks
    text_query_heads = jnp.transpose(query_text.reshape(TXT, HEADS, HD), (1, 0, 2))
    key_block_heads = jnp.transpose(key_video.reshape(blocks, video_block, HEADS, HD), (2, 0, 1, 3))
    value_block_heads = jnp.transpose(value_video.reshape(blocks, video_block, HEADS, HD), (2, 0, 1, 3))
    text_key_heads = jnp.transpose(key_text.reshape(blocks, text_block, HEADS, HD), (2, 0, 1, 3))
    text_value_heads = jnp.transpose(value_text.reshape(blocks, text_block, HEADS, HD), (2, 0, 1, 3))
    block_ok = text_ok.reshape(blocks, text_block)

    def one_head(head_data):
        asking_token_array, adjacent_tile_lookups, value_rows, subtitle_lookup_entries, text_value_rows = head_data
        asking_token_array = asking_token_array.astype(jnp.float32)
        frame_affinity_array = jnp.einsum('pb,dmb->dpm', asking_token_array, adjacent_tile_lookups.astype(jnp.float32)) * inverse_root_dimension
        wording_affinity_array = jnp.einsum('pb,dmb->dpm', asking_token_array, subtitle_lookup_entries.astype(jnp.float32)) * inverse_root_dimension
        wording_affinity_array = jnp.where(block_ok[:, None, :], wording_affinity_array, -jnp.inf)
        scores = jnp.concatenate([frame_affinity_array, wording_affinity_array], axis=-1)
        block_max = lax.optimization_barrier(jnp.max(scores, axis=-1))
        weights = jnp.exp(scores - block_max[:, :, None])
        block_total = lax.optimization_barrier(jnp.sum(weights, axis=-1))
        rounded_scores = rounded_copy(weights)
        combined_value_rows = jnp.concatenate([value_rows, text_value_rows], axis=1).astype(jnp.float32)
        block_weight_sum = jnp.einsum('ywu,yuo->ywo', rounded_scores, combined_value_rows)
        overall_peak = lax.optimization_barrier(jnp.max(block_max, axis=0))
        factor = jnp.exp(block_max - overall_peak[None, :])
        text_total = lax.optimization_barrier(jnp.sum(block_total * factor, axis=0))
        text_acc = lax.optimization_barrier(jnp.sum(block_weight_sum * factor[:, :, None], axis=0))
        return text_acc / text_total[:, None]
    head_results = lax.map(one_head, (text_query_heads, key_block_heads, value_block_heads, text_key_heads, text_value_heads))
    text_out = jnp.transpose(head_results, (1, 0, 2)).reshape(TXT, feature_width).astype(jnp.bfloat16)
    return (video_out, text_out)
```

```python
import functools
import math

import jax
import jax.numpy as jnp
from jax import lax
from jax.experimental import pallas as pl
from jax.experimental.pallas import tpu as pltpu
from jax.sharding import PartitionSpec as P

TILE = 384
HD = 128
REACH = 2
CHUNK = 3
C2 = math.log2(math.e) / math.sqrt(HD)


def qk(q, k):
    return lax.dot_general(q, k, (((1,), (1,)), ((), ())), preferred_element_type=jnp.float32)


def pv(p, v):
    return lax.dot_general(
        p.astype(jnp.bfloat16), v, (((1,), (0,)), ((), ())), preferred_element_type=jnp.float32
    )


def softmax_parts(scores, values):
    peak = functools.reduce(jnp.maximum, [jnp.max(s, axis=-1, keepdims=True) for s in scores])
    total, acc = None, None
    for s, v in zip(scores, values):
        w = jnp.exp2((s - peak) * C2)
        t = jnp.sum(w, axis=-1, keepdims=True)
        a = pv(w, v)
        total = t if total is None else total + t
        acc = a if acc is None else acc + a
    return peak, total, acc


def video_kernel(meta, q, own, m2, p2, sib, fwd, tk, tv, prev, out):
    lo_p2 = meta[0] == 2
    hi_sib = meta[1] == 3
    hi_fwd = meta[1] == 4
    tiles = []
    for j in range(2):
        far_m, far_p = m2[j], p2[j]
        lo = jnp.where(lo_p2, far_p, far_m)
        hi = jnp.where(hi_fwd, fwd[j], jnp.where(hi_sib, sib[j], far_p))
        tiles.append((own[j], lo, hi))
    key_words = tk[...]
    value_words = tv[...]
    ok = lax.broadcasted_iota(jnp.int32, (1, key_words.shape[0]), 1) < meta[2]
    rows = 128
    for r in range(q.shape[0] // rows):
        qr = q[pl.ds(r * rows, rows), :]
        scores = [qk(qr, k) for k in tiles[0]]
        scores.append(jnp.where(ok, qk(qr, key_words), -jnp.inf))
        _, total, acc = softmax_parts(scores, list(tiles[1]) + [value_words])
        out[pl.ds(r * rows, rows), :] = (acc / total).astype(jnp.bfloat16)


def text_kernel(meta, q, k, v, kt, vt, peak_out, total_out, acc_out):
    h = pl.program_id(0)
    own = kt.shape[0]
    ok = lax.broadcasted_iota(jnp.int32, (1, own), 1) < meta[3]
    scores = [qk(q[...], k[...]), jnp.where(ok, qk(q[...], kt[...]), -jnp.inf)]
    peak, total, acc = softmax_parts(scores, [v[...], vt[...]])
    lane = lax.broadcasted_iota(jnp.int32, peak_out.shape, 1) == h
    peak_out[...] = jnp.where(lane, peak, jnp.where(h == 0, 0.0, peak_out[...]))
    total_out[...] = jnp.where(lane, total, jnp.where(h == 0, 1.0, total_out[...]))
    acc_out[...] = acc


def spread_heads(values, heads):
    return jnp.repeat(values[..., :heads], HD, axis=-1)


def on_device(qv, kv, vv, qt, kt, vt, key_tiles, tile_owner, text_count):
    n = lax.axis_size("ctx")
    me = lax.axis_index("ctx")
    rows, width = qv.shape
    heads = width // HD
    here = qt.shape[0]
    even = me % 2 == 0
    cols = CHUNK * HD
    chunks = heads // CHUNK

    text = lax.all_gather(jnp.stack([qt, kt, vt]), "ctx", axis=1, tiled=True)
    tq, tk, tv = text[0], text[1], text[2]

    tiles = tile_owner.shape[0]
    match = key_tiles[0][:, None] == jnp.arange(tiles, dtype=jnp.int32)[None, :]
    slots = jnp.sum(jnp.where(match, tile_owner[None, :], 0), axis=-1)
    off = slots - me
    near = jnp.where(even == (off == 1), 3, 4)
    code = jnp.where(off == 0, 0, jnp.where(off == -2, 1, jnp.where(off == 2, 2, near)))
    hi = jnp.max(code)
    lo = jnp.sum(code) - hi
    meta = jnp.stack([lo, hi, text_count[0], text_count[0] - me * here]).astype(jnp.int32)

    up = [(i, i - 2) for i in range(2, n)]
    down = [(i, i + 2) for i in range(n - 2)]
    swap = [(i, i ^ 1) for i in range(n)]
    fetched = []
    for c in range(chunks):
        sl = slice(c * cols, (c + 1) * cols)
        own = jnp.stack([kv[:, sl], vv[:, sl]])
        p2 = lax.ppermute(own, "ctx", up)
        m2 = lax.ppermute(own, "ctx", down)
        sib = lax.ppermute(own, "ctx", swap)
        fwd = lax.ppermute(jnp.where(even, p2, m2), "ctx", swap)
        fetched.append((own, m2, p2, sib, fwd))

    col = lambda h: (0, h)
    text_rows = tq.shape[0]
    smem = pl.BlockSpec(memory_space=pltpu.SMEM)
    peak, total, acc = pl.pallas_call(
        text_kernel,
        grid=(heads,),
        in_specs=[
            smem,
            pl.BlockSpec((text_rows, HD), col),
            pl.BlockSpec((rows, HD), col),
            pl.BlockSpec((rows, HD), col),
            pl.BlockSpec((here, HD), col),
            pl.BlockSpec((here, HD), col),
        ],
        out_specs=[
            pl.BlockSpec((text_rows, 128), lambda h: (0, 0)),
            pl.BlockSpec((text_rows, 128), lambda h: (0, 0)),
            pl.BlockSpec((text_rows, HD), col),
        ],
        out_shape=[
            jax.ShapeDtypeStruct((text_rows, 128), jnp.float32),
            jax.ShapeDtypeStruct((text_rows, 128), jnp.float32),
            jax.ShapeDtypeStruct((text_rows, width), jnp.float32),
        ],
        cost_estimate=pl.CostEstimate(
            flops=4 * text_rows * rows * width * 4, bytes_accessed=6 << 20, transcendentals=0
        ),
        name="text_partials",
    )(meta, tq, kv, vv, kt, vt)

    out = jnp.zeros((rows, width), jnp.bfloat16)
    for c in range(chunks):
        own, m2, p2, sib, fwd = fetched[c]
        tile_spec = pl.BlockSpec((2, rows, HD), lambda h: (0, 0, h))
        wide = lambda h, c=c: (0, h + c * CHUNK)
        out = pl.pallas_call(
            video_kernel,
            grid=(CHUNK,),
            in_specs=[smem, pl.BlockSpec((rows, HD), wide)]
            + [tile_spec] * 5
            + [pl.BlockSpec((text_rows, HD), wide)] * 2
            + [pl.BlockSpec(memory_space=pl.ANY)],
            out_specs=pl.BlockSpec((rows, HD), wide),
            out_shape=jax.ShapeDtypeStruct((rows, width), jnp.bfloat16),
            input_output_aliases={9: 0},
            compiler_params=pltpu.CompilerParams(vmem_limit_bytes=32 << 20),
            cost_estimate=pl.CostEstimate(
                flops=4 * rows * (3 * rows + text_rows) * cols * 4,
                bytes_accessed=8 << 20,
                transcendentals=0,
            ),
            name="video_chunk",
        )(meta, qv, own, m2, p2, sib, fwd, tk, tv, out)

    blocks = n
    stats = jnp.stack([peak, total]).reshape(2, blocks, here, 128)
    acc = acc.reshape(blocks, here, width)
    step = 1
    while step < n:
        blocks //= 2
        bit = (me // step) % 2
        pairs = [(i, i ^ step) for i in range(n)]
        stats4 = stats.reshape(2, blocks, 2, here, 128)
        acc4 = acc.reshape(blocks, 2, here, width)
        pick = lambda x, b, ax: jnp.where(
            b == 0, lax.index_in_dim(x, 0, ax, False), lax.index_in_dim(x, 1, ax, False)
        )
        their_s = lax.ppermute(pick(stats4, 1 - bit, 2), "ctx", pairs)
        their_a = lax.ppermute(pick(acc4, 1 - bit, 1), "ctx", pairs)
        my_s = pick(stats4, bit, 2)
        my_a = pick(acc4, bit, 1)
        joint = jnp.maximum(my_s[0], their_s[0])
        f_my = jnp.exp2((my_s[0] - joint) * C2)
        f_their = jnp.exp2((their_s[0] - joint) * C2)
        stats = jnp.stack([joint, my_s[1] * f_my + their_s[1] * f_their])
        acc = my_a * spread_heads(f_my, heads) + their_a * spread_heads(f_their, heads)
        step *= 2
    text_out = (acc[0] / spread_heads(stats[1, 0], heads)).astype(jnp.bfloat16)
    return (out, text_out)


def plane_kernel(n, listed, owner, count, *refs):
    q_hbm, k_hbm, v_hbm, qt_hbm, kt_hbm, vt_hbm, out, text_out = refs[:8]
    heads = q_hbm.shape[1] // HD
    mine = heads // 4
    kv = refs[8 : 8 + mine]
    (
        qb,
        ob,
        tx,
        part,
        got,
        tob,
        list_out,
        list_in,
        lists,
        in_send,
        in_recv,
        tx_send,
        tx_recv,
        chain_send,
        chain_recv,
        halo_send,
        halo_recv,
        o_send,
        o_recv,
        p_send,
        p_recv,
        t_send,
        t_recv,
        l_send,
        l_recv,
        l_in,
    ) = refs[8 + mine :]
    rows = q_hbm.shape[0]
    here = qt_hbm.shape[0]
    block = 4 * here
    nz = n // 4
    wide = mine * HD
    me = lax.axis_index("ctx")
    g = lax.rem(me, 4)
    core = lax.rem(g, 2)
    side = g // 2
    row = me // 4
    base = row * 4
    sib = g + 1 - 2 * core
    pair = g + 2 - 4 * side
    diag = sib + 2 - 4 * side
    mates = [pair, diag, sib]
    above, below = me + 4, me - 4
    has_above, has_below = row < nz - 1, row > 0
    peers = [lax.rem(row + k, nz) for k in range(1, nz)]
    sources = [lax.rem(row + nz - k, nz) for k in range(1, nz)]

    def cols(start, size):
        return pl.ds(pl.multiple_of(start, HD), size)

    def remote(src, dst, send, recv, dev):
        return pltpu.make_async_remote_copy(
            src_ref=src,
            dst_ref=dst,
            send_sem=send,
            recv_sem=recv,
            device_id={"ctx": dev},
            device_id_type=pl.DeviceIdType.MESH,
        )

    def greet(barrier, dev):
        pl.semaphore_signal(
            barrier, inc=1, device_id={"ctx": dev}, device_id_type=pl.DeviceIdType.MESH
        )

    barrier = pltpu.get_barrier_semaphore()
    for mate in mates:
        greet(barrier, base + mate)
    for peer in peers:
        greet(barrier, peer * 4 + g)

    arrays = (k_hbm, v_hbm, q_hbm)
    text_arrays = (qt_hbm, kt_hbm, vt_hbm)

    def spot(j, x, s):
        return qb.at[j, s] if x == 2 else kv[j].at[2 + s, x]

    def source(j, x, s):
        return arrays[x].at[:, cols((s * mine + j) * HD, HD)]

    def own_in(j, x):
        return pltpu.make_async_copy(source(j, x, g), spot(j, x, g), in_recv.at[j, x, g])

    def send_in(j, x, k):
        return remote(
            source(j, x, mates[k]), spot(j, x, g), in_send.at[j, x, k], in_recv.at[j, x, g],
            base + mates[k],
        )

    def wait_in(j, x, s):
        pltpu.make_async_copy(source(j, x, s), spot(j, x, s), in_recv.at[j, x, s]).wait()

    def own_text(x):
        return pltpu.make_async_copy(
            text_arrays[x].at[:, cols(g * wide, wide)], tx.at[row, x, g], tx_recv.at[x, g]
        )

    def send_text(x, k):
        return remote(
            text_arrays[x].at[:, cols(mates[k] * wide, wide)],
            tx.at[row, x, g],
            tx_send.at[x, k],
            tx_recv.at[x, g],
            base + mates[k],
        )

    def wait_text(x, s):
        pltpu.make_async_copy(
            text_arrays[x].at[:, cols(s * wide, wide)], tx.at[row, x, s], tx_recv.at[x, s]
        ).wait()

    def send_list(k):
        return remote(list_out, list_in.at[g], l_send.at[k], l_recv.at[g], base + mates[k])

    for x in range(3):
        own_text(x).start()
    for j in range(mine):
        for x in range(3):
            own_in(j, x).start()
    lane = lax.broadcasted_iota(jnp.int32, list_out.shape, 1)
    spots = jnp.zeros(list_out.shape, jnp.int32)
    for i in range(listed.shape[1]):
        spots = jnp.where(lane == i, owner[listed[0, i]], spots)
    list_out[...] = spots
    list_in[g] = spots

    pl.semaphore_wait(barrier, 3 + nz - 1)
    for k in range(3):
        for x in range(3):
            send_text(x, k).start()
        send_list(k).start()
    for j in range(mine):
        for x in range(3):
            for k in range(3):
                send_in(j, x, k).start()

    limit = count[0]
    place = lax.broadcasted_iota(jnp.int32, (1, n * here), 1)
    bias_all = jnp.where(place < limit, 0.0, -jnp.inf).astype(jnp.float32)
    place = row * block + lax.broadcasted_iota(jnp.int32, (1, block), 1)
    bias_own = jnp.where(place < limit, 0.0, -jnp.inf).astype(jnp.float32)

    def chain(z, up):
        return remote(
            tx.at[z], tx.at[z], chain_send.at[0 if up else 1, z], chain_recv.at[z],
            above if up else below,
        )

    def chain_wait(z):
        pltpu.make_async_copy(tx.at[z], tx.at[z], chain_recv.at[z]).wait()

    def chain_step(d):
        up_from, down_from = row - d, row + d
        if d > 0:
            pl.when(up_from >= 0)(lambda: chain_wait(up_from))
        pl.when(jnp.logical_and(up_from >= 0, has_above))(lambda: chain(up_from, True).start())
        if d > 0:
            pl.when(down_from < nz)(lambda: chain_wait(down_from))
        pl.when(jnp.logical_and(down_from < nz, has_below))(
            lambda: chain(down_from, False).start()
        )

    def chain_drain(d):
        up_from, down_from = row - d, row + d
        pl.when(jnp.logical_and(up_from >= 0, has_above))(
            lambda: chain(up_from, True).wait_send()
        )
        pl.when(jnp.logical_and(down_from < nz, has_below))(
            lambda: chain(down_from, False).wait_send()
        )

    halo_to = (6, 7, 0, 1)

    def halo(j, s):
        return remote(
            kv[j].at[2 + s], kv[j].at[halo_to[s]], halo_send.at[j, s], halo_recv.at[j, s],
            below if s < 2 else above,
        )

    def halo_start(j):
        for s in range(4):
            wait_in(j, 0, s)
            wait_in(j, 1, s)
            pl.when(has_below if s < 2 else has_above)(lambda s=s: halo(j, s).start())

    def halo_wait(j):
        for s in range(4):
            pl.when(has_above if s < 2 else has_below)(lambda s=s: halo(j, s).wait_recv())

    def halo_drain(j):
        for s in range(4):
            pl.when(has_below if s < 2 else has_above)(lambda s=s: halo(j, s).wait_send())

    def text_words(x, j):
        return tx[:, x, :, :, j * HD : (j + 1) * HD].reshape(n * here, HD)

    def text_head(j):
        q = text_words(0, j)
        keys = [kv[j][2 + s, 0] for s in range(4)]
        values = [kv[j][2 + s, 1] for s in range(4)]
        own = [tx[row, x, :, :, j * HD : (j + 1) * HD].reshape(block, HD) for x in (1, 2)]
        scores = [qk(q, key) for key in keys] + [qk(q, own[0]) + bias_own]
        peak, total, acc = softmax_parts(scores, values + [own[1]])
        part[j] = acc.reshape(nz, block, HD)
        lane = lax.broadcasted_iota(jnp.int32, (n * here, 128), 1)
        old = part[mine].reshape(n * here, 128) if j else jnp.ones((n * here, 128), jnp.float32)
        new = jnp.where(lane == j, peak, jnp.where(lane == mine + j, total, old))
        part[mine] = new.reshape(nz, block, 128)

    def part_z(j, k):
        return remote(
            part.at[j, peers[k]], got.at[k, j], p_send.at[j, k], p_recv.at[j, k],
            peers[k] * 4 + g,
        )

    def out_spot(j, s):
        return out.at[:, cols((s * mine + j) * HD, HD)]

    def send_out(j, s):
        return remote(ob.at[j, s], out_spot(j, g), o_send.at[j, s], o_recv.at[j, g], base + s)

    def keep_out(j, s):
        return pltpu.make_async_copy(ob.at[j, s], out_spot(j, g), o_recv.at[j, g])

    def video_tile(j, s):
        at = [jnp.clip(lists[s, 0, i] - (base - 2), 0, 7) for i in range(listed.shape[1])]
        keys = [kv[j][i, 0] for i in at] + [text_words(1, j)]
        values = [kv[j][i, 1] for i in at] + [text_words(2, j)]
        step = 128
        for r in range(rows // step):
            qr = qb[j, s, r * step : (r + 1) * step, :]
            scores = [qk(qr, key) for key in keys]
            scores[-1] = scores[-1] + bias_all
            _, total, acc = softmax_parts(scores, values)
            ob[j, s, r * step : (r + 1) * step, :] = (acc / total).astype(jnp.bfloat16)
        pl.when(s == g)(lambda: keep_out(j, s).start())
        pl.when(s != g)(lambda: send_out(j, s).start())

    def video_tiles(j, lo, hi):
        def one(i, _):
            video_tile(j, lax.rem(i + 2 * (1 - side), 4))
            return 0

        lax.fori_loop(lo, hi, one, 0)

    def text_final():
        for j in range(mine + 1):
            for k in range(nz - 1):
                part_z(j, k).wait_recv()
        stats = [part[mine, row]] + [got[k, mine] for k in range(nz - 1)]
        for j in range(mine):
            peaks = [x[:, j : j + 1] for x in stats]
            totals = [x[:, mine + j : mine + j + 1] for x in stats]
            accs = [part[j, row]] + [got[k, j] for k in range(nz - 1)]
            joint = functools.reduce(jnp.maximum, peaks)
            weights = [jnp.exp2((p - joint) * C2) for p in peaks]
            total = sum(t * w for t, w in zip(totals, weights))
            acc = sum(a * w for a, w in zip(accs, weights))
            tob[:, :, j * HD : (j + 1) * HD] = (
                (acc / total).astype(jnp.bfloat16).reshape(4, here, HD)
            )

    def text_spot(s):
        return text_out.at[:, cols(s * wide, wide)]

    def send_words(k):
        s = mates[k]
        return remote(tob.at[s], text_spot(g), t_send.at[k], t_recv.at[g], base + s)

    def keep_words():
        return pltpu.make_async_copy(tob.at[g], text_spot(g), t_recv.at[g])

    for x in range(3):
        for s in range(4):
            wait_text(x, s)
    chain_step(0)
    for k in range(3):
        pltpu.make_async_copy(list_out, list_in.at[mates[k]], l_recv.at[mates[k]]).wait()
    lists_in = pltpu.make_async_copy(list_in, lists, l_in)
    lists_in.start()
    lists_in.wait()
    for d in range(1, nz - 1):
        chain_step(d)
    halo_start(0)
    pl.when(row - (nz - 1) >= 0)(lambda: chain_wait(row - (nz - 1)))
    pl.when(row + nz - 1 < nz)(lambda: chain_wait(row + nz - 1))

    for j in range(mine):
        if j:
            halo_start(j)
        text_head(j)
        for k in range(nz - 1):
            part_z(j, k).start()
        if j == mine - 1:
            for k in range(nz - 1):
                part_z(mine, k).start()
        for s in range(4):
            wait_in(j, 2, s)
        halo_wait(j)
        if j < mine - 1:
            video_tiles(j, 0, 4)
        else:
            video_tiles(j, 0, 2)
            text_final()
            for k in range(3):
                send_words(k).start()
            keep_words().start()
            video_tiles(j, 2, 4)

    for j in range(mine):
        for s in range(4):
            pltpu.make_async_copy(ob.at[j, s], out_spot(j, s), o_recv.at[j, s]).wait()
            pl.when(s != g)(lambda s=s: send_out(j, s).wait_send())
        for x in range(3):
            for k in range(3):
                send_in(j, x, k).wait_send()
        halo_drain(j)
    for s in range(4):
        pltpu.make_async_copy(tob.at[s], text_spot(s), t_recv.at[s]).wait()
    for k in range(3):
        send_words(k).wait_send()
        send_list(k).wait_send()
        for x in range(3):
            send_text(x, k).wait_send()
    for d in range(nz - 1):
        chain_drain(d)
    for j in range(mine + 1):
        for k in range(nz - 1):
            part_z(j, k).wait_send()


def fused(qv, kv, vv, qt, kt, vt, key_tiles, tile_owner, text_count):
    n = lax.axis_size("ctx")
    rows, width = qv.shape
    mine = width // HD // 4
    here = qt.shape[0]
    nz = n // 4
    dma = pltpu.SemaphoreType.DMA
    return pl.pallas_call(
        functools.partial(plane_kernel, n),
        in_specs=[pl.BlockSpec(memory_space=pltpu.SMEM)] * 3
        + [pl.BlockSpec(memory_space=pl.ANY)] * 6,
        out_specs=[pl.BlockSpec(memory_space=pl.ANY)] * 2,
        out_shape=[
            jax.ShapeDtypeStruct((rows, width), jnp.bfloat16),
            jax.ShapeDtypeStruct((here, width), jnp.bfloat16),
        ],
        scratch_shapes=[pltpu.VMEM((8, 2, rows, HD), jnp.bfloat16)] * mine
        + [
            pltpu.VMEM((mine, 4, rows, HD), jnp.bfloat16),
            pltpu.VMEM((mine, 4, rows, HD), jnp.bfloat16),
            pltpu.VMEM((nz, 3, 4, here, mine * HD), jnp.bfloat16),
            pltpu.VMEM((mine + 1, nz, 4 * here, HD), jnp.float32),
            pltpu.VMEM((nz - 1, mine + 1, 4 * here, HD), jnp.float32),
            pltpu.VMEM((4, here, mine * HD), jnp.bfloat16),
            pltpu.VMEM((8, 128), jnp.int32),
            pltpu.VMEM((4, 8, 128), jnp.int32),
            pltpu.SMEM((4, 8, 128), jnp.int32),
        ]
        + [dma((mine, 3, 3)), dma((mine, 3, 4)), dma((3, 3)), dma((3, 4))]
        + [dma((2, nz)), dma((nz,)), dma((mine, 4)), dma((mine, 4))]
        + [dma((mine, 4)), dma((mine, 4)), dma((mine + 1, nz - 1)), dma((mine + 1, nz - 1))]
        + [dma((3,)), dma((4,)), dma((3,)), dma((4,)), dma],
        compiler_params=pltpu.CompilerParams(
            collective_id=0, has_side_effects=True, vmem_limit_bytes=56 << 20
        ),
        name="tile_attention",
    )(key_tiles, tile_owner, text_count, qv, kv, vv, qt, kt, vt)


def whole_device(*args):
    n = lax.axis_size("ctx")
    rows, width = args[0].shape
    here = args[3].shape[0]
    if rows == TILE and n % 4 == 0 and n >= 8 and n & (n - 1) == 0 and here in (16, 32, 64) and width // HD == 12:
        return fused(*args)
    return on_device(*args)


def solution(mesh):
    split = P(("groups", "ctx"), None)
    return jax.shard_map(
        whole_device,
        mesh=mesh,
        in_specs=(split,) * 7 + (P("groups"), P("groups")),
        out_specs=(split, split),
        check_vma=False,
    )
```

```python
import functools
import math

import jax
import jax.numpy as jnp
from jax import lax
from jax.experimental import pallas as pl
from jax.experimental.pallas import tpu as pltpu
from jax.sharding import PartitionSpec as P

TILE = 384
HD = 128
REACH = 2
CHUNK = 3
C2 = math.log2(math.e) / math.sqrt(HD)


def qk(q, k):
    return lax.dot_general(q, k, (((1,), (1,)), ((), ())), preferred_element_type=jnp.float32)


def pv(p, v):
    return lax.dot_general(
        p.astype(jnp.bfloat16), v, (((1,), (0,)), ((), ())), preferred_element_type=jnp.float32
    )


def softmax_parts(scores, values):
    peak = functools.reduce(jnp.maximum, [jnp.max(s, axis=-1, keepdims=True) for s in scores])
    total, acc = None, None
    for s, v in zip(scores, values):
        w = jnp.exp2((s - peak) * C2)
        t = jnp.sum(w, axis=-1, keepdims=True)
        a = pv(w, v)
        total = t if total is None else total + t
        acc = a if acc is None else acc + a
    return peak, total, acc


def video_kernel(meta, q, own, m2, p2, sib, fwd, tk, tv, prev, out):
    lo_p2 = meta[0] == 2
    hi_sib = meta[1] == 3
    hi_fwd = meta[1] == 4
    tiles = []
    for j in range(2):
        far_m, far_p = m2[j], p2[j]
        lo = jnp.where(lo_p2, far_p, far_m)
        hi = jnp.where(hi_fwd, fwd[j], jnp.where(hi_sib, sib[j], far_p))
        tiles.append((own[j], lo, hi))
    key_words = tk[...]
    value_words = tv[...]
    ok = lax.broadcasted_iota(jnp.int32, (1, key_words.shape[0]), 1) < meta[2]
    rows = 128
    for r in range(q.shape[0] // rows):
        qr = q[pl.ds(r * rows, rows), :]
        scores = [qk(qr, k) for k in tiles[0]]
        scores.append(jnp.where(ok, qk(qr, key_words), -jnp.inf))
        _, total, acc = softmax_parts(scores, list(tiles[1]) + [value_words])
        out[pl.ds(r * rows, rows), :] = (acc / total).astype(jnp.bfloat16)


def text_kernel(meta, q, k, v, kt, vt, peak_out, total_out, acc_out):
    h = pl.program_id(0)
    own = kt.shape[0]
    ok = lax.broadcasted_iota(jnp.int32, (1, own), 1) < meta[3]
    scores = [qk(q[...], k[...]), jnp.where(ok, qk(q[...], kt[...]), -jnp.inf)]
    peak, total, acc = softmax_parts(scores, [v[...], vt[...]])
    lane = lax.broadcasted_iota(jnp.int32, peak_out.shape, 1) == h
    peak_out[...] = jnp.where(lane, peak, jnp.where(h == 0, 0.0, peak_out[...]))
    total_out[...] = jnp.where(lane, total, jnp.where(h == 0, 1.0, total_out[...]))
    acc_out[...] = acc


def spread_heads(values, heads):
    return jnp.repeat(values[..., :heads], HD, axis=-1)


def on_device(qv, kv, vv, qt, kt, vt, key_tiles, tile_owner, text_count):
    n = lax.axis_size("ctx")
    me = lax.axis_index("ctx")
    rows, width = qv.shape
    heads = width // HD
    here = qt.shape[0]
    even = me % 2 == 0
    cols = CHUNK * HD
    chunks = heads // CHUNK

    text = lax.all_gather(jnp.stack([qt, kt, vt]), "ctx", axis=1, tiled=True)
    tq, tk, tv = text[0], text[1], text[2]

    tiles = tile_owner.shape[0]
    match = key_tiles[0][:, None] == jnp.arange(tiles, dtype=jnp.int32)[None, :]
    slots = jnp.sum(jnp.where(match, tile_owner[None, :], 0), axis=-1)
    off = slots - me
    near = jnp.where(even == (off == 1), 3, 4)
    code = jnp.where(off == 0, 0, jnp.where(off == -2, 1, jnp.where(off == 2, 2, near)))
    hi = jnp.max(code)
    lo = jnp.sum(code) - hi
    meta = jnp.stack([lo, hi, text_count[0], text_count[0] - me * here]).astype(jnp.int32)

    up = [(i, i - 2) for i in range(2, n)]
    down = [(i, i + 2) for i in range(n - 2)]
    swap = [(i, i ^ 1) for i in range(n)]
    fetched = []
    for c in range(chunks):
        sl = slice(c * cols, (c + 1) * cols)
        own = jnp.stack([kv[:, sl], vv[:, sl]])
        p2 = lax.ppermute(own, "ctx", up)
        m2 = lax.ppermute(own, "ctx", down)
        sib = lax.ppermute(own, "ctx", swap)
        fwd = lax.ppermute(jnp.where(even, p2, m2), "ctx", swap)
        fetched.append((own, m2, p2, sib, fwd))

    col = lambda h: (0, h)
    text_rows = tq.shape[0]
    smem = pl.BlockSpec(memory_space=pltpu.SMEM)
    peak, total, acc = pl.pallas_call(
        text_kernel,
        grid=(heads,),
        in_specs=[
            smem,
            pl.BlockSpec((text_rows, HD), col),
            pl.BlockSpec((rows, HD), col),
            pl.BlockSpec((rows, HD), col),
            pl.BlockSpec((here, HD), col),
            pl.BlockSpec((here, HD), col),
        ],
        out_specs=[
            pl.BlockSpec((text_rows, 128), lambda h: (0, 0)),
            pl.BlockSpec((text_rows, 128), lambda h: (0, 0)),
            pl.BlockSpec((text_rows, HD), col),
        ],
        out_shape=[
            jax.ShapeDtypeStruct((text_rows, 128), jnp.float32),
            jax.ShapeDtypeStruct((text_rows, 128), jnp.float32),
            jax.ShapeDtypeStruct((text_rows, width), jnp.float32),
        ],
        cost_estimate=pl.CostEstimate(
            flops=4 * text_rows * rows * width * 4, bytes_accessed=6 << 20, transcendentals=0
        ),
        name="text_partials",
    )(meta, tq, kv, vv, kt, vt)

    out = jnp.zeros((rows, width), jnp.bfloat16)
    for c in range(chunks):
        own, m2, p2, sib, fwd = fetched[c]
        tile_spec = pl.BlockSpec((2, rows, HD), lambda h: (0, 0, h))
        wide = lambda h, c=c: (0, h + c * CHUNK)
        out = pl.pallas_call(
            video_kernel,
            grid=(CHUNK,),
            in_specs=[smem, pl.BlockSpec((rows, HD), wide)]
            + [tile_spec] * 5
            + [pl.BlockSpec((text_rows, HD), wide)] * 2
            + [pl.BlockSpec(memory_space=pl.ANY)],
            out_specs=pl.BlockSpec((rows, HD), wide),
            out_shape=jax.ShapeDtypeStruct((rows, width), jnp.bfloat16),
            input_output_aliases={9: 0},
            compiler_params=pltpu.CompilerParams(vmem_limit_bytes=32 << 20),
            cost_estimate=pl.CostEstimate(
                flops=4 * rows * (3 * rows + text_rows) * cols * 4,
                bytes_accessed=8 << 20,
                transcendentals=0,
            ),
            name="video_chunk",
        )(meta, qv, own, m2, p2, sib, fwd, tk, tv, out)

    blocks = n
    stats = jnp.stack([peak, total]).reshape(2, blocks, here, 128)
    acc = acc.reshape(blocks, here, width)
    step = 1
    while step < n:
        blocks //= 2
        bit = (me // step) % 2
        pairs = [(i, i ^ step) for i in range(n)]
        stats4 = stats.reshape(2, blocks, 2, here, 128)
        acc4 = acc.reshape(blocks, 2, here, width)
        pick = lambda x, b, ax: jnp.where(
            b == 0, lax.index_in_dim(x, 0, ax, False), lax.index_in_dim(x, 1, ax, False)
        )
        their_s = lax.ppermute(pick(stats4, 1 - bit, 2), "ctx", pairs)
        their_a = lax.ppermute(pick(acc4, 1 - bit, 1), "ctx", pairs)
        my_s = pick(stats4, bit, 2)
        my_a = pick(acc4, bit, 1)
        joint = jnp.maximum(my_s[0], their_s[0])
        f_my = jnp.exp2((my_s[0] - joint) * C2)
        f_their = jnp.exp2((their_s[0] - joint) * C2)
        stats = jnp.stack([joint, my_s[1] * f_my + their_s[1] * f_their])
        acc = my_a * spread_heads(f_my, heads) + their_a * spread_heads(f_their, heads)
        step *= 2
    text_out = (acc[0] / spread_heads(stats[1, 0], heads)).astype(jnp.bfloat16)
    return (out, text_out)


def plane_kernel(n, *refs):
    listed_hbm, owner_hbm, count_hbm = refs[:3]
    q_hbm, k_hbm, v_hbm, qt_hbm, kt_hbm, vt_hbm, out, text_out = refs[3:11]
    heads = q_hbm.shape[1] // HD
    mine = heads // 4
    kv = refs[11 : 11 + mine]
    (
        qb,
        ob,
        tx,
        part,
        got,
        tob,
        list_out,
        list_in,
        lists,
        listed,
        owner,
        count,
        in_send,
        kv_recv,
        q_recv,
        tx_send,
        tx_recv,
        chain_send,
        chain_recv,
        halo_send,
        halo_recv,
        o_send,
        o_recv,
        p_send,
        p_recv,
        t_send,
        t_recv,
        l_send,
        l_recv,
        l_in,
        s_in,
    ) = refs[11 + mine :]
    rows = q_hbm.shape[0]
    here = qt_hbm.shape[0]
    block = 4 * here
    nz = n // 4
    wide = mine * HD
    me = lax.axis_index("ctx")
    g = lax.rem(me, 4)
    core = lax.rem(g, 2)
    side = g // 2
    row = me // 4
    base = row * 4
    sib = g + 1 - 2 * core
    pair = g + 2 - 4 * side
    diag = sib + 2 - 4 * side
    mates = [pair, diag, sib]
    above, below = me + 4, me - 4
    has_above, has_below = row < nz - 1, row > 0
    peers = [lax.rem(row + k, nz) for k in range(1, nz)]
    sources = [lax.rem(row + nz - k, nz) for k in range(1, nz)]

    def cols(start, size):
        return pl.ds(pl.multiple_of(start, HD), size)

    def remote(src, dst, send, recv, dev):
        return pltpu.make_async_remote_copy(
            src_ref=src,
            dst_ref=dst,
            send_sem=send,
            recv_sem=recv,
            device_id={"ctx": dev},
            device_id_type=pl.DeviceIdType.MESH,
        )

    def greet(barrier, dev):
        pl.semaphore_signal(
            barrier, inc=1, device_id={"ctx": dev}, device_id_type=pl.DeviceIdType.MESH
        )

    barrier = pltpu.get_barrier_semaphore()
    for mate in mates:
        greet(barrier, base + mate)
    pl.when(has_above)(lambda: greet(barrier, above))
    pl.when(has_below)(lambda: greet(barrier, below))
    scalars = [
        pltpu.make_async_copy(src, dst, s_in.at[i])
        for i, (src, dst) in enumerate(
            ((listed_hbm, listed), (owner_hbm, owner), (count_hbm, count))
        )
    ]
    for copy in scalars:
        copy.start()

    arrays = (k_hbm, v_hbm, q_hbm)
    text_arrays = (qt_hbm, kt_hbm, vt_hbm)

    def spot(j, x, s):
        return qb.at[j, s] if x == 2 else kv[j].at[2 + s, x]

    def source(j, x, s):
        return arrays[x].at[:, cols((s * mine + j) * HD, HD)]

    def arrival(j, x, s):
        return q_recv.at[j] if x == 2 else kv_recv.at[j, s]

    def own_in(j, x):
        return pltpu.make_async_copy(source(j, x, g), spot(j, x, g), arrival(j, x, g))

    def send_in(j, x, k):
        return remote(
            source(j, x, mates[k]), spot(j, x, g), in_send.at[x], arrival(j, x, g),
            base + mates[k],
        )

    def wait_on(ref, sem):
        pltpu.make_async_copy(ref, ref, sem).wait()

    def own_text(x):
        return pltpu.make_async_copy(
            text_arrays[x].at[:, cols(g * wide, wide)], tx.at[row, x, g], tx_recv
        )

    def send_text(x, k):
        return remote(
            text_arrays[x].at[:, cols(mates[k] * wide, wide)],
            tx.at[row, x, g],
            tx_send,
            tx_recv,
            base + mates[k],
        )

    def send_list(k):
        return remote(list_out, list_in.at[g], l_send, l_recv, base + mates[k])

    for x in range(3):
        own_text(x).start()
    for j in range(mine):
        for x in range(3):
            own_in(j, x).start()
    for copy in scalars:
        copy.wait()
    lane = lax.broadcasted_iota(jnp.int32, list_out.shape, 1)
    spots = jnp.zeros(list_out.shape, jnp.int32)
    for i in range(listed.shape[1]):
        spots = jnp.where(lane == i, owner[listed[0, i]], spots)
    list_out[...] = spots
    list_in[g] = spots

    beside = has_above.astype(jnp.int32) + has_below.astype(jnp.int32)
    pl.semaphore_wait(barrier, 3 + beside)
    for k in range(3):
        for x in range(3):
            send_text(x, k).start()
        send_list(k).start()
    order = [(0, 0), (0, 1), (0, 2)] + [(j, x) for j in range(1, mine) for x in range(2)]
    for j, x in order + [(j, 2) for j in range(1, mine)]:
        for k in range(3):
            send_in(j, x, k).start()

    limit = count[0]
    place = lax.broadcasted_iota(jnp.int32, (1, n * here), 1)
    bias_all = jnp.where(place < limit, 0.0, -jnp.inf).astype(jnp.float32)
    place = row * block + lax.broadcasted_iota(jnp.int32, (1, block), 1)
    bias_own = jnp.where(place < limit, 0.0, -jnp.inf).astype(jnp.float32)

    def chain(z, up):
        return remote(
            tx.at[z], tx.at[z], chain_send.at[0 if up else 1, z], chain_recv.at[z],
            above if up else below,
        )

    def chain_wait(z):
        pltpu.make_async_copy(tx.at[z], tx.at[z], chain_recv.at[z]).wait()

    def chain_step(d):
        up_from, down_from = row - d, row + d
        if d > 0:
            pl.when(up_from >= 0)(lambda: chain_wait(up_from))
        pl.when(jnp.logical_and(up_from >= 0, has_above))(lambda: chain(up_from, True).start())
        if d > 0:
            pl.when(down_from < nz)(lambda: chain_wait(down_from))
        pl.when(jnp.logical_and(down_from < nz, has_below))(
            lambda: chain(down_from, False).start()
        )

    def chain_drain(d):
        up_from, down_from = row - d, row + d
        pl.when(jnp.logical_and(up_from >= 0, has_above))(
            lambda: chain(up_from, True).wait_send()
        )
        pl.when(jnp.logical_and(down_from < nz, has_below))(
            lambda: chain(down_from, False).wait_send()
        )

    halo_to = (6, 7, 0, 1)

    def halo(j, s):
        return remote(
            kv[j].at[2 + s], kv[j].at[halo_to[s]], halo_send.at[j, s // 2],
            halo_recv.at[j, s // 2], below if s < 2 else above,
        )

    def halo_start(j):
        for s in range(4):
            wait_on(kv[j].at[2 + s], kv_recv.at[j, s])
            pl.when(has_below if s < 2 else has_above)(lambda s=s: halo(j, s).start())

    def halo_wait(j):
        pl.when(has_above)(lambda: wait_on(kv[j].at[6:8], halo_recv.at[j, 0]))
        pl.when(has_below)(lambda: wait_on(kv[j].at[0:2], halo_recv.at[j, 1]))

    def halo_drain(j):
        pl.when(has_below)(lambda: wait_on(kv[j].at[2:4], halo_send.at[j, 0]))
        pl.when(has_above)(lambda: wait_on(kv[j].at[4:6], halo_send.at[j, 1]))

    def text_words(x, j):
        return tx[:, x, :, :, j * HD : (j + 1) * HD].reshape(n * here, HD)

    def text_head(j):
        q = text_words(0, j)
        keys = [kv[j][2 + s, 0] for s in range(4)]
        values = [kv[j][2 + s, 1] for s in range(4)]
        own = [tx[row, x, :, :, j * HD : (j + 1) * HD].reshape(block, HD) for x in (1, 2)]
        scores = [qk(q, key) for key in keys] + [qk(q, own[0]) + bias_own]
        peak, total, acc = softmax_parts(scores, values + [own[1]])
        part[j] = acc.reshape(nz, block, HD)
        lane = lax.broadcasted_iota(jnp.int32, (n * here, 128), 1)
        old = part[mine].reshape(n * here, 128) if j else jnp.ones((n * here, 128), jnp.float32)
        new = jnp.where(lane == j, peak, jnp.where(lane == mine + j, total, old))
        part[mine] = new.reshape(nz, block, 128)

    def part_z(j, k):
        return remote(
            part.at[j, peers[k]], got.at[k, j], p_send, p_recv, peers[k] * 4 + g
        )

    def out_spot(j, s):
        return out.at[:, cols((s * mine + j) * HD, HD)]

    def send_out(j, s):
        return remote(ob.at[j, s], out_spot(j, g), o_send, o_recv, base + s)

    def keep_out(j, s):
        return pltpu.make_async_copy(ob.at[j, s], out_spot(j, g), o_recv)

    def video_tile(j, s):
        at = [jnp.clip(lists[s, 0, i] - (base - 2), 0, 7) for i in range(listed.shape[1])]
        keys = [kv[j][i, 0] for i in at] + [text_words(1, j)]
        values = [kv[j][i, 1] for i in at] + [text_words(2, j)]
        step = rows
        for r in range(rows // step):
            qr = qb[j, s, r * step : (r + 1) * step, :]
            scores = [qk(qr, key) for key in keys]
            scores[-1] = scores[-1] + bias_all
            _, total, acc = softmax_parts(scores, values)
            ob[j, s, r * step : (r + 1) * step, :] = (acc / total).astype(jnp.bfloat16)
        pl.when(s == g)(lambda: keep_out(j, s).start())
        pl.when(s != g)(lambda: send_out(j, s).start())

    def video_tiles(j, lo, hi):
        def one(i, _):
            video_tile(j, lax.rem(i + 2 * (1 - side), 4))
            return 0

        lax.fori_loop(lo, hi, one, 0)

    def text_final():
        wait_on(got, p_recv)
        stats = [part[mine, row]] + [got[k, mine] for k in range(nz - 1)]
        for j in range(mine):
            peaks = [x[:, j : j + 1] for x in stats]
            totals = [x[:, mine + j : mine + j + 1] for x in stats]
            accs = [part[j, row]] + [got[k, j] for k in range(nz - 1)]
            joint = functools.reduce(jnp.maximum, peaks)
            weights = [jnp.exp2((p - joint) * C2) for p in peaks]
            total = sum(t * w for t, w in zip(totals, weights))
            acc = sum(a * w for a, w in zip(accs, weights))
            tob[:, :, j * HD : (j + 1) * HD] = (
                (acc / total).astype(jnp.bfloat16).reshape(4, here, HD)
            )

    def text_spot(s):
        return text_out.at[:, cols(s * wide, wide)]

    def send_words(k):
        s = mates[k]
        return remote(tob.at[s], text_spot(g), t_send, t_recv, base + s)

    def keep_words():
        return pltpu.make_async_copy(tob.at[g], text_spot(g), t_recv)

    wait_on(tx.at[row], tx_recv)
    chain_step(0)
    wait_on(list_in.at[0:3], l_recv)
    lists_in = pltpu.make_async_copy(list_in, lists, l_in)
    lists_in.start()
    lists_in.wait()
    for d in range(1, nz - 1):
        chain_step(d)
    halo_start(0)
    pl.when(row - (nz - 1) >= 0)(lambda: chain_wait(row - (nz - 1)))
    pl.when(row + nz - 1 < nz)(lambda: chain_wait(row + nz - 1))

    def text_part(j):
        text_head(j)
        for k in range(nz - 1):
            part_z(j, k).start()
        if j == mine - 1:
            for k in range(nz - 1):
                part_z(mine, k).start()

    def video_wait(j):
        wait_on(qb.at[j], q_recv.at[j])
        halo_wait(j)

    text_part(0)
    video_wait(0)
    video_tiles(0, 0, 4)
    for j in range(1, mine):
        halo_start(j)
        text_part(j)
    for j in range(1, mine):
        video_wait(j)
        if j < mine - 1:
            video_tiles(j, 0, 4)
        else:
            video_tiles(j, 0, 2)
            text_final()
            for k in range(3):
                send_words(k).start()
            keep_words().start()
            video_tiles(j, 2, 4)

    wait_on(out, o_recv)
    wait_on(text_out, t_recv)
    for x in range(3):
        wait_on(arrays[x].at[:, : 3 * wide], in_send.at[x])
    wait_on(q_hbm.at[:, : 3 * wide], o_send)
    wait_on(tx.at[0, :, 0:3], tx_send)
    wait_on(list_in.at[0:3], l_send)
    wait_on(tob.at[0:3], t_send)
    wait_on(got, p_send)
    for j in range(mine):
        halo_drain(j)
    for d in range(nz - 1):
        chain_drain(d)


def fused(qv, kv, vv, qt, kt, vt, key_tiles, tile_owner, text_count):
    n = lax.axis_size("ctx")
    rows, width = qv.shape
    mine = width // HD // 4
    here = qt.shape[0]
    nz = n // 4
    dma = pltpu.SemaphoreType.DMA
    shapes = [
        jax.ShapeDtypeStruct((rows, width), jnp.bfloat16),
        jax.ShapeDtypeStruct((here, width), jnp.bfloat16),
    ]
    anywhere = pl.BlockSpec(memory_space=pl.ANY)
    results = pl.pallas_call(
        functools.partial(plane_kernel, n),
        in_specs=[anywhere] * 9,
        out_specs=[anywhere] * 2,
        out_shape=shapes,
        scratch_shapes=[pltpu.VMEM((8, 2, rows, HD), jnp.bfloat16)] * mine
        + [
            pltpu.VMEM((mine, 4, rows, HD), jnp.bfloat16),
            pltpu.VMEM((mine, 4, rows, HD), jnp.bfloat16),
            pltpu.VMEM((nz, 3, 4, here, mine * HD), jnp.bfloat16),
            pltpu.VMEM((mine + 1, nz, 4 * here, HD), jnp.float32),
            pltpu.VMEM((nz - 1, mine + 1, 4 * here, HD), jnp.float32),
            pltpu.VMEM((4, here, mine * HD), jnp.bfloat16),
            pltpu.VMEM((8, 128), jnp.int32),
            pltpu.VMEM((4, 8, 128), jnp.int32),
            pltpu.SMEM((4, 8, 128), jnp.int32),
            pltpu.SMEM(key_tiles.shape, jnp.int32),
            pltpu.SMEM(tile_owner.shape, jnp.int32),
            pltpu.SMEM(text_count.shape, jnp.int32),
        ]
        + [dma((3,)), dma((mine, 4)), dma((mine,)), dma, dma]
        + [dma((2, nz)), dma((nz,)), dma((mine, 2)), dma((mine, 2))]
        + [dma] * 9
        + [dma((3,))],
        compiler_params=pltpu.CompilerParams(
            collective_id=0, has_side_effects=True, vmem_limit_bytes=56 << 20
        ),
        name="tile_attention",
    )(key_tiles, tile_owner, text_count, qv, kv, vv, qt, kt, vt)
    return results


def whole_device(*args):
    n = lax.axis_size("ctx")
    rows, width = args[0].shape
    here = args[3].shape[0]
    if rows == TILE and n % 4 == 0 and n >= 8 and n & (n - 1) == 0 and here in (16, 32, 64) and width // HD == 12:
        return fused(*args)
    return on_device(*args)


def solution(mesh):
    split = P(("groups", "ctx"), None)
    return jax.shard_map(
        whole_device,
        mesh=mesh,
        in_specs=(split,) * 7 + (P("groups"), P("groups")),
        out_specs=(split, split),
        check_vma=False,
    )
```

```python
import functools
import math

import jax
import jax.numpy as jnp
from jax import lax
from jax.experimental import pallas as pl
from jax.experimental.pallas import tpu as pltpu
from jax.sharding import PartitionSpec as P

TILE = 384
HD = 128
REACH = 2
CHUNK = 3
C2 = math.log2(math.e) / math.sqrt(HD)


def qk(q, k):
    return lax.dot_general(q, k, (((1,), (1,)), ((), ())), preferred_element_type=jnp.float32)


def pv(p, v):
    return lax.dot_general(
        p.astype(jnp.bfloat16), v, (((1,), (0,)), ((), ())), preferred_element_type=jnp.float32
    )


def softmax_parts(scores, values):
    peak = functools.reduce(jnp.maximum, [jnp.max(s, axis=-1, keepdims=True) for s in scores])
    total, acc = None, None
    for s, v in zip(scores, values):
        w = jnp.exp2((s - peak) * C2)
        t = jnp.sum(w, axis=-1, keepdims=True)
        a = pv(w, v)
        total = t if total is None else total + t
        acc = a if acc is None else acc + a
    return peak, total, acc


def video_kernel(meta, q, own, m2, p2, sib, fwd, tk, tv, prev, out):
    lo_p2 = meta[0] == 2
    hi_sib = meta[1] == 3
    hi_fwd = meta[1] == 4
    tiles = []
    for j in range(2):
        far_m, far_p = m2[j], p2[j]
        lo = jnp.where(lo_p2, far_p, far_m)
        hi = jnp.where(hi_fwd, fwd[j], jnp.where(hi_sib, sib[j], far_p))
        tiles.append((own[j], lo, hi))
    key_words = tk[...]
    value_words = tv[...]
    ok = lax.broadcasted_iota(jnp.int32, (1, key_words.shape[0]), 1) < meta[2]
    rows = 128
    for r in range(q.shape[0] // rows):
        qr = q[pl.ds(r * rows, rows), :]
        scores = [qk(qr, k) for k in tiles[0]]
        scores.append(jnp.where(ok, qk(qr, key_words), -jnp.inf))
        _, total, acc = softmax_parts(scores, list(tiles[1]) + [value_words])
        out[pl.ds(r * rows, rows), :] = (acc / total).astype(jnp.bfloat16)


def text_kernel(meta, q, k, v, kt, vt, peak_out, total_out, acc_out):
    h = pl.program_id(0)
    own = kt.shape[0]
    ok = lax.broadcasted_iota(jnp.int32, (1, own), 1) < meta[3]
    scores = [qk(q[...], k[...]), jnp.where(ok, qk(q[...], kt[...]), -jnp.inf)]
    peak, total, acc = softmax_parts(scores, [v[...], vt[...]])
    lane = lax.broadcasted_iota(jnp.int32, peak_out.shape, 1) == h
    peak_out[...] = jnp.where(lane, peak, jnp.where(h == 0, 0.0, peak_out[...]))
    total_out[...] = jnp.where(lane, total, jnp.where(h == 0, 1.0, total_out[...]))
    acc_out[...] = acc


def spread_heads(values, heads):
    return jnp.repeat(values[..., :heads], HD, axis=-1)


def on_device(qv, kv, vv, qt, kt, vt, key_tiles, tile_owner, text_count):
    n = lax.axis_size("ctx")
    me = lax.axis_index("ctx")
    rows, width = qv.shape
    heads = width // HD
    here = qt.shape[0]
    even = me % 2 == 0
    cols = CHUNK * HD
    chunks = heads // CHUNK

    text = lax.all_gather(jnp.stack([qt, kt, vt]), "ctx", axis=1, tiled=True)
    tq, tk, tv = text[0], text[1], text[2]

    tiles = tile_owner.shape[0]
    match = key_tiles[0][:, None] == jnp.arange(tiles, dtype=jnp.int32)[None, :]
    slots = jnp.sum(jnp.where(match, tile_owner[None, :], 0), axis=-1)
    off = slots - me
    near = jnp.where(even == (off == 1), 3, 4)
    code = jnp.where(off == 0, 0, jnp.where(off == -2, 1, jnp.where(off == 2, 2, near)))
    hi = jnp.max(code)
    lo = jnp.sum(code) - hi
    meta = jnp.stack([lo, hi, text_count[0], text_count[0] - me * here]).astype(jnp.int32)

    up = [(i, i - 2) for i in range(2, n)]
    down = [(i, i + 2) for i in range(n - 2)]
    swap = [(i, i ^ 1) for i in range(n)]
    fetched = []
    for c in range(chunks):
        sl = slice(c * cols, (c + 1) * cols)
        own = jnp.stack([kv[:, sl], vv[:, sl]])
        p2 = lax.ppermute(own, "ctx", up)
        m2 = lax.ppermute(own, "ctx", down)
        sib = lax.ppermute(own, "ctx", swap)
        fwd = lax.ppermute(jnp.where(even, p2, m2), "ctx", swap)
        fetched.append((own, m2, p2, sib, fwd))

    col = lambda h: (0, h)
    text_rows = tq.shape[0]
    smem = pl.BlockSpec(memory_space=pltpu.SMEM)
    peak, total, acc = pl.pallas_call(
        text_kernel,
        grid=(heads,),
        in_specs=[
            smem,
            pl.BlockSpec((text_rows, HD), col),
            pl.BlockSpec((rows, HD), col),
            pl.BlockSpec((rows, HD), col),
            pl.BlockSpec((here, HD), col),
            pl.BlockSpec((here, HD), col),
        ],
        out_specs=[
            pl.BlockSpec((text_rows, 128), lambda h: (0, 0)),
            pl.BlockSpec((text_rows, 128), lambda h: (0, 0)),
            pl.BlockSpec((text_rows, HD), col),
        ],
        out_shape=[
            jax.ShapeDtypeStruct((text_rows, 128), jnp.float32),
            jax.ShapeDtypeStruct((text_rows, 128), jnp.float32),
            jax.ShapeDtypeStruct((text_rows, width), jnp.float32),
        ],
        cost_estimate=pl.CostEstimate(
            flops=4 * text_rows * rows * width * 4, bytes_accessed=6 << 20, transcendentals=0
        ),
        name="text_partials",
    )(meta, tq, kv, vv, kt, vt)

    out = jnp.zeros((rows, width), jnp.bfloat16)
    for c in range(chunks):
        own, m2, p2, sib, fwd = fetched[c]
        tile_spec = pl.BlockSpec((2, rows, HD), lambda h: (0, 0, h))
        wide = lambda h, c=c: (0, h + c * CHUNK)
        out = pl.pallas_call(
            video_kernel,
            grid=(CHUNK,),
            in_specs=[smem, pl.BlockSpec((rows, HD), wide)]
            + [tile_spec] * 5
            + [pl.BlockSpec((text_rows, HD), wide)] * 2
            + [pl.BlockSpec(memory_space=pl.ANY)],
            out_specs=pl.BlockSpec((rows, HD), wide),
            out_shape=jax.ShapeDtypeStruct((rows, width), jnp.bfloat16),
            input_output_aliases={9: 0},
            compiler_params=pltpu.CompilerParams(vmem_limit_bytes=32 << 20),
            cost_estimate=pl.CostEstimate(
                flops=4 * rows * (3 * rows + text_rows) * cols * 4,
                bytes_accessed=8 << 20,
                transcendentals=0,
            ),
            name="video_chunk",
        )(meta, qv, own, m2, p2, sib, fwd, tk, tv, out)

    blocks = n
    stats = jnp.stack([peak, total]).reshape(2, blocks, here, 128)
    acc = acc.reshape(blocks, here, width)
    step = 1
    while step < n:
        blocks //= 2
        bit = (me // step) % 2
        pairs = [(i, i ^ step) for i in range(n)]
        stats4 = stats.reshape(2, blocks, 2, here, 128)
        acc4 = acc.reshape(blocks, 2, here, width)
        pick = lambda x, b, ax: jnp.where(
            b == 0, lax.index_in_dim(x, 0, ax, False), lax.index_in_dim(x, 1, ax, False)
        )
        their_s = lax.ppermute(pick(stats4, 1 - bit, 2), "ctx", pairs)
        their_a = lax.ppermute(pick(acc4, 1 - bit, 1), "ctx", pairs)
        my_s = pick(stats4, bit, 2)
        my_a = pick(acc4, bit, 1)
        joint = jnp.maximum(my_s[0], their_s[0])
        f_my = jnp.exp2((my_s[0] - joint) * C2)
        f_their = jnp.exp2((their_s[0] - joint) * C2)
        stats = jnp.stack([joint, my_s[1] * f_my + their_s[1] * f_their])
        acc = my_a * spread_heads(f_my, heads) + their_a * spread_heads(f_their, heads)
        step *= 2
    text_out = (acc[0] / spread_heads(stats[1, 0], heads)).astype(jnp.bfloat16)
    return (out, text_out)


def plane_kernel(n, *refs):
    listed_hbm, owner_hbm, count_hbm = refs[:3]
    q_hbm, k_hbm, v_hbm, qt_hbm, kt_hbm, vt_hbm, out, text_out = refs[3:11]
    heads = q_hbm.shape[1] // HD
    mine = heads // 4
    kv = refs[11 : 11 + mine]
    (
        qb,
        ob,
        tx,
        part,
        stats,
        sums,
        got,
        got_stats,
        tob,
        list_out,
        list_in,
        lists,
        listed,
        owner,
        count,
        in_send,
        kv_recv,
        q_recv,
        tx_send,
        tx_recv,
        chain_send,
        chain_recv,
        halo_send,
        halo_recv,
        o_send,
        o_recv,
        p_send,
        p_recv,
        ps_send,
        ps_recv,
        t_send,
        t_recv,
        l_send,
        l_recv,
        l_in,
        s_in,
    ) = refs[11 + mine :]
    rows = q_hbm.shape[0]
    here = qt_hbm.shape[0]
    block = 4 * here
    nz = n // 4
    wide = mine * HD
    me = lax.axis_index("ctx")
    g = lax.rem(me, 4)
    core = lax.rem(g, 2)
    side = g // 2
    row = me // 4
    base = row * 4
    sib = g + 1 - 2 * core
    pair = g + 2 - 4 * side
    diag = sib + 2 - 4 * side
    mates = [pair, diag, sib]
    above, below = me + 4, me - 4
    has_above, has_below = row < nz - 1, row > 0
    peers = [lax.rem(row + k, nz) for k in range(1, nz)]
    sources = [lax.rem(row + nz - k, nz) for k in range(1, nz)]

    def cols(start, size):
        return pl.ds(pl.multiple_of(start, HD), size)

    def remote(src, dst, send, recv, dev):
        return pltpu.make_async_remote_copy(
            src_ref=src,
            dst_ref=dst,
            send_sem=send,
            recv_sem=recv,
            device_id={"ctx": dev},
            device_id_type=pl.DeviceIdType.MESH,
        )

    def greet(barrier, dev):
        pl.semaphore_signal(
            barrier, inc=1, device_id={"ctx": dev}, device_id_type=pl.DeviceIdType.MESH
        )

    barrier = pltpu.get_barrier_semaphore()
    for mate in mates:
        greet(barrier, base + mate)
    pl.when(has_above)(lambda: greet(barrier, above))
    pl.when(has_below)(lambda: greet(barrier, below))
    scalars = [
        pltpu.make_async_copy(src, dst, s_in.at[i])
        for i, (src, dst) in enumerate(
            ((listed_hbm, listed), (owner_hbm, owner), (count_hbm, count))
        )
    ]
    for copy in scalars:
        copy.start()

    arrays = (k_hbm, v_hbm, q_hbm)
    text_arrays = (qt_hbm, kt_hbm, vt_hbm)

    def spot(j, x, s):
        return qb.at[j, s] if x == 2 else kv[j].at[2 + s, x]

    def source(j, x, s):
        return arrays[x].at[:, cols((s * mine + j) * HD, HD)]

    def arrival(j, x, s):
        return q_recv.at[j] if x == 2 else kv_recv.at[j, x, s]

    def own_in(j, x):
        return pltpu.make_async_copy(source(j, x, g), spot(j, x, g), arrival(j, x, g))

    def send_in(j, x, k):
        return remote(
            source(j, x, mates[k]), spot(j, x, g), in_send.at[x], arrival(j, x, g),
            base + mates[k],
        )

    def wait_on(ref, sem):
        pltpu.make_async_copy(ref, ref, sem).wait()

    def own_text(x):
        return pltpu.make_async_copy(
            text_arrays[x].at[:, cols(g * wide, wide)], tx.at[row, x, g], tx_recv
        )

    def send_text(x, k):
        return remote(
            text_arrays[x].at[:, cols(mates[k] * wide, wide)],
            tx.at[row, x, g],
            tx_send,
            tx_recv,
            base + mates[k],
        )

    def send_list(k):
        return remote(list_out, list_in.at[g], l_send, l_recv, base + mates[k])

    for x in range(3):
        own_text(x).start()
    for j in range(mine):
        for x in range(3):
            own_in(j, x).start()
    for copy in scalars:
        copy.wait()
    lane = lax.broadcasted_iota(jnp.int32, list_out.shape, 1)
    spots = jnp.zeros(list_out.shape, jnp.int32)
    for i in range(listed.shape[1]):
        spots = jnp.where(lane == i, owner[listed[0, i]], spots)
    list_out[...] = spots
    list_in[g] = spots

    beside = has_above.astype(jnp.int32) + has_below.astype(jnp.int32)
    pl.semaphore_wait(barrier, 3 + beside)
    for k in range(3):
        for x in range(3):
            send_text(x, k).start()
        send_list(k).start()
    order = [(j, x) for j in range(mine) for x in range(2)]
    for j, x in order + [(j, 2) for j in range(mine)]:
        for k in range(3):
            send_in(j, x, k).start()

    limit = count[0]
    place = lax.broadcasted_iota(jnp.int32, (1, n * here), 1)
    bias_all = jnp.where(place < limit, 0.0, -jnp.inf).astype(jnp.float32)
    place = row * block + lax.broadcasted_iota(jnp.int32, (1, block), 1)
    bias_own = jnp.where(place < limit, 0.0, -jnp.inf).astype(jnp.float32)

    def chain(z, up):
        return remote(
            tx.at[z], tx.at[z], chain_send.at[0 if up else 1, z], chain_recv.at[z],
            above if up else below,
        )

    def chain_wait(z):
        pltpu.make_async_copy(tx.at[z], tx.at[z], chain_recv.at[z]).wait()

    def chain_step(d):
        up_from, down_from = row - d, row + d
        if d > 0:
            pl.when(up_from >= 0)(lambda: chain_wait(up_from))
        pl.when(jnp.logical_and(up_from >= 0, has_above))(lambda: chain(up_from, True).start())
        if d > 0:
            pl.when(down_from < nz)(lambda: chain_wait(down_from))
        pl.when(jnp.logical_and(down_from < nz, has_below))(
            lambda: chain(down_from, False).start()
        )

    def chain_drain(d):
        up_from, down_from = row - d, row + d
        pl.when(jnp.logical_and(up_from >= 0, has_above))(
            lambda: chain(up_from, True).wait_send()
        )
        pl.when(jnp.logical_and(down_from < nz, has_below))(
            lambda: chain(down_from, False).wait_send()
        )

    def halo_first(far):
        return 2 * (1 - side) if far else 2 * side

    def halo_goes(far):
        up = side == 0 if far else side == 1
        return jnp.logical_or(
            jnp.logical_and(up, has_above), jnp.logical_and(jnp.logical_not(up), has_below)
        )

    def halo(j, far, x, i):
        s = halo_first(far) + i
        return remote(
            kv[j].at[2 + s, x],
            kv[j].at[lax.rem(s + 6, 8), x],
            halo_send.at[j, int(far)],
            halo_recv.at[j, 1 - side if far else side],
            me + 4 - 8 * side if far else me - 4 + 8 * side,
        )

    def halo_start(j, far, arrays=(0, 1)):
        for x in arrays:
            for i in range(2):
                s = halo_first(far) + i
                wait_on(kv[j].at[2 + s, x], kv_recv.at[j, x, s])
                pl.when(halo_goes(far))(lambda x=x, i=i: halo(j, far, x, i).start())

    def halo_wait(j):
        pl.when(has_above)(lambda: wait_on(kv[j].at[6:8], halo_recv.at[j, 0]))
        pl.when(has_below)(lambda: wait_on(kv[j].at[0:2], halo_recv.at[j, 1]))

    def halo_drain(j):
        for far in (True, False):
            pl.when(halo_goes(far))(lambda: wait_on(kv[j].at[2:4], halo_send.at[j, int(far)]))

    def text_words(x, j):
        return tx[:, x, :, :, j * HD : (j + 1) * HD].reshape(n * here, HD)

    def text_head(j):
        q = text_words(0, j)
        keys = [kv[j][2 + s, 0] for s in range(4)]
        values = [kv[j][2 + s, 1] for s in range(4)]
        own = [tx[row, x, :, :, j * HD : (j + 1) * HD].reshape(block, HD) for x in (1, 2)]
        scores = [qk(q, key) for key in keys] + [qk(q, own[0]) + bias_own]
        peak, total, acc = softmax_parts(scores, values + [own[1]])
        part[j] = acc.reshape(nz, block, HD)
        sums[j] = acc.astype(jnp.bfloat16).reshape(nz, block, HD)
        lane = lax.broadcasted_iota(jnp.int32, (n * here, 128), 1)
        old = stats[...].reshape(n * here, 128) if j else jnp.ones((n * here, 128), jnp.float32)
        new = jnp.where(lane == j, peak, jnp.where(lane == mine + j, total, old))
        stats[...] = new.reshape(nz, block, 128)

    def part_z(j, k):
        return remote(
            sums.at[j, peers[k]], got.at[k, j], p_send, p_recv, peers[k] * 4 + g
        )

    def stats_z(k):
        return remote(
            stats.at[peers[k]], got_stats.at[k], ps_send, ps_recv, peers[k] * 4 + g
        )

    def out_spot(j, s):
        return out.at[:, cols((s * mine + j) * HD, HD)]

    def send_out(j, s):
        return remote(ob.at[j, s], out_spot(j, g), o_send, o_recv, base + s)

    def keep_out(j, s):
        return pltpu.make_async_copy(ob.at[j, s], out_spot(j, g), o_recv)

    def video_tile(j, s):
        at = [jnp.clip(lists[s, 0, i] - (base - 2), 0, 7) for i in range(listed.shape[1])]
        keys = [kv[j][i, 0] for i in at] + [text_words(1, j)]
        values = [kv[j][i, 1] for i in at] + [text_words(2, j)]
        step = rows
        for r in range(rows // step):
            qr = qb[j, s, r * step : (r + 1) * step, :]
            scores = [qk(qr, key) for key in keys]
            scores[-1] = scores[-1] + bias_all
            _, total, acc = softmax_parts(scores, values)
            ob[j, s, r * step : (r + 1) * step, :] = (acc / total).astype(jnp.bfloat16)
        pl.when(s == g)(lambda: keep_out(j, s).start())
        pl.when(s != g)(lambda: send_out(j, s).start())

    def video_tiles(j, lo, hi):
        def one(i, _):
            video_tile(j, lax.rem(i + 2 * (1 - side), 4))
            return 0

        lax.fori_loop(lo, hi, one, 0)

    def text_final():
        wait_on(got, p_recv)
        wait_on(got_stats, ps_recv)
        known = [stats[row]] + [got_stats[k] for k in range(nz - 1)]
        for j in range(mine):
            peaks = [x[:, j : j + 1] for x in known]
            totals = [x[:, mine + j : mine + j + 1] for x in known]
            accs = [part[j, row]] + [got[k, j].astype(jnp.float32) for k in range(nz - 1)]
            joint = functools.reduce(jnp.maximum, peaks)
            weights = [jnp.exp2((p - joint) * C2) for p in peaks]
            total = sum(t * w for t, w in zip(totals, weights))
            acc = sum(a * w for a, w in zip(accs, weights))
            tob[:, :, j * HD : (j + 1) * HD] = (
                (acc / total).astype(jnp.bfloat16).reshape(4, here, HD)
            )

    def text_spot(s):
        return text_out.at[:, cols(s * wide, wide)]

    def send_words(k):
        s = mates[k]
        return remote(tob.at[s], text_spot(g), t_send, t_recv, base + s)

    def keep_words():
        return pltpu.make_async_copy(tob.at[g], text_spot(g), t_recv)

    halo_start(0, False, (0,))
    wait_on(tx.at[row], tx_recv)
    chain_step(0)
    halo_start(0, False, (1,))
    wait_on(list_in.at[0:3], l_recv)
    lists_in = pltpu.make_async_copy(list_in, lists, l_in)
    lists_in.start()
    lists_in.wait()
    halo_start(0, True)
    for d in range(1, nz - 1):
        chain_step(d)
        if d < mine:
            halo_start(d, False)
    for j in range(max(1, nz - 1), mine):
        halo_start(j, False)

    def text_part(j):
        text_head(j)
        for k in range(nz - 1):
            part_z(j, k).start()
        if j == mine - 1:
            for k in range(nz - 1):
                stats_z(k).start()

    def video_wait(j):
        wait_on(qb.at[j], q_recv.at[j])
        halo_wait(j)

    halo_start(1, True)
    pl.when(row - (nz - 1) >= 0)(lambda: chain_wait(row - (nz - 1)))
    pl.when(row + nz - 1 < nz)(lambda: chain_wait(row + nz - 1))
    text_part(0)
    halo_start(2, True)
    text_part(1)
    text_part(2)
    for j in range(mine):
        video_wait(j)
        if j < mine - 1:
            video_tiles(j, 0, 4)
        else:
            video_tiles(j, 0, 2)
            text_final()
            for k in range(3):
                send_words(k).start()
            keep_words().start()
            video_tiles(j, 2, 4)

    wait_on(out, o_recv)
    wait_on(text_out, t_recv)
    for x in range(3):
        wait_on(arrays[x].at[:, : 3 * wide], in_send.at[x])
    wait_on(q_hbm.at[:, : 3 * wide], o_send)
    wait_on(tx.at[0, :, 0:3], tx_send)
    wait_on(list_in.at[0:3], l_send)
    wait_on(tob.at[0:3], t_send)
    wait_on(got, p_send)
    wait_on(got_stats, ps_send)
    for j in range(mine):
        halo_drain(j)
    for d in range(nz - 1):
        chain_drain(d)


def fused(qv, kv, vv, qt, kt, vt, key_tiles, tile_owner, text_count):
    n = lax.axis_size("ctx")
    rows, width = qv.shape
    mine = width // HD // 4
    here = qt.shape[0]
    nz = n // 4
    dma = pltpu.SemaphoreType.DMA
    shapes = [
        jax.ShapeDtypeStruct((rows, width), jnp.bfloat16),
        jax.ShapeDtypeStruct((here, width), jnp.bfloat16),
    ]
    anywhere = pl.BlockSpec(memory_space=pl.ANY)
    results = pl.pallas_call(
        functools.partial(plane_kernel, n),
        in_specs=[anywhere] * 9,
        out_specs=[anywhere] * 2,
        out_shape=shapes,
        scratch_shapes=[pltpu.VMEM((8, 2, rows, HD), jnp.bfloat16)] * mine
        + [
            pltpu.VMEM((mine, 4, rows, HD), jnp.bfloat16),
            pltpu.VMEM((mine, 4, rows, HD), jnp.bfloat16),
            pltpu.VMEM((nz, 3, 4, here, mine * HD), jnp.bfloat16),
            pltpu.VMEM((mine, nz, 4 * here, HD), jnp.float32),
            pltpu.VMEM((nz, 4 * here, 128), jnp.float32),
            pltpu.VMEM((mine, nz, 4 * here, HD), jnp.bfloat16),
            pltpu.VMEM((nz - 1, mine, 4 * here, HD), jnp.bfloat16),
            pltpu.VMEM((nz - 1, 4 * here, 128), jnp.float32),
            pltpu.VMEM((4, here, mine * HD), jnp.bfloat16),
            pltpu.VMEM((8, 128), jnp.int32),
            pltpu.VMEM((4, 8, 128), jnp.int32),
            pltpu.SMEM((4, 8, 128), jnp.int32),
            pltpu.SMEM(key_tiles.shape, jnp.int32),
            pltpu.SMEM(tile_owner.shape, jnp.int32),
            pltpu.SMEM(text_count.shape, jnp.int32),
        ]
        + [dma((3,)), dma((mine, 2, 4)), dma((mine,)), dma, dma]
        + [dma((2, nz)), dma((nz,)), dma((mine, 2)), dma((mine, 2))]
        + [dma] * 11
        + [dma((3,))],
        compiler_params=pltpu.CompilerParams(
            collective_id=0, has_side_effects=True, vmem_limit_bytes=56 << 20
        ),
        name="tile_attention",
    )(key_tiles, tile_owner, text_count, qv, kv, vv, qt, kt, vt)
    return results


def whole_device(*args):
    n = lax.axis_size("ctx")
    rows, width = args[0].shape
    here = args[3].shape[0]
    if rows == TILE and n % 4 == 0 and n >= 8 and n & (n - 1) == 0 and here in (16, 32, 64) and width // HD == 12:
        return fused(*args)
    return on_device(*args)


def solution(mesh):
    split = P(("groups", "ctx"), None)
    return jax.shard_map(
        whole_device,
        mesh=mesh,
        in_specs=(split,) * 7 + (P("groups"), P("groups")),
        out_specs=(split, split),
        check_vma=False,
    )
```

```python
import functools
import math

import jax
import jax.numpy as jnp
from jax import lax
from jax.experimental import pallas as pl
from jax.experimental.pallas import tpu as pltpu
from jax.sharding import PartitionSpec as P

TILE = 384
HD = 128
REACH = 2
CHUNK = 3
C2 = math.log2(math.e) / math.sqrt(HD)


def qk(q, k):
    return lax.dot_general(q, k, (((1,), (1,)), ((), ())), preferred_element_type=jnp.float32)


def pv(p, v):
    return lax.dot_general(
        p.astype(jnp.bfloat16), v, (((1,), (0,)), ((), ())), preferred_element_type=jnp.float32
    )


def softmax_parts(scores, values):
    peak = functools.reduce(jnp.maximum, [jnp.max(s, axis=-1, keepdims=True) for s in scores])
    total, acc = None, None
    for s, v in zip(scores, values):
        w = jnp.exp2((s - peak) * C2)
        t = jnp.sum(w, axis=-1, keepdims=True)
        a = pv(w, v)
        total = t if total is None else total + t
        acc = a if acc is None else acc + a
    return peak, total, acc


def video_kernel(meta, q, own, m2, p2, sib, fwd, tk, tv, prev, out):
    lo_p2 = meta[0] == 2
    hi_sib = meta[1] == 3
    hi_fwd = meta[1] == 4
    tiles = []
    for j in range(2):
        far_m, far_p = m2[j], p2[j]
        lo = jnp.where(lo_p2, far_p, far_m)
        hi = jnp.where(hi_fwd, fwd[j], jnp.where(hi_sib, sib[j], far_p))
        tiles.append((own[j], lo, hi))
    key_words = tk[...]
    value_words = tv[...]
    ok = lax.broadcasted_iota(jnp.int32, (1, key_words.shape[0]), 1) < meta[2]
    rows = 128
    for r in range(q.shape[0] // rows):
        qr = q[pl.ds(r * rows, rows), :]
        scores = [qk(qr, k) for k in tiles[0]]
        scores.append(jnp.where(ok, qk(qr, key_words), -jnp.inf))
        _, total, acc = softmax_parts(scores, list(tiles[1]) + [value_words])
        out[pl.ds(r * rows, rows), :] = (acc / total).astype(jnp.bfloat16)


def text_kernel(meta, q, k, v, kt, vt, peak_out, total_out, acc_out):
    h = pl.program_id(0)
    own = kt.shape[0]
    ok = lax.broadcasted_iota(jnp.int32, (1, own), 1) < meta[3]
    scores = [qk(q[...], k[...]), jnp.where(ok, qk(q[...], kt[...]), -jnp.inf)]
    peak, total, acc = softmax_parts(scores, [v[...], vt[...]])
    lane = lax.broadcasted_iota(jnp.int32, peak_out.shape, 1) == h
    peak_out[...] = jnp.where(lane, peak, jnp.where(h == 0, 0.0, peak_out[...]))
    total_out[...] = jnp.where(lane, total, jnp.where(h == 0, 1.0, total_out[...]))
    acc_out[...] = acc


def spread_heads(values, heads):
    return jnp.repeat(values[..., :heads], HD, axis=-1)


def on_device(qv, kv, vv, qt, kt, vt, key_tiles, tile_owner, text_count):
    n = lax.axis_size("ctx")
    me = lax.axis_index("ctx")
    rows, width = qv.shape
    heads = width // HD
    here = qt.shape[0]
    even = me % 2 == 0
    cols = CHUNK * HD
    chunks = heads // CHUNK

    text = lax.all_gather(jnp.stack([qt, kt, vt]), "ctx", axis=1, tiled=True)
    tq, tk, tv = text[0], text[1], text[2]

    tiles = tile_owner.shape[0]
    match = key_tiles[0][:, None] == jnp.arange(tiles, dtype=jnp.int32)[None, :]
    slots = jnp.sum(jnp.where(match, tile_owner[None, :], 0), axis=-1)
    off = slots - me
    near = jnp.where(even == (off == 1), 3, 4)
    code = jnp.where(off == 0, 0, jnp.where(off == -2, 1, jnp.where(off == 2, 2, near)))
    hi = jnp.max(code)
    lo = jnp.sum(code) - hi
    meta = jnp.stack([lo, hi, text_count[0], text_count[0] - me * here]).astype(jnp.int32)

    up = [(i, i - 2) for i in range(2, n)]
    down = [(i, i + 2) for i in range(n - 2)]
    swap = [(i, i ^ 1) for i in range(n)]
    fetched = []
    for c in range(chunks):
        sl = slice(c * cols, (c + 1) * cols)
        own = jnp.stack([kv[:, sl], vv[:, sl]])
        p2 = lax.ppermute(own, "ctx", up)
        m2 = lax.ppermute(own, "ctx", down)
        sib = lax.ppermute(own, "ctx", swap)
        fwd = lax.ppermute(jnp.where(even, p2, m2), "ctx", swap)
        fetched.append((own, m2, p2, sib, fwd))

    col = lambda h: (0, h)
    text_rows = tq.shape[0]
    smem = pl.BlockSpec(memory_space=pltpu.SMEM)
    peak, total, acc = pl.pallas_call(
        text_kernel,
        grid=(heads,),
        in_specs=[
            smem,
            pl.BlockSpec((text_rows, HD), col),
            pl.BlockSpec((rows, HD), col),
            pl.BlockSpec((rows, HD), col),
            pl.BlockSpec((here, HD), col),
            pl.BlockSpec((here, HD), col),
        ],
        out_specs=[
            pl.BlockSpec((text_rows, 128), lambda h: (0, 0)),
            pl.BlockSpec((text_rows, 128), lambda h: (0, 0)),
            pl.BlockSpec((text_rows, HD), col),
        ],
        out_shape=[
            jax.ShapeDtypeStruct((text_rows, 128), jnp.float32),
            jax.ShapeDtypeStruct((text_rows, 128), jnp.float32),
            jax.ShapeDtypeStruct((text_rows, width), jnp.float32),
        ],
        cost_estimate=pl.CostEstimate(
            flops=4 * text_rows * rows * width * 4, bytes_accessed=6 << 20, transcendentals=0
        ),
        name="text_partials",
    )(meta, tq, kv, vv, kt, vt)

    out = jnp.zeros((rows, width), jnp.bfloat16)
    for c in range(chunks):
        own, m2, p2, sib, fwd = fetched[c]
        tile_spec = pl.BlockSpec((2, rows, HD), lambda h: (0, 0, h))
        wide = lambda h, c=c: (0, h + c * CHUNK)
        out = pl.pallas_call(
            video_kernel,
            grid=(CHUNK,),
            in_specs=[smem, pl.BlockSpec((rows, HD), wide)]
            + [tile_spec] * 5
            + [pl.BlockSpec((text_rows, HD), wide)] * 2
            + [pl.BlockSpec(memory_space=pl.ANY)],
            out_specs=pl.BlockSpec((rows, HD), wide),
            out_shape=jax.ShapeDtypeStruct((rows, width), jnp.bfloat16),
            input_output_aliases={9: 0},
            compiler_params=pltpu.CompilerParams(vmem_limit_bytes=32 << 20),
            cost_estimate=pl.CostEstimate(
                flops=4 * rows * (3 * rows + text_rows) * cols * 4,
                bytes_accessed=8 << 20,
                transcendentals=0,
            ),
            name="video_chunk",
        )(meta, qv, own, m2, p2, sib, fwd, tk, tv, out)

    blocks = n
    stats = jnp.stack([peak, total]).reshape(2, blocks, here, 128)
    acc = acc.reshape(blocks, here, width)
    step = 1
    while step < n:
        blocks //= 2
        bit = (me // step) % 2
        pairs = [(i, i ^ step) for i in range(n)]
        stats4 = stats.reshape(2, blocks, 2, here, 128)
        acc4 = acc.reshape(blocks, 2, here, width)
        pick = lambda x, b, ax: jnp.where(
            b == 0, lax.index_in_dim(x, 0, ax, False), lax.index_in_dim(x, 1, ax, False)
        )
        their_s = lax.ppermute(pick(stats4, 1 - bit, 2), "ctx", pairs)
        their_a = lax.ppermute(pick(acc4, 1 - bit, 1), "ctx", pairs)
        my_s = pick(stats4, bit, 2)
        my_a = pick(acc4, bit, 1)
        joint = jnp.maximum(my_s[0], their_s[0])
        f_my = jnp.exp2((my_s[0] - joint) * C2)
        f_their = jnp.exp2((their_s[0] - joint) * C2)
        stats = jnp.stack([joint, my_s[1] * f_my + their_s[1] * f_their])
        acc = my_a * spread_heads(f_my, heads) + their_a * spread_heads(f_their, heads)
        step *= 2
    text_out = (acc[0] / spread_heads(stats[1, 0], heads)).astype(jnp.bfloat16)
    return (out, text_out)


def plane_kernel(n, *refs):
    listed_hbm, owner_hbm, count_hbm = refs[:3]
    q_hbm, k_hbm, v_hbm, qt_hbm, kt_hbm, vt_hbm, out, text_out = refs[3:11]
    heads = q_hbm.shape[1] // HD
    mine = heads // 4
    kv = refs[11 : 11 + mine]
    (
        qb,
        ob,
        tx,
        part,
        stats,
        flat,
        got,
        got_stats,
        tall,
        tob,
        list_out,
        list_in,
        lists,
        listed,
        owner,
        count,
        in_send,
        kv_recv,
        q_recv,
        tx_send,
        tx_recv,
        chain_send,
        chain_recv,
        halo_send,
        halo_recv,
        o_send,
        o_recv,
        p_send,
        p_recv,
        ps_send,
        ps_recv,
        t_send,
        t_recv,
        l_send,
        l_recv,
        l_in,
        s_in,
    ) = refs[11 + mine :]
    rows = q_hbm.shape[0]
    here = qt_hbm.shape[0]
    block = 4 * here
    nz = n // 4
    wide = mine * HD
    me = lax.axis_index("ctx")
    g = lax.rem(me, 4)
    core = lax.rem(g, 2)
    side = g // 2
    row = me // 4
    base = row * 4
    sib = g + 1 - 2 * core
    pair = g + 2 - 4 * side
    diag = sib + 2 - 4 * side
    mates = [pair, diag, sib]
    above, below = me + 4, me - 4
    has_above, has_below = row < nz - 1, row > 0
    peers = [lax.rem(row + k, nz) for k in range(1, nz)]
    sources = [lax.rem(row + nz - k, nz) for k in range(1, nz)]

    def cols(start, size):
        return pl.ds(pl.multiple_of(start, HD), size)

    def remote(src, dst, send, recv, dev):
        return pltpu.make_async_remote_copy(
            src_ref=src,
            dst_ref=dst,
            send_sem=send,
            recv_sem=recv,
            device_id={"ctx": dev},
            device_id_type=pl.DeviceIdType.MESH,
        )

    def greet(barrier, dev):
        pl.semaphore_signal(
            barrier, inc=1, device_id={"ctx": dev}, device_id_type=pl.DeviceIdType.MESH
        )

    barrier = pltpu.get_barrier_semaphore()
    for mate in mates:
        greet(barrier, base + mate)
    pl.when(has_above)(lambda: greet(barrier, above))
    pl.when(has_below)(lambda: greet(barrier, below))
    scalars = [
        pltpu.make_async_copy(src, dst, s_in.at[i])
        for i, (src, dst) in enumerate(
            ((listed_hbm, listed), (owner_hbm, owner), (count_hbm, count))
        )
    ]
    for copy in scalars:
        copy.start()

    arrays = (k_hbm, v_hbm, q_hbm)
    text_arrays = (qt_hbm, kt_hbm, vt_hbm)

    def spot(j, x, s):
        return qb.at[j, s] if x == 2 else kv[j].at[2 + s, x]

    def source(j, x, s):
        return arrays[x].at[:, cols((s * mine + j) * HD, HD)]

    def arrival(j, x, s):
        return q_recv.at[j] if x == 2 else kv_recv.at[j, x, s]

    def own_in(j, x):
        return pltpu.make_async_copy(source(j, x, g), spot(j, x, g), arrival(j, x, g))

    def send_in(j, x, k):
        return remote(
            source(j, x, mates[k]), spot(j, x, g), in_send.at[x], arrival(j, x, g),
            base + mates[k],
        )

    def wait_on(ref, sem):
        pltpu.make_async_copy(ref, ref, sem).wait()

    def own_text(x):
        return pltpu.make_async_copy(
            text_arrays[x].at[:, cols(g * wide, wide)], tx.at[row, x, g], tx_recv
        )

    def send_text(x, k):
        return remote(
            text_arrays[x].at[:, cols(mates[k] * wide, wide)],
            tx.at[row, x, g],
            tx_send,
            tx_recv,
            base + mates[k],
        )

    def send_list(k):
        return remote(list_out, list_in.at[g], l_send, l_recv, base + mates[k])

    for x in range(3):
        own_text(x).start()
    for j in range(mine):
        for x in range(3):
            own_in(j, x).start()
    for copy in scalars:
        copy.wait()
    lane = lax.broadcasted_iota(jnp.int32, list_out.shape, 1)
    spots = jnp.zeros(list_out.shape, jnp.int32)
    for i in range(listed.shape[1]):
        spots = jnp.where(lane == i, owner[listed[0, i]], spots)
    list_out[...] = spots
    list_in[g] = spots

    beside = has_above.astype(jnp.int32) + has_below.astype(jnp.int32)
    pl.semaphore_wait(barrier, 3 + beside)
    for k in range(3):
        for x in range(3):
            send_text(x, k).start()
        send_list(k).start()
    order = [(j, x) for j in range(mine) for x in range(2)]
    for j, x in order + [(j, 2) for j in range(mine)]:
        for k in range(3):
            send_in(j, x, k).start()

    limit = count[0]
    place = lax.broadcasted_iota(jnp.int32, (1, n * here), 1)
    bias_all = jnp.where(place < limit, 0.0, -jnp.inf).astype(jnp.float32)
    place = row * block + lax.broadcasted_iota(jnp.int32, (1, block), 1)
    bias_own = jnp.where(place < limit, 0.0, -jnp.inf).astype(jnp.float32)

    def chain(z, up):
        return remote(
            tx.at[z], tx.at[z], chain_send.at[0 if up else 1, z], chain_recv.at[z],
            above if up else below,
        )

    def chain_wait(z):
        pltpu.make_async_copy(tx.at[z], tx.at[z], chain_recv.at[z]).wait()

    def chain_step(d):
        up_from, down_from = row - d, row + d
        if d > 0:
            pl.when(up_from >= 0)(lambda: chain_wait(up_from))
        pl.when(jnp.logical_and(up_from >= 0, has_above))(lambda: chain(up_from, True).start())
        if d > 0:
            pl.when(down_from < nz)(lambda: chain_wait(down_from))
        pl.when(jnp.logical_and(down_from < nz, has_below))(
            lambda: chain(down_from, False).start()
        )

    def chain_drain(d):
        up_from, down_from = row - d, row + d
        pl.when(jnp.logical_and(up_from >= 0, has_above))(
            lambda: chain(up_from, True).wait_send()
        )
        pl.when(jnp.logical_and(down_from < nz, has_below))(
            lambda: chain(down_from, False).wait_send()
        )

    def halo_first(far):
        return 2 * (1 - side) if far else 2 * side

    def halo_goes(far):
        up = side == 0 if far else side == 1
        return jnp.logical_or(
            jnp.logical_and(up, has_above), jnp.logical_and(jnp.logical_not(up), has_below)
        )

    def halo(j, far, x, i):
        s = halo_first(far) + i
        return remote(
            kv[j].at[2 + s, x],
            kv[j].at[lax.rem(s + 6, 8), x],
            halo_send.at[j, int(far)],
            halo_recv.at[j, 1 - side if far else side],
            me + 4 - 8 * side if far else me - 4 + 8 * side,
        )

    def halo_start(j, far, arrays=(0, 1)):
        for x in arrays:
            for i in range(2):
                s = halo_first(far) + i
                wait_on(kv[j].at[2 + s, x], kv_recv.at[j, x, s])
                pl.when(halo_goes(far))(lambda x=x, i=i: halo(j, far, x, i).start())

    def halo_wait(j):
        pl.when(has_above)(lambda: wait_on(kv[j].at[6:8], halo_recv.at[j, 0]))
        pl.when(has_below)(lambda: wait_on(kv[j].at[0:2], halo_recv.at[j, 1]))

    def halo_drain(j):
        for far in (True, False):
            pl.when(halo_goes(far))(lambda: wait_on(kv[j].at[2:4], halo_send.at[j, int(far)]))

    def text_words(x, j):
        return tx[:, x, :, :, j * HD : (j + 1) * HD].reshape(n * here, HD)

    def text_head(j):
        q = text_words(0, j)
        keys = [kv[j][2 + s, 0] for s in range(4)]
        values = [kv[j][2 + s, 1] for s in range(4)]
        own = [tx[row, x, :, :, j * HD : (j + 1) * HD].reshape(block, HD) for x in (1, 2)]
        scores = [qk(q, key) for key in keys] + [qk(q, own[0]) + bias_own]
        peak, total, acc = softmax_parts(scores, values + [own[1]])
        part[j] = acc.reshape(nz, block, HD)
        lane = lax.broadcasted_iota(jnp.int32, stats.shape, 1)
        old = stats[...] if j else jnp.ones(stats.shape, jnp.float32)
        stats[...] = jnp.where(lane == j, peak, jnp.where(lane == mine + j, total, old))
        if j == mine - 1:
            flat[...] = jnp.transpose(stats[...])[:8, :]

    def part_z(j, k):
        return remote(
            part.at[j, peers[k]], got.at[k, j], p_send, p_recv, peers[k] * 4 + g
        )

    def stats_z(k):
        return remote(flat, got_stats.at[k], ps_send, ps_recv, peers[k] * 4 + g)

    def out_spot(j, s):
        return out.at[:, cols((s * mine + j) * HD, HD)]

    def send_out(j, s):
        return remote(ob.at[j, s], out_spot(j, g), o_send, o_recv, base + s)

    def keep_out(j, s):
        return pltpu.make_async_copy(ob.at[j, s], out_spot(j, g), o_recv)

    def video_tile(j, s):
        at = [jnp.clip(lists[s, 0, i] - (base - 2), 0, 7) for i in range(listed.shape[1])]
        keys = [kv[j][i, 0] for i in at] + [text_words(1, j)]
        values = [kv[j][i, 1] for i in at] + [text_words(2, j)]
        step = rows
        for r in range(rows // step):
            qr = qb[j, s, r * step : (r + 1) * step, :]
            scores = [qk(qr, key) for key in keys]
            scores[-1] = scores[-1] + bias_all
            _, total, acc = softmax_parts(scores, values)
            ob[j, s, r * step : (r + 1) * step, :] = (acc / total).astype(jnp.bfloat16)
        pl.when(s == g)(lambda: keep_out(j, s).start())
        pl.when(s != g)(lambda: send_out(j, s).start())

    def video_tiles(j, lo, hi):
        def one(i, _):
            video_tile(j, lax.rem(i + 2 * (1 - side), 4))
            return 0

        lax.fori_loop(lo, hi, one, 0)

    def text_final():
        wait_on(got, p_recv)
        wait_on(got_stats, ps_recv)
        rows_here = pl.ds(pl.multiple_of(row * block, block), block)
        known = [stats[rows_here, :]]
        for k in range(nz - 1):
            full = jnp.concatenate([got_stats[k]] + [jnp.zeros_like(got_stats[k])] * 15, axis=0)
            tall[k] = jnp.transpose(full)
            known.append(tall[k, rows_here, :])
        for j in range(mine):
            peaks = [x[:, j : j + 1] for x in known]
            totals = [x[:, mine + j : mine + j + 1] for x in known]
            accs = [part[j, row]] + [got[k, j] for k in range(nz - 1)]
            joint = functools.reduce(jnp.maximum, peaks)
            weights = [jnp.exp2((p - joint) * C2) for p in peaks]
            total = sum(t * w for t, w in zip(totals, weights))
            acc = sum(a * w for a, w in zip(accs, weights))
            tob[:, :, j * HD : (j + 1) * HD] = (
                (acc / total).astype(jnp.bfloat16).reshape(4, here, HD)
            )

    def text_spot(s):
        return text_out.at[:, cols(s * wide, wide)]

    def send_words(k):
        s = mates[k]
        return remote(tob.at[s], text_spot(g), t_send, t_recv, base + s)

    def keep_words():
        return pltpu.make_async_copy(tob.at[g], text_spot(g), t_recv)

    halo_start(0, False, (0,))
    wait_on(tx.at[row], tx_recv)
    chain_step(0)
    halo_start(0, False, (1,))
    wait_on(list_in.at[0:3], l_recv)
    lists_in = pltpu.make_async_copy(list_in, lists, l_in)
    lists_in.start()
    lists_in.wait()
    halo_start(0, True)
    for d in range(1, nz - 1):
        chain_step(d)
        if d < mine:
            halo_start(d, False)
    for j in range(max(1, nz - 1), mine):
        halo_start(j, False)

    def text_part(j):
        text_head(j)
        for k in range(nz - 1):
            part_z(j, k).start()
        if j == mine - 1:
            for k in range(nz - 1):
                stats_z(k).start()

    def video_wait(j):
        wait_on(qb.at[j], q_recv.at[j])
        halo_wait(j)

    halo_start(1, True)
    pl.when(row - (nz - 1) >= 0)(lambda: chain_wait(row - (nz - 1)))
    pl.when(row + nz - 1 < nz)(lambda: chain_wait(row + nz - 1))
    text_part(0)
    halo_start(2, True)
    text_part(1)
    text_part(2)
    for j in range(mine):
        video_wait(j)
        if j < mine - 1:
            video_tiles(j, 0, 4)
        else:
            video_tiles(j, 0, 2)
            text_final()
            for k in range(3):
                send_words(k).start()
            keep_words().start()
            video_tiles(j, 2, 4)

    wait_on(out, o_recv)
    wait_on(text_out, t_recv)
    for x in range(3):
        wait_on(arrays[x].at[:, : 3 * wide], in_send.at[x])
    wait_on(q_hbm.at[:, : 3 * wide], o_send)
    wait_on(tx.at[0, :, 0:3], tx_send)
    wait_on(list_in.at[0:3], l_send)
    wait_on(tob.at[0:3], t_send)
    wait_on(got, p_send)
    wait_on(got_stats, ps_send)
    for j in range(mine):
        halo_drain(j)
    for d in range(nz - 1):
        chain_drain(d)


def deliver(pieces, video, text, video_out, text_out, sems):
    rows = video.shape[0] // pieces
    copies = [
        pltpu.make_async_copy(
            video.at[i * rows : (i + 1) * rows], video_out.at[i * rows : (i + 1) * rows], sems.at[i]
        )
        for i in range(pieces)
    ]
    copies.append(pltpu.make_async_copy(text, text_out, sems.at[pieces]))
    for copy in copies:
        copy.start()
    for copy in copies:
        copy.wait()


def fused(qv, kv, vv, qt, kt, vt, key_tiles, tile_owner, text_count):
    n = lax.axis_size("ctx")
    rows, width = qv.shape
    mine = width // HD // 4
    here = qt.shape[0]
    nz = n // 4
    dma = pltpu.SemaphoreType.DMA
    shapes = [
        jax.ShapeDtypeStruct((rows, width), jnp.bfloat16),
        jax.ShapeDtypeStruct((here, width), jnp.bfloat16),
    ]
    anywhere = pl.BlockSpec(memory_space=pl.ANY)
    results = pl.pallas_call(
        functools.partial(plane_kernel, n),
        in_specs=[pl.BlockSpec(memory_space=pltpu.HBM)] * 9,
        out_specs=[pl.BlockSpec(memory_space=pltpu.VMEM)] * 2,
        out_shape=[pltpu.VMEM(x.shape, x.dtype) for x in shapes],
        scratch_shapes=[pltpu.VMEM((8, 2, rows, HD), jnp.bfloat16)] * mine
        + [
            pltpu.VMEM((mine, 4, rows, HD), jnp.bfloat16),
            pltpu.VMEM((mine, 4, rows, HD), jnp.bfloat16),
            pltpu.VMEM((nz, 3, 4, here, mine * HD), jnp.bfloat16),
            pltpu.VMEM((mine, nz, 4 * here, HD), jnp.float32),
            pltpu.VMEM((n * here, 128), jnp.float32),
            pltpu.VMEM((8, n * here), jnp.float32),
            pltpu.VMEM((nz - 1, mine, 4 * here, HD), jnp.float32),
            pltpu.VMEM((nz - 1, 8, n * here), jnp.float32),
            pltpu.VMEM((nz - 1, n * here, 128), jnp.float32),
            pltpu.VMEM((4, here, mine * HD), jnp.bfloat16),
            pltpu.VMEM((8, 128), jnp.int32),
            pltpu.VMEM((4, 8, 128), jnp.int32),
            pltpu.SMEM((4, 8, 128), jnp.int32),
            pltpu.SMEM(key_tiles.shape, jnp.int32),
            pltpu.SMEM(tile_owner.shape, jnp.int32),
            pltpu.SMEM(text_count.shape, jnp.int32),
        ]
        + [dma((3,)), dma((mine, 2, 4)), dma((mine,)), dma, dma]
        + [dma((2, nz)), dma((nz,)), dma((mine, 2)), dma((mine, 2))]
        + [dma] * 11
        + [dma((3,))],
        compiler_params=pltpu.CompilerParams(
            collective_id=0, has_side_effects=True, vmem_limit_bytes=125 << 19
        ),
        name="tile_attention",
    )(key_tiles, tile_owner, text_count, qv, kv, vv, qt, kt, vt)
    return results


def whole_device(*args):
    n = lax.axis_size("ctx")
    rows, width = args[0].shape
    here = args[3].shape[0]
    if rows == TILE and n % 4 == 0 and n >= 8 and n & (n - 1) == 0 and here in (16, 32, 64) and width // HD == 12:
        return fused(*args)
    return on_device(*args)


def solution(mesh):
    split = P(("groups", "ctx"), None)
    return jax.shard_map(
        whole_device,
        mesh=mesh,
        in_specs=(split,) * 7 + (P("groups"), P("groups")),
        out_specs=(split, split),
        check_vma=False,
    )
```

```python
import functools
import math

import jax
import jax.numpy as jnp
from jax import lax
from jax.experimental import pallas as pl
from jax.experimental.pallas import tpu as pltpu
from jax.sharding import PartitionSpec as P

TILE = 384
HD = 128
REACH = 2
CHUNK = 3
C2 = math.log2(math.e) / math.sqrt(HD)


def qk(q, k):
    return lax.dot_general(q, k, (((1,), (1,)), ((), ())), preferred_element_type=jnp.float32)


def pv(p, v):
    return lax.dot_general(
        p.astype(jnp.bfloat16), v, (((1,), (0,)), ((), ())), preferred_element_type=jnp.float32
    )


def softmax_parts(scores, values):
    peak = functools.reduce(jnp.maximum, [jnp.max(s, axis=-1, keepdims=True) for s in scores])
    total, acc = None, None
    for s, v in zip(scores, values):
        w = jnp.exp2((s - peak) * C2)
        t = jnp.sum(w, axis=-1, keepdims=True)
        a = pv(w, v)
        total = t if total is None else total + t
        acc = a if acc is None else acc + a
    return peak, total, acc


def video_kernel(meta, q, own, m2, p2, sib, fwd, tk, tv, prev, out):
    lo_p2 = meta[0] == 2
    hi_sib = meta[1] == 3
    hi_fwd = meta[1] == 4
    tiles = []
    for j in range(2):
        far_m, far_p = m2[j], p2[j]
        lo = jnp.where(lo_p2, far_p, far_m)
        hi = jnp.where(hi_fwd, fwd[j], jnp.where(hi_sib, sib[j], far_p))
        tiles.append((own[j], lo, hi))
    key_words = tk[...]
    value_words = tv[...]
    ok = lax.broadcasted_iota(jnp.int32, (1, key_words.shape[0]), 1) < meta[2]
    rows = 128
    for r in range(q.shape[0] // rows):
        qr = q[pl.ds(r * rows, rows), :]
        scores = [qk(qr, k) for k in tiles[0]]
        scores.append(jnp.where(ok, qk(qr, key_words), -jnp.inf))
        _, total, acc = softmax_parts(scores, list(tiles[1]) + [value_words])
        out[pl.ds(r * rows, rows), :] = (acc / total).astype(jnp.bfloat16)


def text_kernel(meta, q, k, v, kt, vt, peak_out, total_out, acc_out):
    h = pl.program_id(0)
    own = kt.shape[0]
    ok = lax.broadcasted_iota(jnp.int32, (1, own), 1) < meta[3]
    scores = [qk(q[...], k[...]), jnp.where(ok, qk(q[...], kt[...]), -jnp.inf)]
    peak, total, acc = softmax_parts(scores, [v[...], vt[...]])
    lane = lax.broadcasted_iota(jnp.int32, peak_out.shape, 1) == h
    peak_out[...] = jnp.where(lane, peak, jnp.where(h == 0, 0.0, peak_out[...]))
    total_out[...] = jnp.where(lane, total, jnp.where(h == 0, 1.0, total_out[...]))
    acc_out[...] = acc


def spread_heads(values, heads):
    return jnp.repeat(values[..., :heads], HD, axis=-1)


def on_device(qv, kv, vv, qt, kt, vt, key_tiles, tile_owner, text_count):
    n = lax.axis_size("ctx")
    me = lax.axis_index("ctx")
    rows, width = qv.shape
    heads = width // HD
    here = qt.shape[0]
    even = me % 2 == 0
    cols = CHUNK * HD
    chunks = heads // CHUNK

    text = lax.all_gather(jnp.stack([qt, kt, vt]), "ctx", axis=1, tiled=True)
    tq, tk, tv = text[0], text[1], text[2]

    tiles = tile_owner.shape[0]
    match = key_tiles[0][:, None] == jnp.arange(tiles, dtype=jnp.int32)[None, :]
    slots = jnp.sum(jnp.where(match, tile_owner[None, :], 0), axis=-1)
    off = slots - me
    near = jnp.where(even == (off == 1), 3, 4)
    code = jnp.where(off == 0, 0, jnp.where(off == -2, 1, jnp.where(off == 2, 2, near)))
    hi = jnp.max(code)
    lo = jnp.sum(code) - hi
    meta = jnp.stack([lo, hi, text_count[0], text_count[0] - me * here]).astype(jnp.int32)

    up = [(i, i - 2) for i in range(2, n)]
    down = [(i, i + 2) for i in range(n - 2)]
    swap = [(i, i ^ 1) for i in range(n)]
    fetched = []
    for c in range(chunks):
        sl = slice(c * cols, (c + 1) * cols)
        own = jnp.stack([kv[:, sl], vv[:, sl]])
        p2 = lax.ppermute(own, "ctx", up)
        m2 = lax.ppermute(own, "ctx", down)
        sib = lax.ppermute(own, "ctx", swap)
        fwd = lax.ppermute(jnp.where(even, p2, m2), "ctx", swap)
        fetched.append((own, m2, p2, sib, fwd))

    col = lambda h: (0, h)
    text_rows = tq.shape[0]
    smem = pl.BlockSpec(memory_space=pltpu.SMEM)
    peak, total, acc = pl.pallas_call(
        text_kernel,
        grid=(heads,),
        in_specs=[
            smem,
            pl.BlockSpec((text_rows, HD), col),
            pl.BlockSpec((rows, HD), col),
            pl.BlockSpec((rows, HD), col),
            pl.BlockSpec((here, HD), col),
            pl.BlockSpec((here, HD), col),
        ],
        out_specs=[
            pl.BlockSpec((text_rows, 128), lambda h: (0, 0)),
            pl.BlockSpec((text_rows, 128), lambda h: (0, 0)),
            pl.BlockSpec((text_rows, HD), col),
        ],
        out_shape=[
            jax.ShapeDtypeStruct((text_rows, 128), jnp.float32),
            jax.ShapeDtypeStruct((text_rows, 128), jnp.float32),
            jax.ShapeDtypeStruct((text_rows, width), jnp.float32),
        ],
        cost_estimate=pl.CostEstimate(
            flops=4 * text_rows * rows * width * 4, bytes_accessed=6 << 20, transcendentals=0
        ),
        name="text_partials",
    )(meta, tq, kv, vv, kt, vt)

    out = jnp.zeros((rows, width), jnp.bfloat16)
    for c in range(chunks):
        own, m2, p2, sib, fwd = fetched[c]
        tile_spec = pl.BlockSpec((2, rows, HD), lambda h: (0, 0, h))
        wide = lambda h, c=c: (0, h + c * CHUNK)
        out = pl.pallas_call(
            video_kernel,
            grid=(CHUNK,),
            in_specs=[smem, pl.BlockSpec((rows, HD), wide)]
            + [tile_spec] * 5
            + [pl.BlockSpec((text_rows, HD), wide)] * 2
            + [pl.BlockSpec(memory_space=pl.ANY)],
            out_specs=pl.BlockSpec((rows, HD), wide),
            out_shape=jax.ShapeDtypeStruct((rows, width), jnp.bfloat16),
            input_output_aliases={9: 0},
            compiler_params=pltpu.CompilerParams(vmem_limit_bytes=32 << 20),
            cost_estimate=pl.CostEstimate(
                flops=4 * rows * (3 * rows + text_rows) * cols * 4,
                bytes_accessed=8 << 20,
                transcendentals=0,
            ),
            name="video_chunk",
        )(meta, qv, own, m2, p2, sib, fwd, tk, tv, out)

    blocks = n
    stats = jnp.stack([peak, total]).reshape(2, blocks, here, 128)
    acc = acc.reshape(blocks, here, width)
    step = 1
    while step < n:
        blocks //= 2
        bit = (me // step) % 2
        pairs = [(i, i ^ step) for i in range(n)]
        stats4 = stats.reshape(2, blocks, 2, here, 128)
        acc4 = acc.reshape(blocks, 2, here, width)
        pick = lambda x, b, ax: jnp.where(
            b == 0, lax.index_in_dim(x, 0, ax, False), lax.index_in_dim(x, 1, ax, False)
        )
        their_s = lax.ppermute(pick(stats4, 1 - bit, 2), "ctx", pairs)
        their_a = lax.ppermute(pick(acc4, 1 - bit, 1), "ctx", pairs)
        my_s = pick(stats4, bit, 2)
        my_a = pick(acc4, bit, 1)
        joint = jnp.maximum(my_s[0], their_s[0])
        f_my = jnp.exp2((my_s[0] - joint) * C2)
        f_their = jnp.exp2((their_s[0] - joint) * C2)
        stats = jnp.stack([joint, my_s[1] * f_my + their_s[1] * f_their])
        acc = my_a * spread_heads(f_my, heads) + their_a * spread_heads(f_their, heads)
        step *= 2
    text_out = (acc[0] / spread_heads(stats[1, 0], heads)).astype(jnp.bfloat16)
    return (out, text_out)


def plane_kernel(n, *refs):
    listed_hbm, owner_hbm, count_hbm = refs[:3]
    q_hbm, k_hbm, v_hbm, qt_hbm, kt_hbm, vt_hbm, out, text_out = refs[3:11]
    heads = q_hbm.shape[1] // HD
    mine = heads // 4
    kv = refs[11 : 11 + mine]
    (
        qb,
        ob,
        tx,
        part,
        stats,
        flat,
        got,
        got_stats,
        tall,
        tob,
        list_out,
        list_in,
        lists,
        listed,
        owner,
        count,
        in_send,
        kv_recv,
        q_recv,
        tx_send,
        tx_recv,
        chain_send,
        chain_recv,
        halo_send,
        halo_recv,
        o_send,
        o_recv,
        p_send,
        p_recv,
        ps_send,
        ps_recv,
        t_send,
        t_recv,
        l_send,
        l_recv,
        l_in,
        s_in,
    ) = refs[11 + mine :]
    rows = q_hbm.shape[0]
    here = qt_hbm.shape[0]
    block = 4 * here
    nz = n // 4
    wide = mine * HD
    me = lax.axis_index("ctx")
    g = lax.rem(me, 4)
    core = lax.rem(g, 2)
    side = g // 2
    row = me // 4
    base = row * 4
    sib = g + 1 - 2 * core
    pair = g + 2 - 4 * side
    diag = sib + 2 - 4 * side
    mates = [pair, diag, sib]
    above, below = me + 4, me - 4
    has_above, has_below = row < nz - 1, row > 0
    peers = [lax.rem(row + k, nz) for k in range(1, nz)]
    sources = [lax.rem(row + nz - k, nz) for k in range(1, nz)]

    def cols(start, size):
        return pl.ds(pl.multiple_of(start, HD), size)

    def remote(src, dst, send, recv, dev):
        return pltpu.make_async_remote_copy(
            src_ref=src,
            dst_ref=dst,
            send_sem=send,
            recv_sem=recv,
            device_id={"ctx": dev},
            device_id_type=pl.DeviceIdType.MESH,
        )

    def greet(barrier, dev):
        pl.semaphore_signal(
            barrier, inc=1, device_id={"ctx": dev}, device_id_type=pl.DeviceIdType.MESH
        )

    barrier = pltpu.get_barrier_semaphore()
    for mate in mates:
        greet(barrier, base + mate)
    pl.when(has_above)(lambda: greet(barrier, above))
    pl.when(has_below)(lambda: greet(barrier, below))
    scalars = [
        pltpu.make_async_copy(src, dst, s_in.at[i])
        for i, (src, dst) in enumerate(
            ((listed_hbm, listed), (owner_hbm, owner), (count_hbm, count))
        )
    ]
    for copy in scalars:
        copy.start()

    arrays = (k_hbm, v_hbm, q_hbm)
    text_arrays = (qt_hbm, kt_hbm, vt_hbm)

    def spot(j, x, s):
        return qb.at[j, s] if x == 2 else kv[j].at[2 + s, x]

    def source(j, x, s):
        return arrays[x].at[:, cols((s * mine + j) * HD, HD)]

    def arrival(j, x, s):
        return q_recv.at[j] if x == 2 else kv_recv.at[j, x, s]

    def own_in(j, x):
        return pltpu.make_async_copy(source(j, x, g), spot(j, x, g), arrival(j, x, g))

    def send_in(j, x, k):
        return remote(
            source(j, x, mates[k]), spot(j, x, g), in_send.at[x], arrival(j, x, g),
            base + mates[k],
        )

    def wait_on(ref, sem):
        pltpu.make_async_copy(ref, ref, sem).wait()

    def own_text(x):
        return pltpu.make_async_copy(
            text_arrays[x].at[:, cols(g * wide, wide)], tx.at[row, x, g], tx_recv
        )

    def send_text(x, k):
        return remote(
            text_arrays[x].at[:, cols(mates[k] * wide, wide)],
            tx.at[row, x, g],
            tx_send,
            tx_recv,
            base + mates[k],
        )

    def send_list(k):
        return remote(list_out, list_in.at[g], l_send, l_recv, base + mates[k])

    order = [(j, x) for j in range(mine) for x in range(2)] + [(j, 2) for j in range(mine)]
    for x in range(3):
        own_text(x).start()
    for x in range(2):
        own_in(0, x).start()
    beside = has_above.astype(jnp.int32) + has_below.astype(jnp.int32)
    pl.semaphore_wait(barrier, 3 + beside)
    for x in range(3):
        for k in range(2):
            send_text(x, k).start()
    for x in range(2):
        for k in range(3):
            send_in(0, x, k).start()
    for x in range(3):
        send_text(x, 2).start()
    for copy in scalars:
        copy.wait()
    lane = lax.broadcasted_iota(jnp.int32, list_out.shape, 1)
    spots = jnp.zeros(list_out.shape, jnp.int32)
    for i in range(listed.shape[1]):
        spots = jnp.where(lane == i, owner[listed[0, i]], spots)
    list_out[...] = spots
    list_in[g] = spots
    for k in range(3):
        send_list(k).start()
    for j, x in order[2:]:
        for k in range(2):
            send_in(j, x, k).start()
    for j, x in order[2:]:
        own_in(j, x).start()
        send_in(j, x, 2).start()
    limit = count[0]
    place = lax.broadcasted_iota(jnp.int32, (1, n * here), 1)
    bias_all = jnp.where(place < limit, 0.0, -jnp.inf).astype(jnp.float32)
    place = row * block + lax.broadcasted_iota(jnp.int32, (1, block), 1)
    bias_own = jnp.where(place < limit, 0.0, -jnp.inf).astype(jnp.float32)

    def chain(z, up):
        return remote(
            tx.at[z], tx.at[z], chain_send.at[0 if up else 1, z], chain_recv.at[z],
            above if up else below,
        )

    def chain_wait(z):
        pltpu.make_async_copy(tx.at[z], tx.at[z], chain_recv.at[z]).wait()

    def chain_step(d):
        up_from, down_from = row - d, row + d
        if d > 0:
            pl.when(up_from >= 0)(lambda: chain_wait(up_from))
        pl.when(jnp.logical_and(up_from >= 0, has_above))(lambda: chain(up_from, True).start())
        if d > 0:
            pl.when(down_from < nz)(lambda: chain_wait(down_from))
        pl.when(jnp.logical_and(down_from < nz, has_below))(
            lambda: chain(down_from, False).start()
        )

    def chain_drain(d):
        up_from, down_from = row - d, row + d
        pl.when(jnp.logical_and(up_from >= 0, has_above))(
            lambda: chain(up_from, True).wait_send()
        )
        pl.when(jnp.logical_and(down_from < nz, has_below))(
            lambda: chain(down_from, False).wait_send()
        )

    def halo_first(far):
        return 2 * (1 - side) if far else 2 * side

    def halo_goes(far):
        up = side == 0 if far else side == 1
        return jnp.logical_or(
            jnp.logical_and(up, has_above), jnp.logical_and(jnp.logical_not(up), has_below)
        )

    def halo(j, far, x, i):
        s = halo_first(far) + i
        return remote(
            kv[j].at[2 + s, x],
            kv[j].at[lax.rem(s + 6, 8), x],
            halo_send.at[j, int(far)],
            halo_recv.at[j, 1 - side if far else side],
            me + 4 - 8 * side if far else me - 4 + 8 * side,
        )

    def halo_start(j, far, arrays=(0, 1)):
        for x in arrays:
            for i in range(2):
                s = halo_first(far) + i
                wait_on(kv[j].at[2 + s, x], kv_recv.at[j, x, s])
                pl.when(halo_goes(far))(lambda x=x, i=i: halo(j, far, x, i).start())

    def halo_wait(j):
        pl.when(has_above)(lambda: wait_on(kv[j].at[6:8], halo_recv.at[j, 0]))
        pl.when(has_below)(lambda: wait_on(kv[j].at[0:2], halo_recv.at[j, 1]))

    def halo_drain(j):
        for far in (True, False):
            pl.when(halo_goes(far))(lambda: wait_on(kv[j].at[2:4], halo_send.at[j, int(far)]))

    def text_words(x, j):
        return tx[:, x, :, :, j * HD : (j + 1) * HD].reshape(n * here, HD)

    def text_head(j):
        q = text_words(0, j)
        keys = [kv[j][2 + s, 0] for s in range(4)]
        values = [kv[j][2 + s, 1] for s in range(4)]
        own = [tx[row, x, :, :, j * HD : (j + 1) * HD].reshape(block, HD) for x in (1, 2)]
        scores = [qk(q, key) for key in keys] + [qk(q, own[0]) + bias_own]
        peak, total, acc = softmax_parts(scores, values + [own[1]])
        part[j] = acc.reshape(nz, block, HD)
        lane = lax.broadcasted_iota(jnp.int32, stats.shape, 1)
        old = stats[...] if j else jnp.ones(stats.shape, jnp.float32)
        stats[...] = jnp.where(lane == j, peak, jnp.where(lane == mine + j, total, old))
        if j == mine - 1:
            flat[...] = jnp.transpose(stats[...])[:8, :]

    def part_z(j, k):
        return remote(
            part.at[j, peers[k]], got.at[k, j], p_send, p_recv, peers[k] * 4 + g
        )

    def stats_z(k):
        return remote(flat, got_stats.at[k], ps_send, ps_recv, peers[k] * 4 + g)

    def out_spot(j, s):
        return out.at[:, cols((s * mine + j) * HD, HD)]

    def send_out(j, s):
        return remote(ob.at[j, s], out_spot(j, g), o_send, o_recv, base + s)

    def keep_out(j, s):
        return pltpu.make_async_copy(ob.at[j, s], out_spot(j, g), o_recv)

    def video_tile(j, s):
        at = [jnp.clip(lists[s, 0, i] - (base - 2), 0, 7) for i in range(listed.shape[1])]
        keys = [kv[j][i, 0] for i in at] + [text_words(1, j)]
        values = [kv[j][i, 1] for i in at] + [text_words(2, j)]
        step = rows
        for r in range(rows // step):
            qr = qb[j, s, r * step : (r + 1) * step, :]
            scores = [qk(qr, key) for key in keys]
            scores[-1] = scores[-1] + bias_all
            _, total, acc = softmax_parts(scores, values)
            ob[j, s, r * step : (r + 1) * step, :] = (acc / total).astype(jnp.bfloat16)
        pl.when(s == g)(lambda: keep_out(j, s).start())
        pl.when(s != g)(lambda: send_out(j, s).start())

    def video_tiles(j, lo, hi):
        def one(i, _):
            video_tile(j, lax.rem(i + 2 * (1 - side), 4))
            return 0

        lax.fori_loop(lo, hi, one, 0)

    def text_final():
        wait_on(got, p_recv)
        wait_on(got_stats, ps_recv)
        rows_here = pl.ds(pl.multiple_of(row * block, block), block)
        known = [stats[rows_here, :]]
        for k in range(nz - 1):
            full = jnp.concatenate([got_stats[k]] + [jnp.zeros_like(got_stats[k])] * 15, axis=0)
            tall[k] = jnp.transpose(full)
            known.append(tall[k, rows_here, :])
        for j in range(mine):
            peaks = [x[:, j : j + 1] for x in known]
            totals = [x[:, mine + j : mine + j + 1] for x in known]
            accs = [part[j, row]] + [got[k, j] for k in range(nz - 1)]
            joint = functools.reduce(jnp.maximum, peaks)
            weights = [jnp.exp2((p - joint) * C2) for p in peaks]
            total = sum(t * w for t, w in zip(totals, weights))
            acc = sum(a * w for a, w in zip(accs, weights))
            tob[:, :, j * HD : (j + 1) * HD] = (
                (acc / total).astype(jnp.bfloat16).reshape(4, here, HD)
            )

    def text_spot(s):
        return text_out.at[:, cols(s * wide, wide)]

    def send_words(k):
        s = mates[k]
        return remote(tob.at[s], text_spot(g), t_send, t_recv, base + s)

    def keep_words():
        return pltpu.make_async_copy(tob.at[g], text_spot(g), t_recv)

    halo_start(0, False, (0,))
    wait_on(tx.at[row], tx_recv)
    chain_step(0)
    halo_start(0, False, (1,))
    halo_start(0, True)
    for d in range(1, nz - 1):
        chain_step(d)
        if d < mine:
            halo_start(d, False)
    for j in range(max(1, nz - 1), mine):
        halo_start(j, False)

    def text_part(j):
        text_head(j)
        for k in range(nz - 1):
            part_z(j, k).start()
        if j == mine - 1:
            for k in range(nz - 1):
                stats_z(k).start()

    def video_wait(j):
        wait_on(qb.at[j], q_recv.at[j])
        halo_wait(j)

    halo_start(1, True)
    pl.when(row - (nz - 1) >= 0)(lambda: chain_wait(row - (nz - 1)))
    pl.when(row + nz - 1 < nz)(lambda: chain_wait(row + nz - 1))
    text_part(0)
    wait_on(list_in.at[0:3], l_recv)
    lists_in = pltpu.make_async_copy(list_in, lists, l_in)
    lists_in.start()
    lists_in.wait()
    halo_start(2, True)
    text_part(1)
    text_part(2)
    for j in range(mine):
        video_wait(j)
        if j < mine - 1:
            video_tiles(j, 0, 4)
        else:
            video_tiles(j, 0, 2)
            text_final()
            for k in range(3):
                send_words(k).start()
            keep_words().start()
            video_tiles(j, 2, 4)

    wait_on(out, o_recv)
    wait_on(text_out, t_recv)
    for x in range(3):
        wait_on(arrays[x].at[:, : 3 * wide], in_send.at[x])
    wait_on(q_hbm.at[:, : 3 * wide], o_send)
    wait_on(tx.at[0, :, 0:3], tx_send)
    wait_on(list_in.at[0:3], l_send)
    wait_on(tob.at[0:3], t_send)
    wait_on(got, p_send)
    wait_on(got_stats, ps_send)
    for j in range(mine):
        halo_drain(j)
    for d in range(nz - 1):
        chain_drain(d)


def deliver(pieces, video, text, video_out, text_out, sems):
    rows = video.shape[0] // pieces
    copies = [
        pltpu.make_async_copy(
            video.at[i * rows : (i + 1) * rows], video_out.at[i * rows : (i + 1) * rows], sems.at[i]
        )
        for i in range(pieces)
    ]
    copies.append(pltpu.make_async_copy(text, text_out, sems.at[pieces]))
    for copy in copies:
        copy.start()
    for copy in copies:
        copy.wait()


def deliver(pieces, video, text, video_out, text_out, sems):
    rows = video.shape[0] // pieces
    copies = [
        pltpu.make_async_copy(
            video.at[i * rows : (i + 1) * rows], video_out.at[i * rows : (i + 1) * rows], sems.at[i]
        )
        for i in range(pieces)
    ]
    copies.append(pltpu.make_async_copy(text, text_out, sems.at[pieces]))
    for copy in copies:
        copy.start()
    for copy in copies:
        copy.wait()


def fused(qv, kv, vv, qt, kt, vt, key_tiles, tile_owner, text_count):
    n = lax.axis_size("ctx")
    rows, width = qv.shape
    mine = width // HD // 4
    here = qt.shape[0]
    nz = n // 4
    dma = pltpu.SemaphoreType.DMA
    shapes = [
        jax.ShapeDtypeStruct((rows, width), jnp.bfloat16),
        jax.ShapeDtypeStruct((here, width), jnp.bfloat16),
    ]
    anywhere = pl.BlockSpec(memory_space=pl.ANY)
    results = pl.pallas_call(
        functools.partial(plane_kernel, n),
        in_specs=[pl.BlockSpec(memory_space=pltpu.HBM)] * 9,
        out_specs=[pl.BlockSpec(memory_space=pltpu.VMEM)] * 2,
        out_shape=[pltpu.VMEM(x.shape, x.dtype) for x in shapes],
        scratch_shapes=[pltpu.VMEM((8, 2, rows, HD), jnp.bfloat16)] * mine
        + [
            pltpu.VMEM((mine, 4, rows, HD), jnp.bfloat16),
            pltpu.VMEM((mine, 4, rows, HD), jnp.bfloat16),
            pltpu.VMEM((nz, 3, 4, here, mine * HD), jnp.bfloat16),
            pltpu.VMEM((mine, nz, 4 * here, HD), jnp.float32),
            pltpu.VMEM((n * here, 128), jnp.float32),
            pltpu.VMEM((8, n * here), jnp.float32),
            pltpu.VMEM((nz - 1, mine, 4 * here, HD), jnp.float32),
            pltpu.VMEM((nz - 1, 8, n * here), jnp.float32),
            pltpu.VMEM((nz - 1, n * here, 128), jnp.float32),
            pltpu.VMEM((4, here, mine * HD), jnp.bfloat16),
            pltpu.VMEM((8, 128), jnp.int32),
            pltpu.VMEM((4, 8, 128), jnp.int32),
            pltpu.SMEM((4, 8, 128), jnp.int32),
            pltpu.SMEM(key_tiles.shape, jnp.int32),
            pltpu.SMEM(tile_owner.shape, jnp.int32),
            pltpu.SMEM(text_count.shape, jnp.int32),
        ]
        + [dma((3,)), dma((mine, 2, 4)), dma((mine,)), dma, dma]
        + [dma((2, nz)), dma((nz,)), dma((mine, 2)), dma((mine, 2))]
        + [dma] * 11
        + [dma((3,))],
        compiler_params=pltpu.CompilerParams(
            collective_id=0, has_side_effects=True, vmem_limit_bytes=125 << 19
        ),
        name="tile_attention",
    )(key_tiles, tile_owner, text_count, qv, kv, vv, qt, kt, vt)
    results = [pltpu.with_memory_space_constraint(x, pltpu.VMEM) for x in results]
    pieces = 4
    return pl.pallas_call(
        functools.partial(deliver, pieces),
        in_specs=[pl.BlockSpec(memory_space=pltpu.VMEM)] * 2,
        out_specs=[pl.BlockSpec(memory_space=pltpu.HBM)] * 2,
        out_shape=shapes,
        scratch_shapes=[dma((pieces + 1,))],
        name="deliver",
    )(*results)


def whole_device(*args):
    n = lax.axis_size("ctx")
    rows, width = args[0].shape
    here = args[3].shape[0]
    if rows == TILE and n % 4 == 0 and n >= 8 and n & (n - 1) == 0 and here in (16, 32, 64) and width // HD == 12:
        return fused(*args)
    return on_device(*args)


def solution(mesh):
    split = P(("groups", "ctx"), None)
    return jax.shard_map(
        whole_device,
        mesh=mesh,
        in_specs=(split,) * 7 + (P("groups"), P("groups")),
        out_specs=(split, split),
        check_vma=False,
    )
```

```python
import functools
import math

import jax
import jax.numpy as jnp
from jax import lax
from jax.experimental import pallas as pl
from jax.experimental.pallas import tpu as pltpu
from jax.sharding import PartitionSpec as P

TILE = 384
HD = 128
REACH = 2
CHUNK = 3
C2 = math.log2(math.e) / math.sqrt(HD)


def qk(q, k):
    return lax.dot_general(q, k, (((1,), (1,)), ((), ())), preferred_element_type=jnp.float32)


def pv(p, v):
    return lax.dot_general(
        p.astype(jnp.bfloat16), v, (((1,), (0,)), ((), ())), preferred_element_type=jnp.float32
    )


def softmax_parts(scores, values):
    peak = functools.reduce(jnp.maximum, [jnp.max(s, axis=-1, keepdims=True) for s in scores])
    total, acc = None, None
    for s, v in zip(scores, values):
        w = jnp.exp2((s - peak) * C2)
        t = jnp.sum(w, axis=-1, keepdims=True)
        a = pv(w, v)
        total = t if total is None else total + t
        acc = a if acc is None else acc + a
    return peak, total, acc


def video_kernel(meta, q, own, m2, p2, sib, fwd, tk, tv, prev, out):
    lo_p2 = meta[0] == 2
    hi_sib = meta[1] == 3
    hi_fwd = meta[1] == 4
    tiles = []
    for j in range(2):
        far_m, far_p = m2[j], p2[j]
        lo = jnp.where(lo_p2, far_p, far_m)
        hi = jnp.where(hi_fwd, fwd[j], jnp.where(hi_sib, sib[j], far_p))
        tiles.append((own[j], lo, hi))
    key_words = tk[...]
    value_words = tv[...]
    ok = lax.broadcasted_iota(jnp.int32, (1, key_words.shape[0]), 1) < meta[2]
    rows = 128
    for r in range(q.shape[0] // rows):
        qr = q[pl.ds(r * rows, rows), :]
        scores = [qk(qr, k) for k in tiles[0]]
        scores.append(jnp.where(ok, qk(qr, key_words), -jnp.inf))
        _, total, acc = softmax_parts(scores, list(tiles[1]) + [value_words])
        out[pl.ds(r * rows, rows), :] = (acc / total).astype(jnp.bfloat16)


def text_kernel(meta, q, k, v, kt, vt, peak_out, total_out, acc_out):
    h = pl.program_id(0)
    own = kt.shape[0]
    ok = lax.broadcasted_iota(jnp.int32, (1, own), 1) < meta[3]
    scores = [qk(q[...], k[...]), jnp.where(ok, qk(q[...], kt[...]), -jnp.inf)]
    peak, total, acc = softmax_parts(scores, [v[...], vt[...]])
    lane = lax.broadcasted_iota(jnp.int32, peak_out.shape, 1) == h
    peak_out[...] = jnp.where(lane, peak, jnp.where(h == 0, 0.0, peak_out[...]))
    total_out[...] = jnp.where(lane, total, jnp.where(h == 0, 1.0, total_out[...]))
    acc_out[...] = acc


def spread_heads(values, heads):
    return jnp.repeat(values[..., :heads], HD, axis=-1)


def on_device(qv, kv, vv, qt, kt, vt, key_tiles, tile_owner, text_count):
    n = lax.axis_size("ctx")
    me = lax.axis_index("ctx")
    rows, width = qv.shape
    heads = width // HD
    here = qt.shape[0]
    even = me % 2 == 0
    cols = CHUNK * HD
    chunks = heads // CHUNK

    text = lax.all_gather(jnp.stack([qt, kt, vt]), "ctx", axis=1, tiled=True)
    tq, tk, tv = text[0], text[1], text[2]

    tiles = tile_owner.shape[0]
    match = key_tiles[0][:, None] == jnp.arange(tiles, dtype=jnp.int32)[None, :]
    slots = jnp.sum(jnp.where(match, tile_owner[None, :], 0), axis=-1)
    off = slots - me
    near = jnp.where(even == (off == 1), 3, 4)
    code = jnp.where(off == 0, 0, jnp.where(off == -2, 1, jnp.where(off == 2, 2, near)))
    hi = jnp.max(code)
    lo = jnp.sum(code) - hi
    meta = jnp.stack([lo, hi, text_count[0], text_count[0] - me * here]).astype(jnp.int32)

    up = [(i, i - 2) for i in range(2, n)]
    down = [(i, i + 2) for i in range(n - 2)]
    swap = [(i, i ^ 1) for i in range(n)]
    fetched = []
    for c in range(chunks):
        sl = slice(c * cols, (c + 1) * cols)
        own = jnp.stack([kv[:, sl], vv[:, sl]])
        p2 = lax.ppermute(own, "ctx", up)
        m2 = lax.ppermute(own, "ctx", down)
        sib = lax.ppermute(own, "ctx", swap)
        fwd = lax.ppermute(jnp.where(even, p2, m2), "ctx", swap)
        fetched.append((own, m2, p2, sib, fwd))

    col = lambda h: (0, h)
    text_rows = tq.shape[0]
    smem = pl.BlockSpec(memory_space=pltpu.SMEM)
    peak, total, acc = pl.pallas_call(
        text_kernel,
        grid=(heads,),
        in_specs=[
            smem,
            pl.BlockSpec((text_rows, HD), col),
            pl.BlockSpec((rows, HD), col),
            pl.BlockSpec((rows, HD), col),
            pl.BlockSpec((here, HD), col),
            pl.BlockSpec((here, HD), col),
        ],
        out_specs=[
            pl.BlockSpec((text_rows, 128), lambda h: (0, 0)),
            pl.BlockSpec((text_rows, 128), lambda h: (0, 0)),
            pl.BlockSpec((text_rows, HD), col),
        ],
        out_shape=[
            jax.ShapeDtypeStruct((text_rows, 128), jnp.float32),
            jax.ShapeDtypeStruct((text_rows, 128), jnp.float32),
            jax.ShapeDtypeStruct((text_rows, width), jnp.float32),
        ],
        cost_estimate=pl.CostEstimate(
            flops=4 * text_rows * rows * width * 4, bytes_accessed=6 << 20, transcendentals=0
        ),
        name="text_partials",
    )(meta, tq, kv, vv, kt, vt)

    out = jnp.zeros((rows, width), jnp.bfloat16)
    for c in range(chunks):
        own, m2, p2, sib, fwd = fetched[c]
        tile_spec = pl.BlockSpec((2, rows, HD), lambda h: (0, 0, h))
        wide = lambda h, c=c: (0, h + c * CHUNK)
        out = pl.pallas_call(
            video_kernel,
            grid=(CHUNK,),
            in_specs=[smem, pl.BlockSpec((rows, HD), wide)]
            + [tile_spec] * 5
            + [pl.BlockSpec((text_rows, HD), wide)] * 2
            + [pl.BlockSpec(memory_space=pl.ANY)],
            out_specs=pl.BlockSpec((rows, HD), wide),
            out_shape=jax.ShapeDtypeStruct((rows, width), jnp.bfloat16),
            input_output_aliases={9: 0},
            compiler_params=pltpu.CompilerParams(vmem_limit_bytes=32 << 20),
            cost_estimate=pl.CostEstimate(
                flops=4 * rows * (3 * rows + text_rows) * cols * 4,
                bytes_accessed=8 << 20,
                transcendentals=0,
            ),
            name="video_chunk",
        )(meta, qv, own, m2, p2, sib, fwd, tk, tv, out)

    blocks = n
    stats = jnp.stack([peak, total]).reshape(2, blocks, here, 128)
    acc = acc.reshape(blocks, here, width)
    step = 1
    while step < n:
        blocks //= 2
        bit = (me // step) % 2
        pairs = [(i, i ^ step) for i in range(n)]
        stats4 = stats.reshape(2, blocks, 2, here, 128)
        acc4 = acc.reshape(blocks, 2, here, width)
        pick = lambda x, b, ax: jnp.where(
            b == 0, lax.index_in_dim(x, 0, ax, False), lax.index_in_dim(x, 1, ax, False)
        )
        their_s = lax.ppermute(pick(stats4, 1 - bit, 2), "ctx", pairs)
        their_a = lax.ppermute(pick(acc4, 1 - bit, 1), "ctx", pairs)
        my_s = pick(stats4, bit, 2)
        my_a = pick(acc4, bit, 1)
        joint = jnp.maximum(my_s[0], their_s[0])
        f_my = jnp.exp2((my_s[0] - joint) * C2)
        f_their = jnp.exp2((their_s[0] - joint) * C2)
        stats = jnp.stack([joint, my_s[1] * f_my + their_s[1] * f_their])
        acc = my_a * spread_heads(f_my, heads) + their_a * spread_heads(f_their, heads)
        step *= 2
    text_out = (acc[0] / spread_heads(stats[1, 0], heads)).astype(jnp.bfloat16)
    return (out, text_out)


def plane_kernel(n, *refs):
    listed_hbm, owner_hbm, count_hbm = refs[:3]
    q_hbm, k_hbm, v_hbm, qt_hbm, kt_hbm, vt_hbm, out, text_out = refs[3:11]
    heads = q_hbm.shape[1] // HD
    mine = heads // 4
    kv = refs[11 : 11 + mine]
    (
        qb,
        ob,
        tx,
        part,
        stats,
        flat,
        got,
        got_stats,
        tall,
        tob,
        list_out,
        list_in,
        lists,
        listed,
        owner,
        count,
        in_send,
        kv_recv,
        q_recv,
        tx_send,
        tx_recv,
        chain_send,
        chain_recv,
        halo_send,
        halo_recv,
        o_send,
        o_recv,
        p_send,
        p_recv,
        ps_send,
        ps_recv,
        t_send,
        t_recv,
        l_send,
        l_recv,
        l_in,
        s_in,
        words,
        words_in,
    ) = refs[11 + mine :]
    rows = q_hbm.shape[0]
    here = qt_hbm.shape[0]
    block = 4 * here
    nz = n // 4
    wide = mine * HD
    me = lax.axis_index("ctx")
    g = lax.rem(me, 4)
    core = lax.rem(g, 2)
    side = g // 2
    row = me // 4
    base = row * 4
    sib = g + 1 - 2 * core
    pair = g + 2 - 4 * side
    diag = sib + 2 - 4 * side
    mates = [pair, diag, sib]
    above, below = me + 4, me - 4
    has_above, has_below = row < nz - 1, row > 0
    peers = [lax.rem(row + k, nz) for k in range(1, nz)]
    sources = [lax.rem(row + nz - k, nz) for k in range(1, nz)]

    def cols(start, size):
        return pl.ds(pl.multiple_of(start, HD), size)

    def remote(src, dst, send, recv, dev):
        return pltpu.make_async_remote_copy(
            src_ref=src,
            dst_ref=dst,
            send_sem=send,
            recv_sem=recv,
            device_id={"ctx": dev},
            device_id_type=pl.DeviceIdType.MESH,
        )

    def greet(barrier, dev):
        pl.semaphore_signal(
            barrier, inc=1, device_id={"ctx": dev}, device_id_type=pl.DeviceIdType.MESH
        )

    barrier = pltpu.get_barrier_semaphore()
    for mate in mates:
        greet(barrier, base + mate)
    pl.when(has_above)(lambda: greet(barrier, above))
    pl.when(has_below)(lambda: greet(barrier, below))
    scalars = [
        pltpu.make_async_copy(src, dst, s_in.at[i])
        for i, (src, dst) in enumerate(
            ((listed_hbm, listed), (owner_hbm, owner), (count_hbm, count))
        )
    ]
    for copy in scalars:
        copy.start()

    arrays = (k_hbm, v_hbm, q_hbm)
    text_arrays = tuple(words.at[x] for x in range(3))
    text_in = [
        pltpu.make_async_copy(ref, words.at[x], words_in.at[x])
        for x, ref in enumerate((qt_hbm, kt_hbm, vt_hbm))
    ]
    for copy in text_in:
        copy.start()

    def spot(j, x, s):
        return qb.at[j, s] if x == 2 else kv[j].at[2 + s, x]

    def source(j, x, s):
        return arrays[x].at[:, cols((s * mine + j) * HD, HD)]

    def arrival(j, x, s):
        return q_recv.at[j] if x == 2 else kv_recv.at[j, x, s]

    def own_in(j, x):
        return pltpu.make_async_copy(source(j, x, g), spot(j, x, g), arrival(j, x, g))

    def send_in(j, x, k):
        return remote(
            source(j, x, mates[k]), spot(j, x, g), in_send.at[x], arrival(j, x, g),
            base + mates[k],
        )

    def wait_on(ref, sem):
        pltpu.make_async_copy(ref, ref, sem).wait()

    def own_text(x):
        return pltpu.make_async_copy(
            text_arrays[x].at[:, cols(g * wide, wide)], tx.at[row, x, g], tx_recv
        )

    def send_text(x, k):
        return remote(
            text_arrays[x].at[:, cols(mates[k] * wide, wide)],
            tx.at[row, x, g],
            tx_send,
            tx_recv,
            base + mates[k],
        )

    def send_list(k):
        return remote(list_out, list_in.at[g], l_send, l_recv, base + mates[k])

    order = [(j, x) for j in range(mine) for x in range(2)] + [(j, 2) for j in range(mine)]
    for x in range(2):
        own_in(0, x).start()
    for copy in text_in:
        copy.wait()
    beside = has_above.astype(jnp.int32) + has_below.astype(jnp.int32)
    pl.semaphore_wait(barrier, 3 + beside)
    for x in range(3):
        for k in range(2):
            send_text(x, k).start()
    for x in range(2):
        for k in range(3):
            send_in(0, x, k).start()
    for x in range(3):
        own_text(x).start()
        send_text(x, 2).start()
    for copy in scalars:
        copy.wait()
    lane = lax.broadcasted_iota(jnp.int32, list_out.shape, 1)
    spots = jnp.zeros(list_out.shape, jnp.int32)
    for i in range(listed.shape[1]):
        spots = jnp.where(lane == i, owner[listed[0, i]], spots)
    list_out[...] = spots
    list_in[g] = spots
    for k in range(3):
        send_list(k).start()
    for j, x in order[2:]:
        for k in range(2):
            send_in(j, x, k).start()
    for j, x in order[2:]:
        own_in(j, x).start()
        send_in(j, x, 2).start()
    limit = count[0]
    place = lax.broadcasted_iota(jnp.int32, (1, n * here), 1)
    bias_all = jnp.where(place < limit, 0.0, -jnp.inf).astype(jnp.float32)
    place = row * block + lax.broadcasted_iota(jnp.int32, (1, block), 1)
    bias_own = jnp.where(place < limit, 0.0, -jnp.inf).astype(jnp.float32)

    def chain(z, up):
        return remote(
            tx.at[z], tx.at[z], chain_send.at[0 if up else 1, z], chain_recv.at[z],
            above if up else below,
        )

    def chain_wait(z):
        pltpu.make_async_copy(tx.at[z], tx.at[z], chain_recv.at[z]).wait()

    def chain_step(d):
        up_from, down_from = row - d, row + d
        if d > 0:
            pl.when(up_from >= 0)(lambda: chain_wait(up_from))
        pl.when(jnp.logical_and(up_from >= 0, has_above))(lambda: chain(up_from, True).start())
        if d > 0:
            pl.when(down_from < nz)(lambda: chain_wait(down_from))
        pl.when(jnp.logical_and(down_from < nz, has_below))(
            lambda: chain(down_from, False).start()
        )

    def chain_drain(d):
        up_from, down_from = row - d, row + d
        pl.when(jnp.logical_and(up_from >= 0, has_above))(
            lambda: chain(up_from, True).wait_send()
        )
        pl.when(jnp.logical_and(down_from < nz, has_below))(
            lambda: chain(down_from, False).wait_send()
        )

    def halo_first(far):
        return 2 * (1 - side) if far else 2 * side

    def halo_goes(far):
        up = side == 0 if far else side == 1
        return jnp.logical_or(
            jnp.logical_and(up, has_above), jnp.logical_and(jnp.logical_not(up), has_below)
        )

    def halo(j, far, x, i):
        s = halo_first(far) + i
        return remote(
            kv[j].at[2 + s, x],
            kv[j].at[lax.rem(s + 6, 8), x],
            halo_send.at[j, int(far)],
            halo_recv.at[j, 1 - side if far else side],
            me + 4 - 8 * side if far else me - 4 + 8 * side,
        )

    def halo_start(j, far, arrays=(0, 1)):
        for x in arrays:
            for i in range(2):
                s = halo_first(far) + i
                wait_on(kv[j].at[2 + s, x], kv_recv.at[j, x, s])
                pl.when(halo_goes(far))(lambda x=x, i=i: halo(j, far, x, i).start())

    def halo_wait(j):
        pl.when(has_above)(lambda: wait_on(kv[j].at[6:8], halo_recv.at[j, 0]))
        pl.when(has_below)(lambda: wait_on(kv[j].at[0:2], halo_recv.at[j, 1]))

    def halo_drain(j):
        for far in (True, False):
            pl.when(halo_goes(far))(lambda: wait_on(kv[j].at[2:4], halo_send.at[j, int(far)]))

    def text_words(x, j):
        return tx[:, x, :, :, j * HD : (j + 1) * HD].reshape(n * here, HD)

    def text_head(j):
        q = text_words(0, j)
        keys = [kv[j][2 + s, 0] for s in range(4)]
        values = [kv[j][2 + s, 1] for s in range(4)]
        own = [tx[row, x, :, :, j * HD : (j + 1) * HD].reshape(block, HD) for x in (1, 2)]
        scores = [qk(q, key) for key in keys] + [qk(q, own[0]) + bias_own]
        peak, total, acc = softmax_parts(scores, values + [own[1]])
        part[j] = acc.reshape(nz, block, HD)
        lane = lax.broadcasted_iota(jnp.int32, stats.shape, 1)
        old = stats[...] if j else jnp.ones(stats.shape, jnp.float32)
        stats[...] = jnp.where(lane == j, peak, jnp.where(lane == mine + j, total, old))
        if j == mine - 1:
            flat[...] = jnp.transpose(stats[...])[:8, :]

    def part_z(j, k):
        return remote(
            part.at[j, peers[k]], got.at[k, j], p_send, p_recv, peers[k] * 4 + g
        )

    def stats_z(k):
        return remote(flat, got_stats.at[k], ps_send, ps_recv, peers[k] * 4 + g)

    def out_spot(j, s):
        return out.at[:, cols((s * mine + j) * HD, HD)]

    def send_out(j, s):
        return remote(ob.at[j, s], out_spot(j, g), o_send, o_recv, base + s)

    def keep_out(j, s):
        return pltpu.make_async_copy(ob.at[j, s], out_spot(j, g), o_recv)

    def video_tile(j, s):
        at = [jnp.clip(lists[s, 0, i] - (base - 2), 0, 7) for i in range(listed.shape[1])]
        keys = [kv[j][i, 0] for i in at] + [text_words(1, j)]
        values = [kv[j][i, 1] for i in at] + [text_words(2, j)]
        step = rows
        for r in range(rows // step):
            qr = qb[j, s, r * step : (r + 1) * step, :]
            scores = [qk(qr, key) for key in keys]
            scores[-1] = scores[-1] + bias_all
            _, total, acc = softmax_parts(scores, values)
            ob[j, s, r * step : (r + 1) * step, :] = (acc / total).astype(jnp.bfloat16)
        pl.when(s == g)(lambda: keep_out(j, s).start())
        pl.when(s != g)(lambda: send_out(j, s).start())

    def video_tiles(j, lo, hi):
        def one(i, _):
            video_tile(j, lax.rem(i + 2 * (1 - side), 4))
            return 0

        lax.fori_loop(lo, hi, one, 0)

    def text_final():
        wait_on(got, p_recv)
        wait_on(got_stats, ps_recv)
        rows_here = pl.ds(pl.multiple_of(row * block, block), block)
        known = [stats[rows_here, :]]
        for k in range(nz - 1):
            full = jnp.concatenate([got_stats[k]] + [jnp.zeros_like(got_stats[k])] * 15, axis=0)
            tall[k] = jnp.transpose(full)
            known.append(tall[k, rows_here, :])
        for j in range(mine):
            peaks = [x[:, j : j + 1] for x in known]
            totals = [x[:, mine + j : mine + j + 1] for x in known]
            accs = [part[j, row]] + [got[k, j] for k in range(nz - 1)]
            joint = functools.reduce(jnp.maximum, peaks)
            weights = [jnp.exp2((p - joint) * C2) for p in peaks]
            total = sum(t * w for t, w in zip(totals, weights))
            acc = sum(a * w for a, w in zip(accs, weights))
            tob[:, :, j * HD : (j + 1) * HD] = (
                (acc / total).astype(jnp.bfloat16).reshape(4, here, HD)
            )

    def text_spot(s):
        return text_out.at[:, cols(s * wide, wide)]

    def send_words(k):
        s = mates[k]
        return remote(tob.at[s], text_spot(g), t_send, t_recv, base + s)

    def keep_words():
        return pltpu.make_async_copy(tob.at[g], text_spot(g), t_recv)

    halo_start(0, False, (0,))
    wait_on(tx.at[row], tx_recv)
    chain_step(0)
    halo_start(0, False, (1,))
    halo_start(0, True)
    for d in range(1, nz - 1):
        chain_step(d)
        if d < mine:
            halo_start(d, False)
    for j in range(max(1, nz - 1), mine):
        halo_start(j, False)

    def text_part(j):
        text_head(j)
        for k in range(nz - 1):
            part_z(j, k).start()
        if j == mine - 1:
            for k in range(nz - 1):
                stats_z(k).start()

    def video_wait(j):
        wait_on(qb.at[j], q_recv.at[j])
        halo_wait(j)

    halo_start(1, True)
    pl.when(row - (nz - 1) >= 0)(lambda: chain_wait(row - (nz - 1)))
    pl.when(row + nz - 1 < nz)(lambda: chain_wait(row + nz - 1))
    text_part(0)
    wait_on(list_in.at[0:3], l_recv)
    lists_in = pltpu.make_async_copy(list_in, lists, l_in)
    lists_in.start()
    lists_in.wait()
    halo_start(2, True)
    text_part(1)
    text_part(2)
    for j in range(mine):
        video_wait(j)
        if j < mine - 1:
            video_tiles(j, 0, 4)
        else:
            video_tiles(j, 0, 2)
            text_final()
            for k in range(3):
                send_words(k).start()
            keep_words().start()
            video_tiles(j, 2, 4)

    for x in range(3):
        wait_on(arrays[x].at[:, : 3 * wide], in_send.at[x])
    wait_on(tx.at[0, :, 0:3], tx_send)
    wait_on(list_in.at[0:3], l_send)
    for j in range(mine):
        halo_drain(j)
    for d in range(nz - 1):
        chain_drain(d)
    wait_on(got, p_send)
    wait_on(got_stats, ps_send)
    wait_on(tob.at[0:3], t_send)
    wait_on(text_out, t_recv)
    wait_on(q_hbm.at[:, : 3 * wide], o_send)
    wait_on(out, o_recv)


def deliver(pieces, video, text, video_out, text_out, sems):
    rows = video.shape[0] // pieces
    copies = [
        pltpu.make_async_copy(
            video.at[i * rows : (i + 1) * rows], video_out.at[i * rows : (i + 1) * rows], sems.at[i]
        )
        for i in range(pieces)
    ]
    copies.append(pltpu.make_async_copy(text, text_out, sems.at[pieces]))
    for copy in copies:
        copy.start()
    for copy in copies:
        copy.wait()


def deliver(pieces, video, text, video_out, text_out, sems):
    rows = video.shape[0] // pieces
    copies = [
        pltpu.make_async_copy(
            video.at[i * rows : (i + 1) * rows], video_out.at[i * rows : (i + 1) * rows], sems.at[i]
        )
        for i in range(pieces)
    ]
    copies.append(pltpu.make_async_copy(text, text_out, sems.at[pieces]))
    for copy in copies:
        copy.start()
    for copy in copies:
        copy.wait()


def fused(qv, kv, vv, qt, kt, vt, key_tiles, tile_owner, text_count):
    n = lax.axis_size("ctx")
    rows, width = qv.shape
    mine = width // HD // 4
    here = qt.shape[0]
    nz = n // 4
    dma = pltpu.SemaphoreType.DMA
    shapes = [
        jax.ShapeDtypeStruct((rows, width), jnp.bfloat16),
        jax.ShapeDtypeStruct((here, width), jnp.bfloat16),
    ]
    anywhere = pl.BlockSpec(memory_space=pl.ANY)
    results = pl.pallas_call(
        functools.partial(plane_kernel, n),
        in_specs=[pl.BlockSpec(memory_space=pltpu.HBM)] * 9,
        out_specs=[pl.BlockSpec(memory_space=pltpu.VMEM)] * 2,
        out_shape=[pltpu.VMEM(x.shape, x.dtype) for x in shapes],
        scratch_shapes=[pltpu.VMEM((8, 2, rows, HD), jnp.bfloat16)] * mine
        + [
            pltpu.VMEM((mine, 4, rows, HD), jnp.bfloat16),
            pltpu.VMEM((mine, 4, rows, HD), jnp.bfloat16),
            pltpu.VMEM((nz, 3, 4, here, mine * HD), jnp.bfloat16),
            pltpu.VMEM((mine, nz, 4 * here, HD), jnp.float32),
            pltpu.VMEM((n * here, 128), jnp.float32),
            pltpu.VMEM((8, n * here), jnp.float32),
            pltpu.VMEM((nz - 1, mine, 4 * here, HD), jnp.float32),
            pltpu.VMEM((nz - 1, 8, n * here), jnp.float32),
            pltpu.VMEM((nz - 1, n * here, 128), jnp.float32),
            pltpu.VMEM((4, here, mine * HD), jnp.bfloat16),
            pltpu.VMEM((8, 128), jnp.int32),
            pltpu.VMEM((4, 8, 128), jnp.int32),
            pltpu.SMEM((4, 8, 128), jnp.int32),
            pltpu.SMEM(key_tiles.shape, jnp.int32),
            pltpu.SMEM(tile_owner.shape, jnp.int32),
            pltpu.SMEM(text_count.shape, jnp.int32),
        ]
        + [dma((3,)), dma((mine, 2, 4)), dma((mine,)), dma, dma]
        + [dma((2, nz)), dma((nz,)), dma((mine, 2)), dma((mine, 2))]
        + [dma] * 11
        + [dma((3,)), pltpu.VMEM((3, here, width), jnp.bfloat16), dma((3,))],
        compiler_params=pltpu.CompilerParams(
            collective_id=0, has_side_effects=True, vmem_limit_bytes=125 << 19
        ),
        name="tile_attention",
    )(key_tiles, tile_owner, text_count, qv, kv, vv, qt, kt, vt)
    results = [pltpu.with_memory_space_constraint(x, pltpu.VMEM) for x in results]
    pieces = 4
    return pl.pallas_call(
        functools.partial(deliver, pieces),
        in_specs=[pl.BlockSpec(memory_space=pltpu.VMEM)] * 2,
        out_specs=[pl.BlockSpec(memory_space=pltpu.HBM)] * 2,
        out_shape=shapes,
        scratch_shapes=[dma((pieces + 1,))],
        name="deliver",
    )(*results)


def whole_device(*args):
    n = lax.axis_size("ctx")
    rows, width = args[0].shape
    here = args[3].shape[0]
    if rows == TILE and n % 4 == 0 and n >= 8 and n & (n - 1) == 0 and here in (16, 32, 64) and width // HD == 12:
        return fused(*args)
    return on_device(*args)


def solution(mesh):
    split = P(("groups", "ctx"), None)
    return jax.shard_map(
        whole_device,
        mesh=mesh,
        in_specs=(split,) * 7 + (P("groups"), P("groups")),
        out_specs=(split, split),
        check_vma=False,
    )
```

```python
import functools
import math

import jax
import jax.numpy as jnp
from jax import lax
from jax.experimental import pallas as pl
from jax.experimental.pallas import tpu as pltpu
from jax.sharding import PartitionSpec as P

TILE = 384
HD = 128
REACH = 2
CHUNK = 3
C2 = math.log2(math.e) / math.sqrt(HD)


def qk(q, k):
    return lax.dot_general(q, k, (((1,), (1,)), ((), ())), preferred_element_type=jnp.float32)


def pv(p, v):
    return lax.dot_general(
        p.astype(jnp.bfloat16), v, (((1,), (0,)), ((), ())), preferred_element_type=jnp.float32
    )


def softmax_parts(scores, values):
    peak = functools.reduce(jnp.maximum, [jnp.max(s, axis=-1, keepdims=True) for s in scores])
    total, acc = None, None
    for s, v in zip(scores, values):
        w = jnp.exp2((s - peak) * C2)
        t = jnp.sum(w, axis=-1, keepdims=True)
        a = pv(w, v)
        total = t if total is None else total + t
        acc = a if acc is None else acc + a
    return peak, total, acc


def video_kernel(meta, q, own, m2, p2, sib, fwd, tk, tv, prev, out):
    lo_p2 = meta[0] == 2
    hi_sib = meta[1] == 3
    hi_fwd = meta[1] == 4
    tiles = []
    for j in range(2):
        far_m, far_p = m2[j], p2[j]
        lo = jnp.where(lo_p2, far_p, far_m)
        hi = jnp.where(hi_fwd, fwd[j], jnp.where(hi_sib, sib[j], far_p))
        tiles.append((own[j], lo, hi))
    key_words = tk[...]
    value_words = tv[...]
    ok = lax.broadcasted_iota(jnp.int32, (1, key_words.shape[0]), 1) < meta[2]
    rows = 128
    for r in range(q.shape[0] // rows):
        qr = q[pl.ds(r * rows, rows), :]
        scores = [qk(qr, k) for k in tiles[0]]
        scores.append(jnp.where(ok, qk(qr, key_words), -jnp.inf))
        _, total, acc = softmax_parts(scores, list(tiles[1]) + [value_words])
        out[pl.ds(r * rows, rows), :] = (acc / total).astype(jnp.bfloat16)


def text_kernel(meta, q, k, v, kt, vt, peak_out, total_out, acc_out):
    h = pl.program_id(0)
    own = kt.shape[0]
    ok = lax.broadcasted_iota(jnp.int32, (1, own), 1) < meta[3]
    scores = [qk(q[...], k[...]), jnp.where(ok, qk(q[...], kt[...]), -jnp.inf)]
    peak, total, acc = softmax_parts(scores, [v[...], vt[...]])
    lane = lax.broadcasted_iota(jnp.int32, peak_out.shape, 1) == h
    peak_out[...] = jnp.where(lane, peak, jnp.where(h == 0, 0.0, peak_out[...]))
    total_out[...] = jnp.where(lane, total, jnp.where(h == 0, 1.0, total_out[...]))
    acc_out[...] = acc


def spread_heads(values, heads):
    return jnp.repeat(values[..., :heads], HD, axis=-1)


def on_device(qv, kv, vv, qt, kt, vt, key_tiles, tile_owner, text_count):
    n = lax.axis_size("ctx")
    me = lax.axis_index("ctx")
    rows, width = qv.shape
    heads = width // HD
    here = qt.shape[0]
    even = me % 2 == 0
    cols = CHUNK * HD
    chunks = heads // CHUNK

    text = lax.all_gather(jnp.stack([qt, kt, vt]), "ctx", axis=1, tiled=True)
    tq, tk, tv = text[0], text[1], text[2]

    tiles = tile_owner.shape[0]
    match = key_tiles[0][:, None] == jnp.arange(tiles, dtype=jnp.int32)[None, :]
    slots = jnp.sum(jnp.where(match, tile_owner[None, :], 0), axis=-1)
    off = slots - me
    near = jnp.where(even == (off == 1), 3, 4)
    code = jnp.where(off == 0, 0, jnp.where(off == -2, 1, jnp.where(off == 2, 2, near)))
    hi = jnp.max(code)
    lo = jnp.sum(code) - hi
    meta = jnp.stack([lo, hi, text_count[0], text_count[0] - me * here]).astype(jnp.int32)

    up = [(i, i - 2) for i in range(2, n)]
    down = [(i, i + 2) for i in range(n - 2)]
    swap = [(i, i ^ 1) for i in range(n)]
    fetched = []
    for c in range(chunks):
        sl = slice(c * cols, (c + 1) * cols)
        own = jnp.stack([kv[:, sl], vv[:, sl]])
        p2 = lax.ppermute(own, "ctx", up)
        m2 = lax.ppermute(own, "ctx", down)
        sib = lax.ppermute(own, "ctx", swap)
        fwd = lax.ppermute(jnp.where(even, p2, m2), "ctx", swap)
        fetched.append((own, m2, p2, sib, fwd))

    col = lambda h: (0, h)
    text_rows = tq.shape[0]
    smem = pl.BlockSpec(memory_space=pltpu.SMEM)
    peak, total, acc = pl.pallas_call(
        text_kernel,
        grid=(heads,),
        in_specs=[
            smem,
            pl.BlockSpec((text_rows, HD), col),
            pl.BlockSpec((rows, HD), col),
            pl.BlockSpec((rows, HD), col),
            pl.BlockSpec((here, HD), col),
            pl.BlockSpec((here, HD), col),
        ],
        out_specs=[
            pl.BlockSpec((text_rows, 128), lambda h: (0, 0)),
            pl.BlockSpec((text_rows, 128), lambda h: (0, 0)),
            pl.BlockSpec((text_rows, HD), col),
        ],
        out_shape=[
            jax.ShapeDtypeStruct((text_rows, 128), jnp.float32),
            jax.ShapeDtypeStruct((text_rows, 128), jnp.float32),
            jax.ShapeDtypeStruct((text_rows, width), jnp.float32),
        ],
        cost_estimate=pl.CostEstimate(
            flops=4 * text_rows * rows * width * 4, bytes_accessed=6 << 20, transcendentals=0
        ),
        name="text_partials",
    )(meta, tq, kv, vv, kt, vt)

    out = jnp.zeros((rows, width), jnp.bfloat16)
    for c in range(chunks):
        own, m2, p2, sib, fwd = fetched[c]
        tile_spec = pl.BlockSpec((2, rows, HD), lambda h: (0, 0, h))
        wide = lambda h, c=c: (0, h + c * CHUNK)
        out = pl.pallas_call(
            video_kernel,
            grid=(CHUNK,),
            in_specs=[smem, pl.BlockSpec((rows, HD), wide)]
            + [tile_spec] * 5
            + [pl.BlockSpec((text_rows, HD), wide)] * 2
            + [pl.BlockSpec(memory_space=pl.ANY)],
            out_specs=pl.BlockSpec((rows, HD), wide),
            out_shape=jax.ShapeDtypeStruct((rows, width), jnp.bfloat16),
            input_output_aliases={9: 0},
            compiler_params=pltpu.CompilerParams(vmem_limit_bytes=32 << 20),
            cost_estimate=pl.CostEstimate(
                flops=4 * rows * (3 * rows + text_rows) * cols * 4,
                bytes_accessed=8 << 20,
                transcendentals=0,
            ),
            name="video_chunk",
        )(meta, qv, own, m2, p2, sib, fwd, tk, tv, out)

    blocks = n
    stats = jnp.stack([peak, total]).reshape(2, blocks, here, 128)
    acc = acc.reshape(blocks, here, width)
    step = 1
    while step < n:
        blocks //= 2
        bit = (me // step) % 2
        pairs = [(i, i ^ step) for i in range(n)]
        stats4 = stats.reshape(2, blocks, 2, here, 128)
        acc4 = acc.reshape(blocks, 2, here, width)
        pick = lambda x, b, ax: jnp.where(
            b == 0, lax.index_in_dim(x, 0, ax, False), lax.index_in_dim(x, 1, ax, False)
        )
        their_s = lax.ppermute(pick(stats4, 1 - bit, 2), "ctx", pairs)
        their_a = lax.ppermute(pick(acc4, 1 - bit, 1), "ctx", pairs)
        my_s = pick(stats4, bit, 2)
        my_a = pick(acc4, bit, 1)
        joint = jnp.maximum(my_s[0], their_s[0])
        f_my = jnp.exp2((my_s[0] - joint) * C2)
        f_their = jnp.exp2((their_s[0] - joint) * C2)
        stats = jnp.stack([joint, my_s[1] * f_my + their_s[1] * f_their])
        acc = my_a * spread_heads(f_my, heads) + their_a * spread_heads(f_their, heads)
        step *= 2
    text_out = (acc[0] / spread_heads(stats[1, 0], heads)).astype(jnp.bfloat16)
    return (out, text_out)


def plane_kernel(n, *refs):
    listed_hbm, owner_hbm, count_hbm = refs[:3]
    q_hbm, k_hbm, v_hbm, qt_hbm, kt_hbm, vt_hbm, out, text_out = refs[3:11]
    heads = q_hbm.shape[1] // HD
    mine = heads // 4
    kv = refs[11 : 11 + mine]
    (
        qb,
        ob,
        tx,
        part,
        stats,
        flat,
        got,
        got_stats,
        tall,
        tob,
        list_out,
        list_in,
        lists,
        listed,
        owner,
        count,
        in_send,
        far_recv,
        near_recv,
        q_recv,
        tx_send,
        tx_recv,
        chain_send,
        chain_recv,
        halo_send,
        halo_recv,
        o_send,
        o_recv,
        p_send,
        p_recv,
        ps_send,
        ps_recv,
        t_send,
        t_recv,
        l_send,
        l_recv,
        l_in,
        s_in,
        words,
        words_in,
    ) = refs[11 + mine :]
    rows = q_hbm.shape[0]
    here = qt_hbm.shape[0]
    block = 4 * here
    nz = n // 4
    wide = mine * HD
    me = lax.axis_index("ctx")
    g = lax.rem(me, 4)
    core = lax.rem(g, 2)
    side = g // 2
    row = me // 4
    base = row * 4
    sib = g + 1 - 2 * core
    pair = g + 2 - 4 * side
    diag = sib + 2 - 4 * side
    mates = [pair, diag, sib]
    above, below = me + 4, me - 4
    has_above, has_below = row < nz - 1, row > 0
    peers = [lax.rem(row + k, nz) for k in range(1, nz)]
    sources = [lax.rem(row + nz - k, nz) for k in range(1, nz)]

    def cols(start, size):
        return pl.ds(pl.multiple_of(start, HD), size)

    def remote(src, dst, send, recv, dev):
        return pltpu.make_async_remote_copy(
            src_ref=src,
            dst_ref=dst,
            send_sem=send,
            recv_sem=recv,
            device_id={"ctx": dev},
            device_id_type=pl.DeviceIdType.MESH,
        )

    def greet(barrier, dev):
        pl.semaphore_signal(
            barrier, inc=1, device_id={"ctx": dev}, device_id_type=pl.DeviceIdType.MESH
        )

    barrier = pltpu.get_barrier_semaphore()
    for mate in mates:
        greet(barrier, base + mate)
    pl.when(has_above)(lambda: greet(barrier, above))
    pl.when(has_below)(lambda: greet(barrier, below))
    scalars = [
        pltpu.make_async_copy(src, dst, s_in.at[i])
        for i, (src, dst) in enumerate(
            ((listed_hbm, listed), (owner_hbm, owner), (count_hbm, count))
        )
    ]
    for copy in scalars:
        copy.start()

    arrays = (k_hbm, v_hbm, q_hbm)
    text_in = [
        pltpu.make_async_copy(ref, words.at[x], words_in)
        for x, ref in enumerate((qt_hbm, kt_hbm, vt_hbm))
    ]
    for copy in text_in:
        copy.start()

    def spot(j, x, s):
        return qb.at[j, s] if x == 2 else kv[j].at[2 + s, x]

    def source(j, x, s):
        return arrays[x].at[:, cols((s * mine + j) * HD, HD)]

    def arrival(j, x, far):
        if x == 2:
            return q_recv.at[j]
        return far_recv.at[j, x, core] if far else near_recv.at[j]

    def own_in(j, x):
        return pltpu.make_async_copy(source(j, x, g), spot(j, x, g), arrival(j, x, False))

    def send_in(j, x, k):
        return remote(
            source(j, x, mates[k]), spot(j, x, g), in_send.at[x], arrival(j, x, k < 2),
            base + mates[k],
        )

    def wait_on(ref, sem):
        pltpu.make_async_copy(ref, ref, sem).wait()

    def own_text():
        return pltpu.make_async_copy(
            words.at[:, :, cols(g * wide, wide)], tx.at[row, :, g], tx_recv
        )

    def send_text(k):
        return remote(
            words.at[:, :, cols(mates[k] * wide, wide)],
            tx.at[row, :, g],
            tx_send,
            tx_recv,
            base + mates[k],
        )

    def send_list(k):
        return remote(list_out, list_in.at[g], l_send, l_recv, base + mates[k])

    order = [(j, x) for j in range(mine) for x in range(2)] + [(j, 2) for j in range(mine)]
    for x in range(2):
        own_in(0, x).start()
    wait_on(words, words_in)
    beside = has_above.astype(jnp.int32) + has_below.astype(jnp.int32)
    pl.semaphore_wait(barrier, 3 + beside)
    for k in range(2):
        send_text(k).start()
    for x in range(2):
        for k in range(3):
            send_in(0, x, k).start()
    own_text().start()
    send_text(2).start()
    for copy in scalars:
        copy.wait()
    lane = lax.broadcasted_iota(jnp.int32, list_out.shape, 1)
    spots = jnp.zeros(list_out.shape, jnp.int32)
    for i in range(listed.shape[1]):
        spots = jnp.where(lane == i, owner[listed[0, i]], spots)
    list_out[...] = spots
    list_in[g] = spots
    for k in range(3):
        send_list(k).start()
    for j, x in order[2:]:
        for k in range(2):
            send_in(j, x, k).start()
    for j, x in order[2:]:
        own_in(j, x).start()
        send_in(j, x, 2).start()
    limit = count[0]
    place = lax.broadcasted_iota(jnp.int32, (1, n * here), 1)
    bias_all = jnp.where(place < limit, 0.0, -jnp.inf).astype(jnp.float32)
    place = row * block + lax.broadcasted_iota(jnp.int32, (1, block), 1)
    bias_own = jnp.where(place < limit, 0.0, -jnp.inf).astype(jnp.float32)

    def chain(z, up):
        return remote(
            tx.at[z], tx.at[z], chain_send.at[0 if up else 1, z], chain_recv.at[z],
            above if up else below,
        )

    def chain_wait(z):
        pltpu.make_async_copy(tx.at[z], tx.at[z], chain_recv.at[z]).wait()

    def chain_step(d):
        up_from, down_from = row - d, row + d
        if d > 0:
            pl.when(up_from >= 0)(lambda: chain_wait(up_from))
        pl.when(jnp.logical_and(up_from >= 0, has_above))(lambda: chain(up_from, True).start())
        if d > 0:
            pl.when(down_from < nz)(lambda: chain_wait(down_from))
        pl.when(jnp.logical_and(down_from < nz, has_below))(
            lambda: chain(down_from, False).start()
        )

    def chain_drain(d):
        up_from, down_from = row - d, row + d
        pl.when(jnp.logical_and(up_from >= 0, has_above))(
            lambda: chain(up_from, True).wait_send()
        )
        pl.when(jnp.logical_and(down_from < nz, has_below))(
            lambda: chain(down_from, False).wait_send()
        )

    def halo_first(far):
        return 2 * (1 - side) if far else 2 * side

    def halo_goes(far):
        up = side == 0 if far else side == 1
        return jnp.logical_or(
            jnp.logical_and(up, has_above), jnp.logical_and(jnp.logical_not(up), has_below)
        )

    def halo(j, far, x, i):
        s = halo_first(far) + i
        return remote(
            kv[j].at[2 + s, x],
            kv[j].at[lax.rem(s + 6, 8), x],
            halo_send.at[int(far)],
            halo_recv.at[j, 1 - side if far else side],
            me + 4 - 8 * side if far else me - 4 + 8 * side,
        )

    def halo_go(j, far, x, i):
        pl.when(halo_goes(far))(lambda: halo(j, far, x, i).start())

    def near_wait(j):
        wait_on(kv[j].at[pl.ds(2 + halo_first(False), 2)], near_recv.at[j])

    def near_go(j, x):
        for i in range(2):
            halo_go(j, False, x, i)

    def far_start(j):
        for x in range(2):
            for i in range(2):
                wait_on(kv[j].at[2 + halo_first(True) + i, x], far_recv.at[j, x, i])
                halo_go(j, True, x, i)

    def halo_wait(j):
        pl.when(has_above)(lambda: wait_on(kv[j].at[6:8], halo_recv.at[j, 0]))
        pl.when(has_below)(lambda: wait_on(kv[j].at[0:2], halo_recv.at[j, 1]))

    def halo_drain():
        for far in (True, False):
            pl.when(halo_goes(far))(lambda: wait_on(qb, halo_send.at[int(far)]))

    def text_words(x, j):
        return tx[:, x, :, :, j * HD : (j + 1) * HD].reshape(n * here, HD)

    def text_head(j):
        q = text_words(0, j)
        keys = [kv[j][2 + s, 0] for s in range(4)]
        values = [kv[j][2 + s, 1] for s in range(4)]
        own = [tx[row, x, :, :, j * HD : (j + 1) * HD].reshape(block, HD) for x in (1, 2)]
        scores = [qk(q, key) for key in keys] + [qk(q, own[0]) + bias_own]
        peak, total, acc = softmax_parts(scores, values + [own[1]])
        part[j] = acc.reshape(nz, block, HD)
        lane = lax.broadcasted_iota(jnp.int32, stats.shape, 1)
        old = stats[...] if j else jnp.ones(stats.shape, jnp.float32)
        stats[...] = jnp.where(lane == j, peak, jnp.where(lane == mine + j, total, old))
        if j == mine - 1:
            flat[...] = jnp.transpose(stats[...])[:8, :]

    def part_z(j, k):
        return remote(
            part.at[j, peers[k]], got.at[k, j], p_send, p_recv, peers[k] * 4 + g
        )

    def stats_z(k):
        return remote(flat, got_stats.at[k], ps_send, ps_recv, peers[k] * 4 + g)

    def out_spot(j, s):
        return out.at[:, cols((s * mine + j) * HD, HD)]

    def send_out(j, s):
        return remote(ob.at[j, s], out_spot(j, g), o_send, o_recv, base + s)

    def keep_out(j, s):
        return pltpu.make_async_copy(ob.at[j, s], out_spot(j, g), o_recv)

    def video_tile(j, s):
        at = [jnp.clip(lists[s, 0, i] - (base - 2), 0, 7) for i in range(listed.shape[1])]
        keys = [kv[j][i, 0] for i in at] + [text_words(1, j)]
        values = [kv[j][i, 1] for i in at] + [text_words(2, j)]
        step = rows
        for r in range(rows // step):
            qr = qb[j, s, r * step : (r + 1) * step, :]
            scores = [qk(qr, key) for key in keys]
            scores[-1] = scores[-1] + bias_all
            _, total, acc = softmax_parts(scores, values)
            ob[j, s, r * step : (r + 1) * step, :] = (acc / total).astype(jnp.bfloat16)
        pl.when(s == g)(lambda: keep_out(j, s).start())
        pl.when(s != g)(lambda: send_out(j, s).start())

    def video_tiles(j, lo, hi):
        def one(i, _):
            video_tile(j, lax.rem(i + 2 * (1 - side), 4))
            return 0

        lax.fori_loop(lo, hi, one, 0)

    def text_final():
        wait_on(got, p_recv)
        wait_on(got_stats, ps_recv)
        rows_here = pl.ds(pl.multiple_of(row * block, block), block)
        known = [stats[rows_here, :]]
        for k in range(nz - 1):
            full = jnp.concatenate([got_stats[k]] + [jnp.zeros_like(got_stats[k])] * 15, axis=0)
            tall[k] = jnp.transpose(full)
            known.append(tall[k, rows_here, :])
        for j in range(mine):
            peaks = [x[:, j : j + 1] for x in known]
            totals = [x[:, mine + j : mine + j + 1] for x in known]
            accs = [part[j, row]] + [got[k, j] for k in range(nz - 1)]
            joint = functools.reduce(jnp.maximum, peaks)
            weights = [jnp.exp2((p - joint) * C2) for p in peaks]
            total = sum(t * w for t, w in zip(totals, weights))
            acc = sum(a * w for a, w in zip(accs, weights))
            tob[:, :, j * HD : (j + 1) * HD] = (
                (acc / total).astype(jnp.bfloat16).reshape(4, here, HD)
            )

    def text_spot(s):
        return text_out.at[:, cols(s * wide, wide)]

    def send_words(k):
        s = mates[k]
        return remote(tob.at[s], text_spot(g), t_send, t_recv, base + s)

    def keep_words():
        return pltpu.make_async_copy(tob.at[g], text_spot(g), t_recv)

    near_wait(0)
    near_go(0, 0)
    wait_on(tx.at[row], tx_recv)
    chain_step(0)
    near_go(0, 1)
    far_start(0)
    for d in range(1, nz - 1):
        chain_step(d)
        if d < mine:
            near_wait(d)
            near_go(d, 0)
            near_go(d, 1)
    for j in range(max(1, nz - 1), mine):
        near_wait(j)
        near_go(j, 0)
        near_go(j, 1)

    def text_part(j):
        text_head(j)
        for k in range(nz - 1):
            part_z(j, k).start()
        if j == mine - 1:
            for k in range(nz - 1):
                stats_z(k).start()

    def video_wait(j):
        wait_on(qb.at[j], q_recv.at[j])
        halo_wait(j)

    far_start(1)
    pl.when(row - (nz - 1) >= 0)(lambda: chain_wait(row - (nz - 1)))
    pl.when(row + nz - 1 < nz)(lambda: chain_wait(row + nz - 1))
    text_part(0)
    wait_on(list_in.at[0:3], l_recv)
    lists_in = pltpu.make_async_copy(list_in, lists, l_in)
    lists_in.start()
    lists_in.wait()
    far_start(2)
    text_part(1)
    text_part(2)
    for j in range(mine):
        video_wait(j)
        if j < mine - 1:
            video_tiles(j, 0, 4)
        else:
            video_tiles(j, 0, 2)
            text_final()
            for k in range(3):
                send_words(k).start()
            keep_words().start()
            video_tiles(j, 2, 4)

    for x in range(3):
        wait_on(arrays[x].at[:, : 3 * wide], in_send.at[x])
    wait_on(tx.at[0, :, 0:3], tx_send)
    wait_on(list_in.at[0:3], l_send)
    halo_drain()
    for d in range(nz - 1):
        chain_drain(d)
    wait_on(got, p_send)
    wait_on(got_stats, ps_send)
    wait_on(tob.at[0:3], t_send)
    wait_on(text_out, t_recv)
    wait_on(q_hbm.at[:, : 3 * wide], o_send)
    wait_on(out, o_recv)


def deliver(pieces, video, text, video_out, text_out, sems):
    rows = video.shape[0] // pieces
    copies = [
        pltpu.make_async_copy(
            video.at[i * rows : (i + 1) * rows], video_out.at[i * rows : (i + 1) * rows], sems.at[i]
        )
        for i in range(pieces)
    ]
    copies.append(pltpu.make_async_copy(text, text_out, sems.at[pieces]))
    for copy in copies:
        copy.start()
    for copy in copies:
        copy.wait()


def deliver(pieces, video, text, video_out, text_out, sems):
    rows = video.shape[0] // pieces
    copies = [
        pltpu.make_async_copy(
            video.at[i * rows : (i + 1) * rows], video_out.at[i * rows : (i + 1) * rows], sems.at[i]
        )
        for i in range(pieces)
    ]
    copies.append(pltpu.make_async_copy(text, text_out, sems.at[pieces]))
    for copy in copies:
        copy.start()
    for copy in copies:
        copy.wait()


def fused(qv, kv, vv, qt, kt, vt, key_tiles, tile_owner, text_count):
    n = lax.axis_size("ctx")
    rows, width = qv.shape
    mine = width // HD // 4
    here = qt.shape[0]
    nz = n // 4
    dma = pltpu.SemaphoreType.DMA
    shapes = [
        jax.ShapeDtypeStruct((rows, width), jnp.bfloat16),
        jax.ShapeDtypeStruct((here, width), jnp.bfloat16),
    ]
    anywhere = pl.BlockSpec(memory_space=pl.ANY)
    results = pl.pallas_call(
        functools.partial(plane_kernel, n),
        in_specs=[pl.BlockSpec(memory_space=pltpu.HBM)] * 9,
        out_specs=[pl.BlockSpec(memory_space=pltpu.VMEM)] * 2,
        out_shape=[pltpu.VMEM(x.shape, x.dtype) for x in shapes],
        scratch_shapes=[pltpu.VMEM((8, 2, rows, HD), jnp.bfloat16)] * mine
        + [
            pltpu.VMEM((mine, 4, rows, HD), jnp.bfloat16),
            pltpu.VMEM((mine, 4, rows, HD), jnp.bfloat16),
            pltpu.VMEM((nz, 3, 4, here, mine * HD), jnp.bfloat16),
            pltpu.VMEM((mine, nz, 4 * here, HD), jnp.float32),
            pltpu.VMEM((n * here, 128), jnp.float32),
            pltpu.VMEM((8, n * here), jnp.float32),
            pltpu.VMEM((nz - 1, mine, 4 * here, HD), jnp.float32),
            pltpu.VMEM((nz - 1, 8, n * here), jnp.float32),
            pltpu.VMEM((nz - 1, n * here, 128), jnp.float32),
            pltpu.VMEM((4, here, mine * HD), jnp.bfloat16),
            pltpu.VMEM((8, 128), jnp.int32),
            pltpu.VMEM((4, 8, 128), jnp.int32),
            pltpu.SMEM((4, 8, 128), jnp.int32),
            pltpu.SMEM(key_tiles.shape, jnp.int32),
            pltpu.SMEM(tile_owner.shape, jnp.int32),
            pltpu.SMEM(text_count.shape, jnp.int32),
        ]
        + [dma((3,)), dma((mine, 2, 2)), dma((mine,)), dma((mine,)), dma, dma]
        + [dma((2, nz)), dma((nz,)), dma((2,)), dma((mine, 2))]
        + [dma] * 11
        + [dma((3,)), pltpu.VMEM((3, here, width), jnp.bfloat16), dma],
        compiler_params=pltpu.CompilerParams(
            collective_id=0, has_side_effects=True, vmem_limit_bytes=125 << 19
        ),
        name="tile_attention",
    )(key_tiles, tile_owner, text_count, qv, kv, vv, qt, kt, vt)
    results = [pltpu.with_memory_space_constraint(x, pltpu.VMEM) for x in results]
    pieces = 4
    return pl.pallas_call(
        functools.partial(deliver, pieces),
        in_specs=[pl.BlockSpec(memory_space=pltpu.VMEM)] * 2,
        out_specs=[pl.BlockSpec(memory_space=pltpu.HBM)] * 2,
        out_shape=shapes,
        scratch_shapes=[dma((pieces + 1,))],
        name="deliver",
    )(*results)


def whole_device(*args):
    n = lax.axis_size("ctx")
    rows, width = args[0].shape
    here = args[3].shape[0]
    if rows == TILE and n % 4 == 0 and n >= 8 and n & (n - 1) == 0 and here in (16, 32, 64) and width // HD == 12:
        return fused(*args)
    return on_device(*args)


def solution(mesh):
    split = P(("groups", "ctx"), None)
    return jax.shard_map(
        whole_device,
        mesh=mesh,
        in_specs=(split,) * 7 + (P("groups"), P("groups")),
        out_specs=(split, split),
        check_vma=False,
    )
```

```python
import functools
import math

import jax
import jax.numpy as jnp
from jax import lax
from jax.experimental import pallas as pl
from jax.experimental.pallas import tpu as pltpu
from jax.sharding import PartitionSpec as P

TILE = 384
HD = 128
REACH = 2
CHUNK = 3
C2 = math.log2(math.e) / math.sqrt(HD)


def qk(q, k):
    return lax.dot_general(q, k, (((1,), (1,)), ((), ())), preferred_element_type=jnp.float32)


def pv(p, v):
    return lax.dot_general(
        p.astype(jnp.bfloat16), v, (((1,), (0,)), ((), ())), preferred_element_type=jnp.float32
    )


def softmax_parts(scores, values):
    peak = functools.reduce(jnp.maximum, [jnp.max(s, axis=-1, keepdims=True) for s in scores])
    total, acc = None, None
    for s, v in zip(scores, values):
        w = jnp.exp2((s - peak) * C2)
        t = jnp.sum(w, axis=-1, keepdims=True)
        a = pv(w, v)
        total = t if total is None else total + t
        acc = a if acc is None else acc + a
    return peak, total, acc


def video_kernel(meta, q, own, m2, p2, sib, fwd, tk, tv, prev, out):
    lo_p2 = meta[0] == 2
    hi_sib = meta[1] == 3
    hi_fwd = meta[1] == 4
    tiles = []
    for j in range(2):
        far_m, far_p = m2[j], p2[j]
        lo = jnp.where(lo_p2, far_p, far_m)
        hi = jnp.where(hi_fwd, fwd[j], jnp.where(hi_sib, sib[j], far_p))
        tiles.append((own[j], lo, hi))
    key_words = tk[...]
    value_words = tv[...]
    ok = lax.broadcasted_iota(jnp.int32, (1, key_words.shape[0]), 1) < meta[2]
    rows = 128
    for r in range(q.shape[0] // rows):
        qr = q[pl.ds(r * rows, rows), :]
        scores = [qk(qr, k) for k in tiles[0]]
        scores.append(jnp.where(ok, qk(qr, key_words), -jnp.inf))
        _, total, acc = softmax_parts(scores, list(tiles[1]) + [value_words])
        out[pl.ds(r * rows, rows), :] = (acc / total).astype(jnp.bfloat16)


def text_kernel(meta, q, k, v, kt, vt, peak_out, total_out, acc_out):
    h = pl.program_id(0)
    own = kt.shape[0]
    ok = lax.broadcasted_iota(jnp.int32, (1, own), 1) < meta[3]
    scores = [qk(q[...], k[...]), jnp.where(ok, qk(q[...], kt[...]), -jnp.inf)]
    peak, total, acc = softmax_parts(scores, [v[...], vt[...]])
    lane = lax.broadcasted_iota(jnp.int32, peak_out.shape, 1) == h
    peak_out[...] = jnp.where(lane, peak, jnp.where(h == 0, 0.0, peak_out[...]))
    total_out[...] = jnp.where(lane, total, jnp.where(h == 0, 1.0, total_out[...]))
    acc_out[...] = acc


def spread_heads(values, heads):
    return jnp.repeat(values[..., :heads], HD, axis=-1)


def on_device(qv, kv, vv, qt, kt, vt, key_tiles, tile_owner, text_count):
    n = lax.axis_size("ctx")
    me = lax.axis_index("ctx")
    rows, width = qv.shape
    heads = width // HD
    here = qt.shape[0]
    even = me % 2 == 0
    cols = CHUNK * HD
    chunks = heads // CHUNK

    text = lax.all_gather(jnp.stack([qt, kt, vt]), "ctx", axis=1, tiled=True)
    tq, tk, tv = text[0], text[1], text[2]

    tiles = tile_owner.shape[0]
    match = key_tiles[0][:, None] == jnp.arange(tiles, dtype=jnp.int32)[None, :]
    slots = jnp.sum(jnp.where(match, tile_owner[None, :], 0), axis=-1)
    off = slots - me
    near = jnp.where(even == (off == 1), 3, 4)
    code = jnp.where(off == 0, 0, jnp.where(off == -2, 1, jnp.where(off == 2, 2, near)))
    hi = jnp.max(code)
    lo = jnp.sum(code) - hi
    meta = jnp.stack([lo, hi, text_count[0], text_count[0] - me * here]).astype(jnp.int32)

    up = [(i, i - 2) for i in range(2, n)]
    down = [(i, i + 2) for i in range(n - 2)]
    swap = [(i, i ^ 1) for i in range(n)]
    fetched = []
    for c in range(chunks):
        sl = slice(c * cols, (c + 1) * cols)
        own = jnp.stack([kv[:, sl], vv[:, sl]])
        p2 = lax.ppermute(own, "ctx", up)
        m2 = lax.ppermute(own, "ctx", down)
        sib = lax.ppermute(own, "ctx", swap)
        fwd = lax.ppermute(jnp.where(even, p2, m2), "ctx", swap)
        fetched.append((own, m2, p2, sib, fwd))

    col = lambda h: (0, h)
    text_rows = tq.shape[0]
    smem = pl.BlockSpec(memory_space=pltpu.SMEM)
    peak, total, acc = pl.pallas_call(
        text_kernel,
        grid=(heads,),
        in_specs=[
            smem,
            pl.BlockSpec((text_rows, HD), col),
            pl.BlockSpec((rows, HD), col),
            pl.BlockSpec((rows, HD), col),
            pl.BlockSpec((here, HD), col),
            pl.BlockSpec((here, HD), col),
        ],
        out_specs=[
            pl.BlockSpec((text_rows, 128), lambda h: (0, 0)),
            pl.BlockSpec((text_rows, 128), lambda h: (0, 0)),
            pl.BlockSpec((text_rows, HD), col),
        ],
        out_shape=[
            jax.ShapeDtypeStruct((text_rows, 128), jnp.float32),
            jax.ShapeDtypeStruct((text_rows, 128), jnp.float32),
            jax.ShapeDtypeStruct((text_rows, width), jnp.float32),
        ],
        cost_estimate=pl.CostEstimate(
            flops=4 * text_rows * rows * width * 4, bytes_accessed=6 << 20, transcendentals=0
        ),
        name="text_partials",
    )(meta, tq, kv, vv, kt, vt)

    out = jnp.zeros((rows, width), jnp.bfloat16)
    for c in range(chunks):
        own, m2, p2, sib, fwd = fetched[c]
        tile_spec = pl.BlockSpec((2, rows, HD), lambda h: (0, 0, h))
        wide = lambda h, c=c: (0, h + c * CHUNK)
        out = pl.pallas_call(
            video_kernel,
            grid=(CHUNK,),
            in_specs=[smem, pl.BlockSpec((rows, HD), wide)]
            + [tile_spec] * 5
            + [pl.BlockSpec((text_rows, HD), wide)] * 2
            + [pl.BlockSpec(memory_space=pl.ANY)],
            out_specs=pl.BlockSpec((rows, HD), wide),
            out_shape=jax.ShapeDtypeStruct((rows, width), jnp.bfloat16),
            input_output_aliases={9: 0},
            compiler_params=pltpu.CompilerParams(vmem_limit_bytes=32 << 20),
            cost_estimate=pl.CostEstimate(
                flops=4 * rows * (3 * rows + text_rows) * cols * 4,
                bytes_accessed=8 << 20,
                transcendentals=0,
            ),
            name="video_chunk",
        )(meta, qv, own, m2, p2, sib, fwd, tk, tv, out)

    blocks = n
    stats = jnp.stack([peak, total]).reshape(2, blocks, here, 128)
    acc = acc.reshape(blocks, here, width)
    step = 1
    while step < n:
        blocks //= 2
        bit = (me // step) % 2
        pairs = [(i, i ^ step) for i in range(n)]
        stats4 = stats.reshape(2, blocks, 2, here, 128)
        acc4 = acc.reshape(blocks, 2, here, width)
        pick = lambda x, b, ax: jnp.where(
            b == 0, lax.index_in_dim(x, 0, ax, False), lax.index_in_dim(x, 1, ax, False)
        )
        their_s = lax.ppermute(pick(stats4, 1 - bit, 2), "ctx", pairs)
        their_a = lax.ppermute(pick(acc4, 1 - bit, 1), "ctx", pairs)
        my_s = pick(stats4, bit, 2)
        my_a = pick(acc4, bit, 1)
        joint = jnp.maximum(my_s[0], their_s[0])
        f_my = jnp.exp2((my_s[0] - joint) * C2)
        f_their = jnp.exp2((their_s[0] - joint) * C2)
        stats = jnp.stack([joint, my_s[1] * f_my + their_s[1] * f_their])
        acc = my_a * spread_heads(f_my, heads) + their_a * spread_heads(f_their, heads)
        step *= 2
    text_out = (acc[0] / spread_heads(stats[1, 0], heads)).astype(jnp.bfloat16)
    return (out, text_out)


def plane_kernel(n, *refs):
    listed_hbm, owner_hbm, count_hbm = refs[:3]
    q_hbm, k_hbm, v_hbm, qt_hbm, kt_hbm, vt_hbm, out, text_out = refs[3:11]
    heads = q_hbm.shape[1] // HD
    mine = heads // 4
    kv = refs[11 : 11 + mine]
    (
        qb,
        ob,
        tx,
        part,
        stats,
        flat,
        got,
        got_stats,
        tall,
        tob,
        list_out,
        list_in,
        lists,
        listed,
        owner,
        count,
        in_send,
        far_recv,
        near_recv,
        q_recv,
        tx_send,
        tx_recv,
        chain_send,
        chain_recv,
        halo_send,
        halo_recv,
        o_send,
        o_recv,
        p_send,
        p_recv,
        ps_send,
        ps_recv,
        t_send,
        t_recv,
        l_send,
        l_recv,
        l_in,
        s_in,
        words,
        words_in,
    ) = refs[11 + mine :]
    rows = q_hbm.shape[0]
    here = qt_hbm.shape[0]
    block = 4 * here
    nz = n // 4
    wide = mine * HD
    me = lax.axis_index("ctx")
    g = lax.rem(me, 4)
    core = lax.rem(g, 2)
    side = g // 2
    row = me // 4
    base = row * 4
    sib = g + 1 - 2 * core
    pair = g + 2 - 4 * side
    diag = sib + 2 - 4 * side
    mates = [pair, diag, sib]
    above, below = me + 4, me - 4
    has_above, has_below = row < nz - 1, row > 0
    peers = [lax.rem(row + k, nz) for k in range(1, nz)]
    sources = [lax.rem(row + nz - k, nz) for k in range(1, nz)]

    def cols(start, size):
        return pl.ds(pl.multiple_of(start, HD), size)

    def remote(src, dst, send, recv, dev):
        return pltpu.make_async_remote_copy(
            src_ref=src,
            dst_ref=dst,
            send_sem=send,
            recv_sem=recv,
            device_id={"ctx": dev},
            device_id_type=pl.DeviceIdType.MESH,
        )

    def greet(barrier, dev):
        pl.semaphore_signal(
            barrier, inc=1, device_id={"ctx": dev}, device_id_type=pl.DeviceIdType.MESH
        )

    barrier = pltpu.get_barrier_semaphore()
    for mate in mates:
        greet(barrier, base + mate)
    pl.when(has_above)(lambda: greet(barrier, above))
    pl.when(has_below)(lambda: greet(barrier, below))
    scalars = [
        pltpu.make_async_copy(src, dst, s_in.at[i])
        for i, (src, dst) in enumerate(
            ((listed_hbm, listed), (owner_hbm, owner), (count_hbm, count))
        )
    ]
    for copy in scalars:
        copy.start()

    arrays = (k_hbm, v_hbm, q_hbm)
    text_in = [
        pltpu.make_async_copy(ref, words.at[x], words_in)
        for x, ref in enumerate((qt_hbm, kt_hbm, vt_hbm))
    ]
    for copy in text_in:
        copy.start()

    def spot(j, x, s):
        return qb.at[j, s] if x == 2 else kv[j].at[2 + s, x]

    def source(j, x, s):
        return arrays[x].at[:, cols((s * mine + j) * HD, HD)]

    def arrival(j, x, far):
        if x == 2:
            return q_recv.at[j]
        return far_recv.at[j, x, core] if far else near_recv.at[j]

    def own_in(j, x):
        return pltpu.make_async_copy(source(j, x, g), spot(j, x, g), arrival(j, x, False))

    def send_in(j, x, k):
        return remote(
            source(j, x, mates[k]), spot(j, x, g), in_send.at[x], arrival(j, x, k < 2),
            base + mates[k],
        )

    def wait_on(ref, sem):
        pltpu.make_async_copy(ref, ref, sem).wait()

    def own_text():
        return pltpu.make_async_copy(
            words.at[:, :, cols(g * wide, wide)], tx.at[row, :, g], tx_recv
        )

    def send_text(k):
        return remote(
            words.at[:, :, cols(mates[k] * wide, wide)],
            tx.at[row, :, g],
            tx_send,
            tx_recv,
            base + mates[k],
        )

    def send_list(k):
        return remote(list_out.at[0:1], list_in.at[g, 0:1], l_send, l_recv, base + mates[k])

    order = [(j, x) for j in range(mine) for x in range(2)] + [(j, 2) for j in range(mine)]
    for x in range(2):
        own_in(0, x).start()
    wait_on(words, words_in)
    beside = has_above.astype(jnp.int32) + has_below.astype(jnp.int32)
    pl.semaphore_wait(barrier, 3 + beside)
    for k in range(2):
        send_text(k).start()
    for x in range(2):
        for k in range(3):
            send_in(0, x, k).start()
    own_text().start()
    send_text(2).start()
    for copy in scalars:
        copy.wait()
    lane = lax.broadcasted_iota(jnp.int32, list_out.shape, 1)
    spots = jnp.zeros(list_out.shape, jnp.int32)
    for i in range(listed.shape[1]):
        spots = jnp.where(lane == i, owner[listed[0, i]], spots)
    list_out[...] = spots
    list_in[g] = spots
    for k in range(3):
        send_list(k).start()
    for j, x in order[2:]:
        for k in range(2):
            send_in(j, x, k).start()
    for j, x in order[2:]:
        own_in(j, x).start()
        send_in(j, x, 2).start()
    limit = count[0]
    place = lax.broadcasted_iota(jnp.int32, (1, n * here), 1)
    bias_all = jnp.where(place < limit, 0.0, -jnp.inf).astype(jnp.float32)
    place = row * block + lax.broadcasted_iota(jnp.int32, (1, block), 1)
    bias_own = jnp.where(place < limit, 0.0, -jnp.inf).astype(jnp.float32)

    def chain(z, up, d):
        return remote(
            tx.at[z], tx.at[z], chain_send.at[0 if up else 1, d], chain_recv.at[z],
            above if up else below,
        )

    def chain_wait(z):
        pltpu.make_async_copy(tx.at[z], tx.at[z], chain_recv.at[z]).wait()

    def chain_step(d):
        up_from, down_from = row - d, row + d
        if d > 0:
            pl.when(up_from >= 0)(lambda: chain_wait(up_from))
        pl.when(jnp.logical_and(up_from >= 0, has_above))(lambda: chain(up_from, True, d).start())
        if d > 0:
            pl.when(down_from < nz)(lambda: chain_wait(down_from))
        pl.when(jnp.logical_and(down_from < nz, has_below))(
            lambda: chain(down_from, False, d).start()
        )

    def chain_drain(d):
        up_from, down_from = row - d, row + d
        pl.when(jnp.logical_and(up_from >= 0, has_above))(
            lambda: chain(up_from, True, d).wait_send()
        )
        pl.when(jnp.logical_and(down_from < nz, has_below))(
            lambda: chain(down_from, False, d).wait_send()
        )

    def halo_first(far):
        return 2 * (1 - side) if far else 2 * side

    def halo_goes(far):
        up = side == 0 if far else side == 1
        return jnp.logical_or(
            jnp.logical_and(up, has_above), jnp.logical_and(jnp.logical_not(up), has_below)
        )

    def halo(j, far, x, i):
        s = halo_first(far) + i
        return remote(
            kv[j].at[2 + s, x],
            kv[j].at[lax.rem(s + 6, 8), x],
            halo_send.at[int(far)],
            halo_recv.at[j, 1 - side if far else side],
            me + 4 - 8 * side if far else me - 4 + 8 * side,
        )

    def halo_go(j, far, x, i):
        pl.when(halo_goes(far))(lambda: halo(j, far, x, i).start())

    def near_wait(j):
        wait_on(kv[j].at[pl.ds(2 + halo_first(False), 2)], near_recv.at[j])

    def near_go(j, x):
        for i in range(2):
            halo_go(j, False, x, i)

    def far_start(j):
        for x in range(2):
            for i in range(2):
                wait_on(kv[j].at[2 + halo_first(True) + i, x], far_recv.at[j, x, i])
                halo_go(j, True, x, i)

    def halo_wait(j):
        pl.when(has_above)(lambda: wait_on(kv[j].at[6:8], halo_recv.at[j, 0]))
        pl.when(has_below)(lambda: wait_on(kv[j].at[0:2], halo_recv.at[j, 1]))

    def halo_drain():
        for far in (True, False):
            pl.when(halo_goes(far))(lambda: wait_on(qb, halo_send.at[int(far)]))

    def text_words(x, j):
        return tx[:, x, :, :, j * HD : (j + 1) * HD].reshape(n * here, HD)

    def text_head(j):
        q = text_words(0, j)
        keys = [kv[j][2 + s, 0] for s in range(4)]
        values = [kv[j][2 + s, 1] for s in range(4)]
        own = [tx[row, x, :, :, j * HD : (j + 1) * HD].reshape(block, HD) for x in (1, 2)]
        scores = [qk(q, key) for key in keys] + [qk(q, own[0]) + bias_own]
        peak, total, acc = softmax_parts(scores, values + [own[1]])
        part[j] = acc.reshape(nz, block, HD)
        lane = lax.broadcasted_iota(jnp.int32, stats.shape, 1)
        old = stats[...] if j else jnp.ones(stats.shape, jnp.float32)
        stats[...] = jnp.where(lane == j, peak, jnp.where(lane == mine + j, total, old))
        if j == mine - 1:
            flat[...] = jnp.transpose(stats[...])[:8, :]

    def part_z(j, k):
        return remote(
            part.at[j, peers[k]], got.at[k, j], p_send, p_recv, peers[k] * 4 + g
        )

    def stats_z(k):
        return remote(flat, got_stats.at[k], ps_send, ps_recv, peers[k] * 4 + g)

    def out_spot(j, s):
        return out.at[:, cols((s * mine + j) * HD, HD)]

    def send_out(j, s):
        return remote(ob.at[j, s], out_spot(j, g), o_send, o_recv, base + s)

    def keep_out(j, s):
        return pltpu.make_async_copy(ob.at[j, s], out_spot(j, g), o_recv)

    def video_tile(j, s):
        at = [jnp.clip(lists[s, 0, i] - (base - 2), 0, 7) for i in range(listed.shape[1])]
        keys = [kv[j][i, 0] for i in at] + [text_words(1, j)]
        values = [kv[j][i, 1] for i in at] + [text_words(2, j)]
        step = rows
        for r in range(rows // step):
            qr = qb[j, s, r * step : (r + 1) * step, :]
            scores = [qk(qr, key) for key in keys]
            scores[-1] = scores[-1] + bias_all
            _, total, acc = softmax_parts(scores, values)
            ob[j, s, r * step : (r + 1) * step, :] = (acc / total).astype(jnp.bfloat16)
        pl.when(s == g)(lambda: keep_out(j, s).start())
        pl.when(s != g)(lambda: send_out(j, s).start())

    def video_tiles(j, lo, hi):
        def one(i, _):
            video_tile(j, lax.rem(i + 2 * (1 - side), 4))
            return 0

        lax.fori_loop(lo, hi, one, 0)

    def text_final():
        wait_on(got, p_recv)
        wait_on(got_stats, ps_recv)
        rows_here = pl.ds(pl.multiple_of(row * block, block), block)
        known = [stats[rows_here, :]]
        for k in range(nz - 1):
            full = jnp.concatenate([got_stats[k]] + [jnp.zeros_like(got_stats[k])] * 15, axis=0)
            tall[k] = jnp.transpose(full)
            known.append(tall[k, rows_here, :])
        for j in range(mine):
            peaks = [x[:, j : j + 1] for x in known]
            totals = [x[:, mine + j : mine + j + 1] for x in known]
            accs = [part[j, row]] + [got[k, j] for k in range(nz - 1)]
            joint = functools.reduce(jnp.maximum, peaks)
            weights = [jnp.exp2((p - joint) * C2) for p in peaks]
            total = sum(t * w for t, w in zip(totals, weights))
            acc = sum(a * w for a, w in zip(accs, weights))
            tob[:, :, j * HD : (j + 1) * HD] = (
                (acc / total).astype(jnp.bfloat16).reshape(4, here, HD)
            )

    def text_spot(s):
        return text_out.at[:, cols(s * wide, wide)]

    def send_words(k):
        s = mates[k]
        return remote(tob.at[s], text_spot(g), t_send, t_recv, base + s)

    def keep_words():
        return pltpu.make_async_copy(tob.at[g], text_spot(g), t_recv)

    near_wait(0)
    near_go(0, 0)
    wait_on(tx.at[row], tx_recv)
    chain_step(0)
    near_go(0, 1)
    far_start(0)
    for d in range(1, nz - 1):
        chain_step(d)
        if d < mine:
            near_wait(d)
            near_go(d, 0)
            near_go(d, 1)
    for j in range(max(1, nz - 1), mine):
        near_wait(j)
        near_go(j, 0)
        near_go(j, 1)

    def text_part(j):
        text_head(j)
        for k in range(nz - 1):
            part_z(j, k).start()
        if j == mine - 1:
            for k in range(nz - 1):
                stats_z(k).start()

    def video_wait(j):
        wait_on(qb.at[j], q_recv.at[j])
        halo_wait(j)

    far_start(1)
    pl.when(row - (nz - 1) >= 0)(lambda: chain_wait(row - (nz - 1)))
    pl.when(row + nz - 1 < nz)(lambda: chain_wait(row + nz - 1))
    text_part(0)
    wait_on(list_in.at[0:3, 0:1], l_recv)
    lists_in = pltpu.make_async_copy(list_in, lists, l_in)
    lists_in.start()
    lists_in.wait()
    far_start(2)
    text_part(1)
    text_part(2)
    for j in range(mine):
        video_wait(j)
        if j < mine - 1:
            video_tiles(j, 0, 4)
        else:
            video_tiles(j, 0, 2)
            text_final()
            for k in range(3):
                send_words(k).start()
            keep_words().start()
            video_tiles(j, 2, 4)

    for x in range(3):
        wait_on(arrays[x].at[:, : 3 * wide], in_send.at[x])
    wait_on(tx.at[0, :, 0:3], tx_send)
    wait_on(list_in.at[0:3, 0:1], l_send)
    halo_drain()
    for d in range(nz - 1):
        chain_drain(d)
    wait_on(got, p_send)
    wait_on(got_stats, ps_send)
    wait_on(tob.at[0:3], t_send)
    wait_on(text_out, t_recv)
    wait_on(q_hbm.at[:, : 3 * wide], o_send)
    wait_on(out, o_recv)


def deliver(pieces, video, text, video_out, text_out, sems):
    rows = video.shape[0] // pieces
    copies = [
        pltpu.make_async_copy(
            video.at[i * rows : (i + 1) * rows], video_out.at[i * rows : (i + 1) * rows], sems.at[i]
        )
        for i in range(pieces)
    ]
    copies.append(pltpu.make_async_copy(text, text_out, sems.at[pieces]))
    for copy in copies:
        copy.start()
    for copy in copies:
        copy.wait()


def deliver(pieces, video, text, video_out, text_out, sems):
    rows = video.shape[0] // pieces
    copies = [
        pltpu.make_async_copy(
            video.at[i * rows : (i + 1) * rows], video_out.at[i * rows : (i + 1) * rows], sems.at[i]
        )
        for i in range(pieces)
    ]
    copies.append(pltpu.make_async_copy(text, text_out, sems.at[pieces]))
    for copy in copies:
        copy.start()
    for copy in copies:
        copy.wait()


def fused(qv, kv, vv, qt, kt, vt, key_tiles, tile_owner, text_count):
    n = lax.axis_size("ctx")
    rows, width = qv.shape
    mine = width // HD // 4
    here = qt.shape[0]
    nz = n // 4
    dma = pltpu.SemaphoreType.DMA
    shapes = [
        jax.ShapeDtypeStruct((rows, width), jnp.bfloat16),
        jax.ShapeDtypeStruct((here, width), jnp.bfloat16),
    ]
    anywhere = pl.BlockSpec(memory_space=pl.ANY)
    results = pl.pallas_call(
        functools.partial(plane_kernel, n),
        in_specs=[pl.BlockSpec(memory_space=pltpu.HBM)] * 9,
        out_specs=[pl.BlockSpec(memory_space=pltpu.VMEM)] * 2,
        out_shape=[pltpu.VMEM(x.shape, x.dtype) for x in shapes],
        scratch_shapes=[pltpu.VMEM((8, 2, rows, HD), jnp.bfloat16)] * mine
        + [
            pltpu.VMEM((mine, 4, rows, HD), jnp.bfloat16),
            pltpu.VMEM((mine, 4, rows, HD), jnp.bfloat16),
            pltpu.VMEM((nz, 3, 4, here, mine * HD), jnp.bfloat16),
            pltpu.VMEM((mine, nz, 4 * here, HD), jnp.float32),
            pltpu.VMEM((n * here, 128), jnp.float32),
            pltpu.VMEM((8, n * here), jnp.float32),
            pltpu.VMEM((nz - 1, mine, 4 * here, HD), jnp.float32),
            pltpu.VMEM((nz - 1, 8, n * here), jnp.float32),
            pltpu.VMEM((nz - 1, n * here, 128), jnp.float32),
            pltpu.VMEM((4, here, mine * HD), jnp.bfloat16),
            pltpu.VMEM((8, 128), jnp.int32),
            pltpu.VMEM((4, 8, 128), jnp.int32),
            pltpu.SMEM((4, 8, 128), jnp.int32),
            pltpu.SMEM(key_tiles.shape, jnp.int32),
            pltpu.SMEM(tile_owner.shape, jnp.int32),
            pltpu.SMEM(text_count.shape, jnp.int32),
        ]
        + [dma((3,)), dma((mine, 2, 2)), dma((mine,)), dma((mine,)), dma, dma]
        + [dma((2, nz - 1)), dma((nz,)), dma((2,)), dma((mine, 2))]
        + [dma] * 11
        + [dma((3,)), pltpu.VMEM((3, here, width), jnp.bfloat16), dma],
        compiler_params=pltpu.CompilerParams(
            collective_id=0, has_side_effects=True, vmem_limit_bytes=125 << 19
        ),
        name="tile_attention",
    )(key_tiles, tile_owner, text_count, qv, kv, vv, qt, kt, vt)
    results = [pltpu.with_memory_space_constraint(x, pltpu.VMEM) for x in results]
    pieces = 4
    return pl.pallas_call(
        functools.partial(deliver, pieces),
        in_specs=[pl.BlockSpec(memory_space=pltpu.VMEM)] * 2,
        out_specs=[pl.BlockSpec(memory_space=pltpu.HBM)] * 2,
        out_shape=shapes,
        scratch_shapes=[dma((pieces + 1,))],
        name="deliver",
    )(*results)


def whole_device(*args):
    n = lax.axis_size("ctx")
    rows, width = args[0].shape
    here = args[3].shape[0]
    if rows == TILE and n % 4 == 0 and n >= 8 and n & (n - 1) == 0 and here in (16, 32, 64) and width // HD == 12:
        return fused(*args)
    return on_device(*args)


def solution(mesh):
    split = P(("groups", "ctx"), None)
    return jax.shard_map(
        whole_device,
        mesh=mesh,
        in_specs=(split,) * 7 + (P("groups"), P("groups")),
        out_specs=(split, split),
        check_vma=False,
    )
```

```python
import functools
import math

import jax
import jax.numpy as jnp
from jax import lax
from jax.experimental import pallas as pl
from jax.experimental.pallas import tpu as pltpu
from jax.sharding import PartitionSpec as P

TILE = 384
HD = 128
REACH = 2
CHUNK = 3
C2 = math.log2(math.e) / math.sqrt(HD)


def qk(q, k):
    return lax.dot_general(q, k, (((1,), (1,)), ((), ())), preferred_element_type=jnp.float32)


def pv(p, v):
    return lax.dot_general(
        p.astype(jnp.bfloat16), v, (((1,), (0,)), ((), ())), preferred_element_type=jnp.float32
    )


def softmax_parts(scores, values):
    peak = functools.reduce(jnp.maximum, [jnp.max(s, axis=-1, keepdims=True) for s in scores])
    total, acc = None, None
    for s, v in zip(scores, values):
        w = jnp.exp2((s - peak) * C2)
        t = jnp.sum(w, axis=-1, keepdims=True)
        a = pv(w, v)
        total = t if total is None else total + t
        acc = a if acc is None else acc + a
    return peak, total, acc


def video_kernel(meta, q, own, m2, p2, sib, fwd, tk, tv, prev, out):
    lo_p2 = meta[0] == 2
    hi_sib = meta[1] == 3
    hi_fwd = meta[1] == 4
    tiles = []
    for j in range(2):
        far_m, far_p = m2[j], p2[j]
        lo = jnp.where(lo_p2, far_p, far_m)
        hi = jnp.where(hi_fwd, fwd[j], jnp.where(hi_sib, sib[j], far_p))
        tiles.append((own[j], lo, hi))
    key_words = tk[...]
    value_words = tv[...]
    ok = lax.broadcasted_iota(jnp.int32, (1, key_words.shape[0]), 1) < meta[2]
    rows = 128
    for r in range(q.shape[0] // rows):
        qr = q[pl.ds(r * rows, rows), :]
        scores = [qk(qr, k) for k in tiles[0]]
        scores.append(jnp.where(ok, qk(qr, key_words), -jnp.inf))
        _, total, acc = softmax_parts(scores, list(tiles[1]) + [value_words])
        out[pl.ds(r * rows, rows), :] = (acc / total).astype(jnp.bfloat16)


def text_kernel(meta, q, k, v, kt, vt, peak_out, total_out, acc_out):
    h = pl.program_id(0)
    own = kt.shape[0]
    ok = lax.broadcasted_iota(jnp.int32, (1, own), 1) < meta[3]
    scores = [qk(q[...], k[...]), jnp.where(ok, qk(q[...], kt[...]), -jnp.inf)]
    peak, total, acc = softmax_parts(scores, [v[...], vt[...]])
    lane = lax.broadcasted_iota(jnp.int32, peak_out.shape, 1) == h
    peak_out[...] = jnp.where(lane, peak, jnp.where(h == 0, 0.0, peak_out[...]))
    total_out[...] = jnp.where(lane, total, jnp.where(h == 0, 1.0, total_out[...]))
    acc_out[...] = acc


def spread_heads(values, heads):
    return jnp.repeat(values[..., :heads], HD, axis=-1)


def on_device(qv, kv, vv, qt, kt, vt, key_tiles, tile_owner, text_count):
    n = lax.axis_size("ctx")
    me = lax.axis_index("ctx")
    rows, width = qv.shape
    heads = width // HD
    here = qt.shape[0]
    even = me % 2 == 0
    cols = CHUNK * HD
    chunks = heads // CHUNK

    text = lax.all_gather(jnp.stack([qt, kt, vt]), "ctx", axis=1, tiled=True)
    tq, tk, tv = text[0], text[1], text[2]

    tiles = tile_owner.shape[0]
    match = key_tiles[0][:, None] == jnp.arange(tiles, dtype=jnp.int32)[None, :]
    slots = jnp.sum(jnp.where(match, tile_owner[None, :], 0), axis=-1)
    off = slots - me
    near = jnp.where(even == (off == 1), 3, 4)
    code = jnp.where(off == 0, 0, jnp.where(off == -2, 1, jnp.where(off == 2, 2, near)))
    hi = jnp.max(code)
    lo = jnp.sum(code) - hi
    meta = jnp.stack([lo, hi, text_count[0], text_count[0] - me * here]).astype(jnp.int32)

    up = [(i, i - 2) for i in range(2, n)]
    down = [(i, i + 2) for i in range(n - 2)]
    swap = [(i, i ^ 1) for i in range(n)]
    fetched = []
    for c in range(chunks):
        sl = slice(c * cols, (c + 1) * cols)
        own = jnp.stack([kv[:, sl], vv[:, sl]])
        p2 = lax.ppermute(own, "ctx", up)
        m2 = lax.ppermute(own, "ctx", down)
        sib = lax.ppermute(own, "ctx", swap)
        fwd = lax.ppermute(jnp.where(even, p2, m2), "ctx", swap)
        fetched.append((own, m2, p2, sib, fwd))

    col = lambda h: (0, h)
    text_rows = tq.shape[0]
    smem = pl.BlockSpec(memory_space=pltpu.SMEM)
    peak, total, acc = pl.pallas_call(
        text_kernel,
        grid=(heads,),
        in_specs=[
            smem,
            pl.BlockSpec((text_rows, HD), col),
            pl.BlockSpec((rows, HD), col),
            pl.BlockSpec((rows, HD), col),
            pl.BlockSpec((here, HD), col),
            pl.BlockSpec((here, HD), col),
        ],
        out_specs=[
            pl.BlockSpec((text_rows, 128), lambda h: (0, 0)),
            pl.BlockSpec((text_rows, 128), lambda h: (0, 0)),
            pl.BlockSpec((text_rows, HD), col),
        ],
        out_shape=[
            jax.ShapeDtypeStruct((text_rows, 128), jnp.float32),
            jax.ShapeDtypeStruct((text_rows, 128), jnp.float32),
            jax.ShapeDtypeStruct((text_rows, width), jnp.float32),
        ],
        cost_estimate=pl.CostEstimate(
            flops=4 * text_rows * rows * width * 4, bytes_accessed=6 << 20, transcendentals=0
        ),
        name="text_partials",
    )(meta, tq, kv, vv, kt, vt)

    out = jnp.zeros((rows, width), jnp.bfloat16)
    for c in range(chunks):
        own, m2, p2, sib, fwd = fetched[c]
        tile_spec = pl.BlockSpec((2, rows, HD), lambda h: (0, 0, h))
        wide = lambda h, c=c: (0, h + c * CHUNK)
        out = pl.pallas_call(
            video_kernel,
            grid=(CHUNK,),
            in_specs=[smem, pl.BlockSpec((rows, HD), wide)]
            + [tile_spec] * 5
            + [pl.BlockSpec((text_rows, HD), wide)] * 2
            + [pl.BlockSpec(memory_space=pl.ANY)],
            out_specs=pl.BlockSpec((rows, HD), wide),
            out_shape=jax.ShapeDtypeStruct((rows, width), jnp.bfloat16),
            input_output_aliases={9: 0},
            compiler_params=pltpu.CompilerParams(vmem_limit_bytes=32 << 20),
            cost_estimate=pl.CostEstimate(
                flops=4 * rows * (3 * rows + text_rows) * cols * 4,
                bytes_accessed=8 << 20,
                transcendentals=0,
            ),
            name="video_chunk",
        )(meta, qv, own, m2, p2, sib, fwd, tk, tv, out)

    blocks = n
    stats = jnp.stack([peak, total]).reshape(2, blocks, here, 128)
    acc = acc.reshape(blocks, here, width)
    step = 1
    while step < n:
        blocks //= 2
        bit = (me // step) % 2
        pairs = [(i, i ^ step) for i in range(n)]
        stats4 = stats.reshape(2, blocks, 2, here, 128)
        acc4 = acc.reshape(blocks, 2, here, width)
        pick = lambda x, b, ax: jnp.where(
            b == 0, lax.index_in_dim(x, 0, ax, False), lax.index_in_dim(x, 1, ax, False)
        )
        their_s = lax.ppermute(pick(stats4, 1 - bit, 2), "ctx", pairs)
        their_a = lax.ppermute(pick(acc4, 1 - bit, 1), "ctx", pairs)
        my_s = pick(stats4, bit, 2)
        my_a = pick(acc4, bit, 1)
        joint = jnp.maximum(my_s[0], their_s[0])
        f_my = jnp.exp2((my_s[0] - joint) * C2)
        f_their = jnp.exp2((their_s[0] - joint) * C2)
        stats = jnp.stack([joint, my_s[1] * f_my + their_s[1] * f_their])
        acc = my_a * spread_heads(f_my, heads) + their_a * spread_heads(f_their, heads)
        step *= 2
    text_out = (acc[0] / spread_heads(stats[1, 0], heads)).astype(jnp.bfloat16)
    return (out, text_out)


def plane_kernel(n, *refs):
    listed_hbm, owner_hbm, count_hbm = refs[:3]
    q_hbm, k_hbm, v_hbm, qt_hbm, kt_hbm, vt_hbm, out, text_out = refs[3:11]
    heads = q_hbm.shape[1] // HD
    mine = heads // 4
    kv = refs[11 : 11 + mine]
    (
        qb,
        ob,
        tx,
        part,
        stats,
        flat,
        got,
        got_stats,
        tall,
        tob,
        list_out,
        list_in,
        lists,
        listed,
        owner,
        count,
        in_send,
        far_recv,
        near_recv,
        q_recv,
        tx_send,
        tx_recv,
        chain_send,
        chain_recv,
        halo_send,
        halo_recv,
        o_send,
        o_recv,
        p_send,
        p_recv,
        ps_send,
        ps_recv,
        t_send,
        t_recv,
        l_send,
        l_recv,
        l_in,
        s_in,
        words,
        words_in,
    ) = refs[11 + mine :]
    rows = q_hbm.shape[0]
    here = qt_hbm.shape[0]
    block = 4 * here
    nz = n // 4
    wide = mine * HD
    me = lax.axis_index("ctx")
    g = lax.rem(me, 4)
    core = lax.rem(g, 2)
    side = g // 2
    row = me // 4
    base = row * 4
    sib = g + 1 - 2 * core
    pair = g + 2 - 4 * side
    diag = sib + 2 - 4 * side
    mates = [pair, diag, sib]
    above, below = me + 4, me - 4
    has_above, has_below = row < nz - 1, row > 0
    peers = [lax.rem(row + k, nz) for k in range(1, nz)]
    sources = [lax.rem(row + nz - k, nz) for k in range(1, nz)]

    def cols(start, size):
        return pl.ds(pl.multiple_of(start, HD), size)

    def remote(src, dst, send, recv, dev):
        return pltpu.make_async_remote_copy(
            src_ref=src,
            dst_ref=dst,
            send_sem=send,
            recv_sem=recv,
            device_id={"ctx": dev},
            device_id_type=pl.DeviceIdType.MESH,
        )

    def greet(barrier, dev):
        pl.semaphore_signal(
            barrier, inc=1, device_id={"ctx": dev}, device_id_type=pl.DeviceIdType.MESH
        )

    barrier = pltpu.get_barrier_semaphore()
    for mate in mates:
        greet(barrier, base + mate)
    pl.when(has_above)(lambda: greet(barrier, above))
    pl.when(has_below)(lambda: greet(barrier, below))
    scalars = [
        pltpu.make_async_copy(src, dst, s_in.at[i])
        for i, (src, dst) in enumerate(
            ((listed_hbm, listed), (owner_hbm, owner), (count_hbm, count))
        )
    ]
    for copy in scalars:
        copy.start()

    arrays = (k_hbm, v_hbm, q_hbm)
    text_in = [
        pltpu.make_async_copy(ref, words.at[x], words_in)
        for x, ref in enumerate((qt_hbm, kt_hbm, vt_hbm))
    ]
    for copy in text_in:
        copy.start()

    def spot(j, x, s):
        return qb.at[j, s] if x == 2 else kv[j].at[2 + s, x]

    def source(j, x, s):
        return arrays[x].at[:, cols((s * mine + j) * HD, HD)]

    def arrival(j, x, far):
        if x == 2:
            return q_recv.at[j]
        return far_recv.at[j, x] if far else near_recv.at[j]

    def own_in(j, x):
        return pltpu.make_async_copy(source(j, x, g), spot(j, x, g), arrival(j, x, False))

    def send_in(j, x, k):
        return remote(
            source(j, x, mates[k]), spot(j, x, g), in_send.at[x], arrival(j, x, k < 2),
            base + mates[k],
        )

    def wait_on(ref, sem):
        pltpu.make_async_copy(ref, ref, sem).wait()

    def own_text():
        return pltpu.make_async_copy(
            words.at[:, :, cols(g * wide, wide)], tx.at[row, :, g], tx_recv
        )

    def send_text(k):
        return remote(
            words.at[:, :, cols(mates[k] * wide, wide)],
            tx.at[row, :, g],
            tx_send,
            tx_recv,
            base + mates[k],
        )

    def send_list(k):
        return remote(list_out.at[0:1], list_in.at[g, 0:1], l_send, l_recv, base + mates[k])

    order = [(j, x) for j in range(mine) for x in range(2)] + [(j, 2) for j in range(mine)]
    for x in range(2):
        own_in(0, x).start()
    wait_on(words, words_in)
    beside = has_above.astype(jnp.int32) + has_below.astype(jnp.int32)
    pl.semaphore_wait(barrier, 3 + beside)
    for k in range(2):
        send_text(k).start()
    for x in range(2):
        for k in range(3):
            send_in(0, x, k).start()
    own_text().start()
    send_text(2).start()
    for copy in scalars:
        copy.wait()
    lane = lax.broadcasted_iota(jnp.int32, list_out.shape, 1)
    spots = jnp.zeros(list_out.shape, jnp.int32)
    for i in range(listed.shape[1]):
        spots = jnp.where(lane == i, owner[listed[0, i]], spots)
    list_out[...] = spots
    list_in[g] = spots
    for k in range(3):
        send_list(k).start()
    for j, x in order[2:]:
        for k in range(2):
            send_in(j, x, k).start()
    for j, x in order[2:]:
        own_in(j, x).start()
        send_in(j, x, 2).start()
    limit = count[0]
    place = lax.broadcasted_iota(jnp.int32, (1, n * here), 1)
    bias_all = jnp.where(place < limit, 0.0, -jnp.inf).astype(jnp.float32)
    place = row * block + lax.broadcasted_iota(jnp.int32, (1, block), 1)
    bias_own = jnp.where(place < limit, 0.0, -jnp.inf).astype(jnp.float32)

    def chain(z, up, d):
        return remote(
            tx.at[z], tx.at[z], chain_send.at[0 if up else 1, d], chain_recv.at[z],
            above if up else below,
        )

    def chain_wait(z):
        pltpu.make_async_copy(tx.at[z], tx.at[z], chain_recv.at[z]).wait()

    def chain_step(d):
        up_from, down_from = row - d, row + d
        if d > 0:
            pl.when(up_from >= 0)(lambda: chain_wait(up_from))
        pl.when(jnp.logical_and(up_from >= 0, has_above))(lambda: chain(up_from, True, d).start())
        if d > 0:
            pl.when(down_from < nz)(lambda: chain_wait(down_from))
        pl.when(jnp.logical_and(down_from < nz, has_below))(
            lambda: chain(down_from, False, d).start()
        )

    def chain_drain(d):
        up_from, down_from = row - d, row + d
        pl.when(jnp.logical_and(up_from >= 0, has_above))(
            lambda: chain(up_from, True, d).wait_send()
        )
        pl.when(jnp.logical_and(down_from < nz, has_below))(
            lambda: chain(down_from, False, d).wait_send()
        )

    def halo_first(far):
        return 2 * (1 - side) if far else 2 * side

    def halo_goes(far):
        up = side == 0 if far else side == 1
        return jnp.logical_or(
            jnp.logical_and(up, has_above), jnp.logical_and(jnp.logical_not(up), has_below)
        )

    def halo(j, far, x, i):
        s = halo_first(far) + i
        return remote(
            kv[j].at[2 + s, x],
            kv[j].at[lax.rem(s + 6, 8), x],
            halo_send.at[int(far)],
            halo_recv.at[j, 1 - side if far else side],
            me + 4 - 8 * side if far else me - 4 + 8 * side,
        )

    def halo_go(j, far, x, i):
        pl.when(halo_goes(far))(lambda: halo(j, far, x, i).start())

    def near_wait(j):
        wait_on(kv[j].at[pl.ds(2 + halo_first(False), 2)], near_recv.at[j])

    def near_go(j, x):
        for i in range(2):
            halo_go(j, False, x, i)

    def far_start(j):
        for x in range(2):
            wait_on(kv[j].at[pl.ds(2 + halo_first(True), 2), x], far_recv.at[j, x])
            for i in range(2):
                halo_go(j, True, x, i)

    def halo_wait(j):
        pl.when(has_above)(lambda: wait_on(kv[j].at[6:8], halo_recv.at[j, 0]))
        pl.when(has_below)(lambda: wait_on(kv[j].at[0:2], halo_recv.at[j, 1]))

    def halo_drain():
        for far in (True, False):
            pl.when(halo_goes(far))(lambda: wait_on(qb, halo_send.at[int(far)]))

    def text_words(x, j):
        return tx[:, x, :, :, j * HD : (j + 1) * HD].reshape(n * here, HD)

    def text_head(j):
        q = text_words(0, j)
        keys = [kv[j][2 + s, 0] for s in range(4)]
        values = [kv[j][2 + s, 1] for s in range(4)]
        own = [tx[row, x, :, :, j * HD : (j + 1) * HD].reshape(block, HD) for x in (1, 2)]
        scores = [qk(q, key) for key in keys] + [qk(q, own[0]) + bias_own]
        peak, total, acc = softmax_parts(scores, values + [own[1]])
        part[j] = acc.reshape(nz, block, HD)
        lane = lax.broadcasted_iota(jnp.int32, stats.shape, 1)
        old = stats[...] if j else jnp.ones(stats.shape, jnp.float32)
        stats[...] = jnp.where(lane == j, peak, jnp.where(lane == mine + j, total, old))
        if j == mine - 1:
            flat[...] = jnp.transpose(stats[...])[:8, :]

    def part_z(j, k):
        return remote(
            part.at[j, peers[k]], got.at[k, j], p_send, p_recv, peers[k] * 4 + g
        )

    def stats_z(k):
        return remote(flat, got_stats.at[k], ps_send, ps_recv, peers[k] * 4 + g)

    def out_spot(j, s):
        return out.at[:, cols((s * mine + j) * HD, HD)]

    def send_out(j, s):
        return remote(ob.at[j, s], out_spot(j, g), o_send, o_recv, base + s)

    def keep_out(j, s):
        return pltpu.make_async_copy(ob.at[j, s], out_spot(j, g), o_recv)

    def video_tile(j, s):
        at = [jnp.clip(lists[s, 0, i] - (base - 2), 0, 7) for i in range(listed.shape[1])]
        keys = [kv[j][i, 0] for i in at] + [text_words(1, j)]
        values = [kv[j][i, 1] for i in at] + [text_words(2, j)]
        step = rows
        for r in range(rows // step):
            qr = qb[j, s, r * step : (r + 1) * step, :]
            scores = [qk(qr, key) for key in keys]
            scores[-1] = scores[-1] + bias_all
            _, total, acc = softmax_parts(scores, values)
            ob[j, s, r * step : (r + 1) * step, :] = (acc / total).astype(jnp.bfloat16)
        pl.when(s == g)(lambda: keep_out(j, s).start())
        pl.when(s != g)(lambda: send_out(j, s).start())

    def video_tiles(j, lo, hi):
        def one(i, _):
            video_tile(j, lax.rem(i + 2 * (1 - side), 4))
            return 0

        lax.fori_loop(lo, hi, one, 0)

    def text_final():
        wait_on(got, p_recv)
        wait_on(got_stats, ps_recv)
        rows_here = pl.ds(pl.multiple_of(row * block, block), block)
        known = [stats[rows_here, :]]
        for k in range(nz - 1):
            full = jnp.concatenate([got_stats[k]] + [jnp.zeros_like(got_stats[k])] * 15, axis=0)
            tall[k] = jnp.transpose(full)
            known.append(tall[k, rows_here, :])
        for j in range(mine):
            peaks = [x[:, j : j + 1] for x in known]
            totals = [x[:, mine + j : mine + j + 1] for x in known]
            accs = [part[j, row]] + [got[k, j] for k in range(nz - 1)]
            joint = functools.reduce(jnp.maximum, peaks)
            weights = [jnp.exp2((p - joint) * C2) for p in peaks]
            total = sum(t * w for t, w in zip(totals, weights))
            acc = sum(a * w for a, w in zip(accs, weights))
            tob[:, :, j * HD : (j + 1) * HD] = (
                (acc / total).astype(jnp.bfloat16).reshape(4, here, HD)
            )

    def text_spot(s):
        return text_out.at[:, cols(s * wide, wide)]

    def send_words(k):
        s = mates[k]
        return remote(tob.at[s], text_spot(g), t_send, t_recv, base + s)

    def keep_words():
        return pltpu.make_async_copy(tob.at[g], text_spot(g), t_recv)

    near_wait(0)
    near_go(0, 0)
    wait_on(tx.at[row], tx_recv)
    chain_step(0)
    near_go(0, 1)
    far_start(0)
    for d in range(1, nz - 1):
        chain_step(d)
        if d < mine:
            near_wait(d)
            near_go(d, 0)
            near_go(d, 1)
    for j in range(max(1, nz - 1), mine):
        near_wait(j)
        near_go(j, 0)
        near_go(j, 1)

    def text_part(j):
        text_head(j)
        for k in range(nz - 1):
            part_z(j, k).start()
        if j == mine - 1:
            for k in range(nz - 1):
                stats_z(k).start()

    def video_wait(j):
        wait_on(qb.at[j], q_recv.at[j])
        halo_wait(j)

    far_start(1)
    pl.when(row - (nz - 1) >= 0)(lambda: chain_wait(row - (nz - 1)))
    pl.when(row + nz - 1 < nz)(lambda: chain_wait(row + nz - 1))
    text_part(0)
    wait_on(list_in.at[0:3, 0:1], l_recv)
    lists_in = pltpu.make_async_copy(list_in, lists, l_in)
    lists_in.start()
    lists_in.wait()
    far_start(2)
    text_part(1)
    text_part(2)
    for j in range(mine):
        video_wait(j)
        if j < mine - 1:
            video_tiles(j, 0, 4)
        else:
            video_tiles(j, 0, 2)
            text_final()
            for k in range(3):
                send_words(k).start()
            keep_words().start()
            video_tiles(j, 2, 4)

    for x in range(3):
        wait_on(arrays[x].at[:, : 3 * wide], in_send.at[x])
    wait_on(tx.at[0, :, 0:3], tx_send)
    wait_on(list_in.at[0:3, 0:1], l_send)
    halo_drain()
    for d in range(nz - 1):
        chain_drain(d)
    wait_on(got, p_send)
    wait_on(got_stats, ps_send)
    wait_on(tob.at[0:3], t_send)
    wait_on(text_out, t_recv)
    wait_on(q_hbm.at[:, : 3 * wide], o_send)
    wait_on(out, o_recv)


def deliver(pieces, video, text, video_out, text_out, sems):
    rows = video.shape[0] // pieces
    copies = [
        pltpu.make_async_copy(
            video.at[i * rows : (i + 1) * rows], video_out.at[i * rows : (i + 1) * rows], sems.at[i]
        )
        for i in range(pieces)
    ]
    copies.append(pltpu.make_async_copy(text, text_out, sems.at[pieces]))
    for copy in copies:
        copy.start()
    for copy in copies:
        copy.wait()


def deliver(pieces, video, text, video_out, text_out, sems):
    rows = video.shape[0] // pieces
    copies = [
        pltpu.make_async_copy(
            video.at[i * rows : (i + 1) * rows], video_out.at[i * rows : (i + 1) * rows], sems.at[i]
        )
        for i in range(pieces)
    ]
    copies.append(pltpu.make_async_copy(text, text_out, sems.at[pieces]))
    for copy in copies:
        copy.start()
    for copy in copies:
        copy.wait()


def fused(qv, kv, vv, qt, kt, vt, key_tiles, tile_owner, text_count):
    n = lax.axis_size("ctx")
    rows, width = qv.shape
    mine = width // HD // 4
    here = qt.shape[0]
    nz = n // 4
    dma = pltpu.SemaphoreType.DMA
    shapes = [
        jax.ShapeDtypeStruct((rows, width), jnp.bfloat16),
        jax.ShapeDtypeStruct((here, width), jnp.bfloat16),
    ]
    anywhere = pl.BlockSpec(memory_space=pl.ANY)
    results = pl.pallas_call(
        functools.partial(plane_kernel, n),
        in_specs=[pl.BlockSpec(memory_space=pltpu.HBM)] * 9,
        out_specs=[pl.BlockSpec(memory_space=pltpu.VMEM)] * 2,
        out_shape=[pltpu.VMEM(x.shape, x.dtype) for x in shapes],
        scratch_shapes=[pltpu.VMEM((8, 2, rows, HD), jnp.bfloat16)] * mine
        + [
            pltpu.VMEM((mine, 4, rows, HD), jnp.bfloat16),
            pltpu.VMEM((mine, 4, rows, HD), jnp.bfloat16),
            pltpu.VMEM((nz, 3, 4, here, mine * HD), jnp.bfloat16),
            pltpu.VMEM((mine, nz, 4 * here, HD), jnp.float32),
            pltpu.VMEM((n * here, 128), jnp.float32),
            pltpu.VMEM((8, n * here), jnp.float32),
            pltpu.VMEM((nz - 1, mine, 4 * here, HD), jnp.float32),
            pltpu.VMEM((nz - 1, 8, n * here), jnp.float32),
            pltpu.VMEM((nz - 1, n * here, 128), jnp.float32),
            pltpu.VMEM((4, here, mine * HD), jnp.bfloat16),
            pltpu.VMEM((8, 128), jnp.int32),
            pltpu.VMEM((4, 8, 128), jnp.int32),
            pltpu.SMEM((4, 8, 128), jnp.int32),
            pltpu.SMEM(key_tiles.shape, jnp.int32),
            pltpu.SMEM(tile_owner.shape, jnp.int32),
            pltpu.SMEM(text_count.shape, jnp.int32),
        ]
        + [dma((3,)), dma((mine, 2)), dma((mine,)), dma((mine,)), dma, dma]
        + [dma((2, nz - 1)), dma((nz,)), dma((2,)), dma((mine, 2))]
        + [dma] * 11
        + [dma((3,)), pltpu.VMEM((3, here, width), jnp.bfloat16), dma],
        compiler_params=pltpu.CompilerParams(
            collective_id=0, has_side_effects=True, vmem_limit_bytes=125 << 19
        ),
        name="tile_attention",
    )(key_tiles, tile_owner, text_count, qv, kv, vv, qt, kt, vt)
    results = [pltpu.with_memory_space_constraint(x, pltpu.VMEM) for x in results]
    pieces = 4
    return pl.pallas_call(
        functools.partial(deliver, pieces),
        in_specs=[pl.BlockSpec(memory_space=pltpu.VMEM)] * 2,
        out_specs=[pl.BlockSpec(memory_space=pltpu.HBM)] * 2,
        out_shape=shapes,
        scratch_shapes=[dma((pieces + 1,))],
        name="deliver",
    )(*results)


def whole_device(*args):
    n = lax.axis_size("ctx")
    rows, width = args[0].shape
    here = args[3].shape[0]
    if rows == TILE and n % 4 == 0 and n >= 8 and n & (n - 1) == 0 and here in (16, 32, 64) and width // HD == 12:
        return fused(*args)
    return on_device(*args)


def solution(mesh):
    split = P(("groups", "ctx"), None)
    return jax.shard_map(
        whole_device,
        mesh=mesh,
        in_specs=(split,) * 7 + (P("groups"), P("groups")),
        out_specs=(split, split),
        check_vma=False,
    )
```
